256 devices in a mesh: ka: 8 (over y, x_hi), rows: 32 (over x_lo, z, core).
Axes of the slice: x: 4 (x_hi: 2, x_lo: 2; x = x_hi * 2 + x_lo), y: 4, z: 8, core: 2. Of those that a mesh axis runs over, the one named last changes fastest.
Arguments:
- drive: float32 [131072, 256], P(('ka', 'rows')), may hold values from -6 to 6
- relax: float32 [131072], P(('ka', 'rows')), may hold values from 0.2 to 1
- blocks: bfloat16 [65536, 4096], P(('ka', 'rows')), may hold values from -0.09375 to 0.09375
- row_block: int32 [65536], P(('ka', 'rows')), may hold values from -1 to 2047, as said below
- col_block: int32 [65536], P(('ka', 'rows')), may hold values from -1 to 2047, as said below
Outputs:
- distribution: float32 [131072, 256], P(('ka', 'rows'))
The draws below stay inside these ranges and needn't reach their ends.
Inputs may be any that keep to these rules, and one draw needn't show every extreme that they name: `row_block`: the slots form groups of 256 in order, one group for each block of 8 row blocks (the row blocks of one device); a group's live slots come first and name row blocks of that group's own 8; -1 marks an empty slot. Every group has at least 85 live slots and some group is full in every draw. `col_block`: with the state blocks numbered (ka index * 32 + rows index) * 8 + block, a live slot's column block has the ka index of its row block or the next one modulo 8, and a rows index that differs from its row block's rows index by at most one, modulo 32; no pair of row and column blocks is named twice; -1 exactly where row_block is -1.
All inputs are finite; a program needn't handle non-finite values.
Results may differ from the reference program's by a relative error of at most 0.0015.
Values may be sent and summed in bfloat16 or wider, within the bound.
No kernel may reach another device: no remote copies, remote signals or barrier semaphores. Data moves between devices by JAX's collectives and lax.ppermute only.
A program may use at most 128 MiB of HBM per device.

```python
import math
import jax
import jax.numpy as jnp
from jax import lax

STATES_PER_BLOCK = 64
CHANNELS = 256
BLOCKS_DEV = 8
SLOTS_PER_ROW = 32
ITERS = 2
KA_DEVS = 8
ROW_DEVS = 32
SLOTS_DEV = 256
NBLK = 2048
ELECTRON_STATES = 131072
KERNEL_SLOTS = 65536


def pattern(key):
    base_key = jax.random.fold_in(key, 11)
    first_key, second_key, third_key = jax.random.split(base_key, 3)
    device_total = KA_DEVS * ROW_DEVS
    full_device = jax.random.randint(first_key, (), 0, device_total)
    live_count = jax.random.randint(second_key, (device_total,), SLOTS_DEV // 3, SLOTS_DEV + 1)
    device_ids = jnp.arange(device_total, dtype=jnp.int32)
    live_count = jnp.where(device_ids == full_device, SLOTS_DEV, live_count)
    pair_count = 6 * BLOCKS_DEV * BLOCKS_DEV
    device_keys = jax.random.split(third_key, device_total)

    def choose_pairs(one_key):
        return jax.random.permutation(one_key, pair_count)[:SLOTS_DEV]
    chosen = jax.vmap(choose_pairs)(device_keys).astype(jnp.int32)
    row_local = chosen % BLOCKS_DEV
    remain = chosen // BLOCKS_DEV
    column_within_block = remain % BLOCKS_DEV
    remain = remain // BLOCKS_DEV
    row_step = remain % 3
    ka_step = remain // 3
    ka_here = (device_ids // ROW_DEVS)[:, None]
    row_here = (device_ids % ROW_DEVS)[:, None]
    target_ka = (ka_here + ka_step) % KA_DEVS
    target_row = (row_here + row_step - 1 + ROW_DEVS) % ROW_DEVS
    rows_out = device_ids[:, None] * BLOCKS_DEV + row_local
    cols_out = (target_ka * ROW_DEVS + target_row) * BLOCKS_DEV + column_within_block
    slot_ids = jnp.arange(SLOTS_DEV, dtype=jnp.int32)
    live_slot = slot_ids[None, :] < live_count[:, None]
    rows_out = jnp.where(live_slot, rows_out, -1).astype(jnp.int32)
    cols_out = jnp.where(live_slot, cols_out, -1).astype(jnp.int32)
    return (rows_out.reshape(-1), cols_out.reshape(-1))


def draw_row_block(key, part):
    return pattern(key)[0]


def draw_col_block(key, part):
    return pattern(key)[1]


def levels(rng, extent, cuts, low, high):
    def one(axis_at, parts):
        steps = jax.random.uniform(jax.random.fold_in(jax.random.fold_in(rng, 6), axis_at), (parts,), jnp.float32, low / len(cuts), high / len(cuts))
        return jnp.repeat(jnp.exp(steps), extent[axis_at] // parts).reshape((-1,) + (1,) * (len(extent) - axis_at - 1))

    factor_of = one(*cuts[0])
    for cut in cuts[1:]:
        factor_of = factor_of * one(*cut)
    return factor_of


def bell_draw(key, extent, spread, limit, cuts=(), kind=jnp.bfloat16):
    drawn = jax.random.normal(key, extent, jnp.float32) * spread
    if len(cuts) > 0:
        drawn = levels(key, extent, cuts, -0.22, 0.18) * drawn
    return jnp.clip(drawn, min=-limit, max=limit).astype(kind)


def setup_inputs(seed: int = 0) -> dict:
    streams_of = jax.random.split(jax.random.key(seed), 6)
    return {
        "drive": bell_draw(streams_of[0], (ELECTRON_STATES, CHANNELS), 1.0, 6.0, ((0, 256),), jnp.float32),
        "relax": jnp.clip(jnp.exp(math.log(1.0) - 1.609438 * jax.random.uniform(streams_of[1], (ELECTRON_STATES,), jnp.float32) ** levels(streams_of[1], (ELECTRON_STATES,), ((0, 256),), -0.2, 0.2)), 0.2, 1.0),
        "blocks": bell_draw(streams_of[2], (KERNEL_SLOTS, STATES_PER_BLOCK * STATES_PER_BLOCK), (2 * SLOTS_PER_ROW * STATES_PER_BLOCK) ** -0.5, 0.09375, ((0, 256),)),
        "row_block": draw_row_block(jax.random.fold_in(streams_of[5], 71), 0),
        "col_block": draw_col_block(jax.random.fold_in(streams_of[5], 71), 0),
    }


def kernel_product(wire_field, blocks, row_block, col_block):
    device_total = KA_DEVS * ROW_DEVS
    field_blocks = wire_field.reshape(NBLK, STATES_PER_BLOCK, CHANNELS).astype(jnp.float32)
    kernels = blocks.reshape(device_total, SLOTS_DEV, STATES_PER_BLOCK, STATES_PER_BLOCK)
    row_groups = row_block.reshape(device_total, SLOTS_DEV)
    col_groups = col_block.reshape(device_total, SLOTS_DEV)

    def visit_device(totals, slot_items):
        kernel, row_ids, col_ids = slot_items
        live_slot = row_ids >= 0
        clamped_row = jnp.where(live_slot, row_ids, 0).astype(jnp.int32)
        col_safe = jnp.where(live_slot, col_ids, 0).astype(jnp.int32)
        slot_weight = live_slot.astype(jnp.float32)[:, None, None]
        kernel_wide = kernel.astype(jnp.float32)
        forward = jnp.einsum("sij,sjc->sic", kernel_wide, field_blocks[col_safe]) * slot_weight
        backward = jnp.einsum("sji,sjc->sic", kernel_wide, field_blocks[clamped_row]) * slot_weight
        totals = totals.at[clamped_row].add(forward)
        totals = totals.at[col_safe].add(backward)
        return totals, None

    initial_totals = jnp.zeros((NBLK, STATES_PER_BLOCK, CHANNELS), jnp.float32)
    totals, _ = lax.scan(visit_device, initial_totals, (kernels, row_groups, col_groups))
    return totals.reshape(ELECTRON_STATES, CHANNELS)


def reference(drive, relax, blocks, row_block, col_block):
    state_field = drive
    for sweep_index in range(ITERS):
        wire_field = state_field.astype(jnp.bfloat16)
        state_field = drive + relax[:, None] * kernel_product(wire_field, blocks, row_block, col_block)
    return state_field
```

```python
import functools

import jax
import jax.numpy as jnp
from jax import lax
from jax.experimental import pallas as pl
from jax.experimental.pallas import tpu as pltpu
from jax.sharding import PartitionSpec as P

SIDE = 64
LANES = 128
ITERS = 2
TN = (((0,), (0,)), ((), ()))


def shifted(value, axis, steps):
    count = lax.axis_size(axis)
    pairs = [(source, (source + steps) % count) for source in range(count)]
    return lax.ppermute(value, axis, pairs)


def log2(n):
    assert n & (n - 1) == 0
    return n.bit_length() - 1


def call(kernel, outs, flops, *args, scratch=()):
    nbytes = sum(a.size * a.dtype.itemsize for a in args)
    return pl.pallas_call(
        kernel,
        out_shape=outs,
        in_specs=[pl.BlockSpec(memory_space=pltpu.VMEM)] * len(args),
        out_specs=jax.tree.map(lambda _: pl.BlockSpec(memory_space=pltpu.VMEM), outs),
        scratch_shapes=list(scratch),
        cost_estimate=pl.CostEstimate(flops=flops, transcendentals=0, bytes_accessed=nbytes),
        compiler_params=pltpu.CompilerParams(vmem_limit_bytes=40 << 20),
    )(*args)


def to_interleaved(value, dst_ref, scratch_ref, count):
    for g in range(value.shape[1] // LANES):
        lanes = slice(g * LANES, (g + 1) * LANES)
        scratch_ref[g] = value[:, lanes]
        for t in range(SIDE // 2):
            pair = [scratch_ref[g, pl.ds(2 * t + h, count, stride=SIDE), :] for h in range(2)]
            dst_ref[2 * t * count : (2 * t + 2) * count, lanes] = jnp.concatenate(pair, axis=0).astype(jnp.bfloat16)


def split_transposed(matrix, field, left_ref, middle_ref, right_ref):
    rows = left_ref.shape[0]
    for k, ref in enumerate((left_ref, middle_ref, right_ref)):
        part = lax.dot_general(matrix[:, k * rows : (k + 1) * rows], field, TN, preferred_element_type=jnp.float32)
        ref[...] = part.astype(ref.dtype)


def build_body(half, sizes, blocks_ref, row_ref, col_ref, drive_ref, matrix_ref, field_ref, left_ref, middle_ref, right_ref, scratch_ref):
    count, row_devs, ka_devs = sizes
    bits, row_bits = log2(count), log2(row_devs)
    row = row_ref[...]
    col = col_ref[...]
    ka_step = ((col >> (bits + row_bits)) - (row >> (bits + row_bits))) & (ka_devs - 1)
    row_step = (((col >> bits) & (row_devs - 1)) - ((row >> bits) & (row_devs - 1)) + 1) & (row_devs - 1)
    band = row_step * count + (col & (count - 1))
    groups = 3 * count // 2
    place = ((band & 1) * groups + (band >> 1)) * count + (row & (count - 1))
    place = jnp.where((row >= 0) & (ka_step == half), place, -1)
    slots = blocks_ref.shape[0]
    total = 2 * groups * count
    chosen = lax.broadcasted_iota(jnp.int32, (total, slots), 0) == place
    chosen = jnp.where(chosen, 1.0, 0.0).astype(jnp.bfloat16)
    low = lax.broadcasted_iota(jnp.int32, (groups * count, 2 * SIDE), 1) < SIDE
    for u in range(SIDE // 4):
        found = jnp.dot(chosen, blocks_ref[:, u * 4 * SIDE : (u + 1) * 4 * SIDE], preferred_element_type=jnp.float32)
        for w in range(2):
            t = 2 * u + w
            even = found[: groups * count, w * 2 * SIDE : (w + 1) * 2 * SIDE]
            odd = found[groups * count :, w * 2 * SIDE : (w + 1) * 2 * SIDE]
            first = jnp.where(low, even, pltpu.roll(odd, SIDE, 1))
            second = jnp.where(low, pltpu.roll(even, SIDE, 1), odd)
            for q in range(groups):
                pair = [v[q * count : (q + 1) * count, :] for v in (first, second)]
                matrix_ref[2 * t * count : (2 * t + 2) * count, 2 * q * SIDE : (2 * q + 2) * SIDE] = jnp.concatenate(
                    pair, axis=0
                ).astype(jnp.bfloat16)
    to_interleaved(drive_ref[...], field_ref, scratch_ref, count)
    split_transposed(matrix_ref[...], field_ref[...], left_ref, middle_ref, right_ref)


def forward_body(count, cross_ref, own_ref, *refs):
    fields = refs[:6]
    middle_ref, left_ref, right_ref, out_ref, scratch_ref = refs[6:]
    rows = out_ref.shape[0]
    acc = None
    for k in range(3):
        for matrix, field in ((own_ref, fields[k]), (cross_ref, fields[3 + k])):
            part = jnp.dot(matrix[:, k * rows : (k + 1) * rows], field[...], preferred_element_type=jnp.float32)
            acc = part if acc is None else acc + part
    for g in range(acc.shape[1] // LANES):
        lanes = slice(g * LANES, (g + 1) * LANES)
        scratch_ref[g] = acc[:, lanes]
        for b in range(count):
            here = slice(b * SIDE, (b + 1) * SIDE)
            extra = middle_ref[here, lanes] + left_ref[here, lanes].astype(jnp.float32) + right_ref[here, lanes].astype(jnp.float32)
            out_ref[here, lanes] = scratch_ref[g, pl.ds(b, SIDE, stride=count), :] + extra


def update_body(count, drive_ref, relax_ref, forward_ref, received_ref, cross_ref, wire_ref, field_ref, left_ref, middle_ref, right_ref, scratch_ref):
    field = drive_ref[...] + relax_ref[...] * (forward_ref[...] + received_ref[...].astype(jnp.float32))
    wire_ref[...] = field.astype(jnp.bfloat16)
    to_interleaved(field, field_ref, scratch_ref, count)
    split_transposed(cross_ref[...], field_ref[...], left_ref, middle_ref, right_ref)


def transposed_body(matrix_ref, field_ref, left_ref, middle_ref, right_ref):
    split_transposed(matrix_ref[...], field_ref[...], left_ref, middle_ref, right_ref)


def final_body(drive_ref, relax_ref, forward_ref, received_ref, out_ref):
    out_ref[...] = drive_ref[...] + relax_ref[...] * (forward_ref[...] + received_ref[...].astype(jnp.float32))


def halo(value):
    return shifted(value, "rows", 1), shifted(value, "rows", -1)


def local(drive, relax, blocks, row_block, col_block):
    rows, channels = drive.shape
    count = rows // SIDE
    sizes = (count, lax.axis_size("rows"), lax.axis_size("ka"))
    bf16, f32 = jnp.bfloat16, jnp.float32
    small = jax.ShapeDtypeStruct((rows, channels), bf16)
    wide = jax.ShapeDtypeStruct((rows, channels), f32)
    matrix = jax.ShapeDtypeStruct((rows, 3 * rows), bf16)
    staging = pltpu.VMEM((channels // LANES, rows, LANES), f32)
    row2 = row_block.reshape(1, -1)
    col2 = col_block.reshape(1, -1)
    relax2 = relax.reshape(-1, 1)
    work = 2 * rows * rows * 3 * channels
    wire = drive.astype(bf16)
    cross, field, left, middle, right = call(
        functools.partial(build_body, 1, sizes), (matrix, small, small, wide, small), 2 * work, blocks, row2, col2, drive,
        scratch=[staging],
    )
    own, _, own_left, own_middle, own_right = call(
        functools.partial(build_body, 0, sizes), (matrix, small, small, wide, small), 2 * work, blocks, row2, col2, drive,
        scratch=[staging],
    )
    for sweep in range(ITERS):
        down = shifted(wire, "ka", -1)
        before, after = halo(wire)
        got = middle + shifted(left, "rows", -1).astype(f32) + shifted(right, "rows", 1).astype(f32)
        received = shifted(got.astype(bf16), "ka", 1)
        own_after = shifted(own_left, "rows", -1)
        own_before = shifted(own_right, "rows", 1)
        down_before, down_after = halo(down)
        forward = call(
            functools.partial(forward_body, count), wide, 2 * work,
            cross, own, before, wire, after, down_before, down, down_after, own_middle, own_after, own_before,
            scratch=[staging],
        )
        if sweep + 1 == ITERS:
            return call(final_body, wide, 0, drive, relax2, forward, received)
        wire, field, left, middle, right = call(
            functools.partial(update_body, count), (small, small, small, wide, small), work,
            drive, relax2, forward, received, cross, scratch=[staging],
        )
        own_left, own_middle, own_right = call(transposed_body, (small, wide, small), work, own, field)


def solution(mesh):
    spread = P(("ka", "rows"))
    wide = P(("ka", "rows"), None)
    return jax.shard_map(
        local, mesh=mesh, in_specs=(wide, spread, wide, spread, spread), out_specs=wide, check_vma=False
    )
```

```python
import functools

import jax
import jax.numpy as jnp
from jax import lax
from jax.experimental import pallas as pl
from jax.experimental.pallas import tpu as pltpu
from jax.sharding import PartitionSpec as P

SIDE = 64
LANES = 128
ITERS = 2
PIECES = 4
BF16, F32 = jnp.bfloat16, jnp.float32
VMEM = pl.BlockSpec(memory_space=pltpu.VMEM)
HBM = pl.BlockSpec(memory_space=pltpu.HBM)


def log2(n):
    assert n & (n - 1) == 0
    return n.bit_length() - 1


def shifted(value, axis, steps):
    count = lax.axis_size(axis)
    return lax.ppermute(value, axis, [(source, (source + steps) % count) for source in range(count)])


def mate(value):
    return lax.ppermute(value, "rows", [(i, i ^ 1) for i in range(lax.axis_size("rows"))])


def far(value):
    count = lax.axis_size("rows")
    return lax.ppermute(value, "rows", [(i, (i + 1 if i & 1 else i - 1) % count) for i in range(count)])


def call(kernel, outs, flops, args, specs=None, scratch=()):
    if specs:
        args = [pltpu.with_memory_space_constraint(a, pltpu.HBM) for a in args]
    nbytes = sum(a.size * a.dtype.itemsize for a in args)
    return pl.pallas_call(
        kernel,
        out_shape=outs,
        in_specs=specs or [VMEM] * len(args),
        out_specs=jax.tree.map(lambda _: VMEM, outs),
        scratch_shapes=list(scratch),
        cost_estimate=pl.CostEstimate(flops=flops, transcendentals=0, bytes_accessed=nbytes),
        compiler_params=pltpu.CompilerParams(vmem_limit_bytes=5 << 20),
    )(*args)


def dot(a, b):
    return jnp.dot(a, b, preferred_element_type=F32)


def dot_t(a, b):
    return lax.dot_general(a, b, (((0,), (0,)), ((), ())), preferred_element_type=F32)


def interleave(value, scratch_ref, dst_ref):
    count = value.shape[0] // SIDE
    for g in range(value.shape[1] // LANES):
        lanes = slice(g * LANES, (g + 1) * LANES)
        scratch_ref[g] = value[:, lanes]
        for t in range(SIDE // 2):
            pair = [scratch_ref[g, pl.ds(2 * t + h, count, stride=SIDE), :] for h in range(2)]
            dst_ref[2 * t * count : (2 * t + 2) * count, lanes] = jnp.concatenate(pair, axis=0).astype(BF16)


def restored(value, scratch_ref):
    count = value.shape[0] // SIDE
    columns = []
    for g in range(value.shape[1] // LANES):
        scratch_ref[g] = value[:, g * LANES : (g + 1) * LANES]
        columns.append(jnp.concatenate([scratch_ref[g, pl.ds(b, SIDE, stride=count), :] for b in range(count)], axis=0))
    return jnp.concatenate(columns, axis=1)


def build(half, sizes, blocks_hbm, row_hbm, col_hbm, blocks, ids, sems, stores):
    count, row_devs, ka_devs = sizes
    bits, row_bits = log2(count), log2(row_devs)
    copies = [pltpu.make_async_copy(h, ids.at[k : k + 1], sems.at[k]) for k, h in enumerate((row_hbm, col_hbm))]
    width = blocks.shape[1] // PIECES
    for k in range(PIECES):
        lanes = pl.ds(k * width, width)
        copies.append(pltpu.make_async_copy(blocks_hbm.at[:, lanes], blocks.at[:, lanes], sems.at[2 + k]))
    for copy in copies:
        copy.start()
    copies[0].wait()
    copies[1].wait()
    row = ids[0:1, :]
    col = ids[1:2, :]
    row_place = (row >> bits) & (row_devs - 1)
    ka_step = ((col >> (bits + row_bits)) - (row >> (bits + row_bits))) & (ka_devs - 1)
    row_step = (((col >> bits) & (row_devs - 1)) - row_place + 1) & (row_devs - 1)
    is_mate = (row_step >> 1) == ((row_place & 1) ^ 1)
    group = jnp.where(row_step == 1, 0, jnp.where(is_mate, 1, 2))
    band = group * count + (col & (count - 1))
    pairs = 3 * count // 2
    place = ((band & 1) * pairs + (band >> 1)) * count + (row & (count - 1))
    place = jnp.where((row >= 0) & (ka_step == half), place, -1)
    slots = blocks.shape[0]
    chosen = lax.broadcasted_iota(jnp.int32, (2 * pairs * count, slots), 0) == place
    chosen = jnp.where(chosen, 1.0, 0.0).astype(BF16)
    low = lax.broadcasted_iota(jnp.int32, (pairs * count, LANES), 1) < SIDE
    for u in range(SIDE // 4):
        if u % (SIDE // 4 // PIECES) == 0:
            copies[2 + u // (SIDE // 4 // PIECES)].wait()
        found = dot(chosen, blocks[:, u * 2 * LANES : (u + 1) * 2 * LANES])
        for w in range(2):
            t = 2 * u + w
            even = found[: pairs * count, w * LANES : (w + 1) * LANES]
            odd = found[pairs * count :, w * LANES : (w + 1) * LANES]
            first = jnp.where(low, even, pltpu.roll(odd, SIDE, 1))
            second = jnp.where(low, pltpu.roll(even, SIDE, 1), odd)
            for q in range(pairs):
                pair = [v[q * count : (q + 1) * count, :] for v in (first, second)]
                tile = jnp.concatenate(pair, axis=0).astype(BF16)
                per = pairs // 3
                lanes = slice((q % per) * LANES, (q % per + 1) * LANES)
                stores[q // per][2 * t * count : (2 * t + 2) * count, lanes] = tile


def emit(cross, wire, perm_ref, wire_ref, self_ref, mate_ref, far_ref):
    perm = perm_ref[...]
    wire_ref[...] = wire
    self_ref[...] = dot_t(cross[0][...], perm)
    for k, ref in ((2, far_ref), (1, mate_ref)):
        ref[0] = dot_t(cross[k][...], perm).astype(BF16)
        ref[1] = wire


def first_body(sizes, blocks_hbm, row_hbm, col_hbm, drive_hbm, relax_hbm, *refs):
    cross, (perm_ref, wire_ref, self_ref, mate_ref, far_ref, spread_ref) = refs[:3], refs[3:9]
    blocks, ids, drive, relax, scratch, sems = refs[9:]
    later = [
        pltpu.make_async_copy(drive_hbm, drive, sems.at[2 + PIECES]),
        pltpu.make_async_copy(relax_hbm, relax, sems.at[3 + PIECES]),
    ]
    for copy in later:
        copy.start()
    build(1, sizes, blocks_hbm, row_hbm, col_hbm, blocks, ids, sems, cross)
    for copy in later:
        copy.wait()
    spread_ref[...] = jnp.broadcast_to(relax[...], (LANES, relax.shape[1])).T
    field = drive[...]
    interleave(field, scratch, perm_ref)
    emit(cross, field.astype(BF16), perm_ref, wire_ref, self_ref, mate_ref, far_ref)


def second_body(sizes, blocks_hbm, row_hbm, col_hbm, *refs):
    build(0, sizes, blocks_hbm, row_hbm, col_hbm, *refs[3:], refs[:3])


def own_body(*refs):
    mats, sent, (wire_ref, perm_ref, mate_ref, far_ref) = refs[:3], refs[3:5], refs[5:9]
    out_ref, scratch, other = refs[9:]
    total = dot_t(mats[0][...], perm_ref[...])
    straight = dot(mats[0][...], wire_ref[...])
    for k, ref in ((0, mate_ref), (1, far_ref)):
        wire = ref[1]
        interleave(wire.astype(F32), scratch, other)
        straight += dot(mats[k + 1][...], wire)
        total += dot_t(sent[k][...], other[...])
    out_ref[...] = total + restored(straight, scratch)


def new_field(cross, nexts, own_ref, received_ref, drive_ref, relax_ref, scratch):
    straight = dot(cross[0][...], nexts[0][...])
    straight += dot(cross[1][...], nexts[1][...])
    straight += dot(cross[2][...], nexts[2][...])
    product = own_ref[...] + received_ref[...].astype(F32) + restored(straight, scratch)
    scale = jnp.concatenate([relax_ref[...]] * (product.shape[1] // LANES), axis=1)
    return drive_ref[...] + scale * product


def update_body(*refs):
    cross, nexts, rest = refs[:3], refs[3:6], refs[6:10]
    perm_ref, wire_ref, self_ref, mate_ref, far_ref, scratch = refs[10:]
    field = new_field(cross, nexts, *rest, scratch)
    interleave(field, scratch, perm_ref)
    emit(cross, field.astype(BF16), perm_ref, wire_ref, self_ref, mate_ref, far_ref)


def final_body(*refs):
    refs[10][...] = new_field(refs[:3], refs[3:6], *refs[6:10], refs[11])


def local(drive, relax, blocks, row_block, col_block):
    rows, channels = drive.shape
    slots = blocks.shape[0]
    sizes = (rows // SIDE, lax.axis_size("rows"), lax.axis_size("ka"))
    small = jax.ShapeDtypeStruct((rows, channels), BF16)
    double = jax.ShapeDtypeStruct((2, rows, channels), BF16)
    wide = jax.ShapeDtypeStruct((rows, channels), F32)
    matrices = (jax.ShapeDtypeStruct((rows, rows), BF16),) * 3
    emitted = (small, small, wide, double, double)
    staging = pltpu.VMEM((channels // LANES, rows, LANES), F32)
    fetch = [pltpu.VMEM(blocks.shape, BF16), pltpu.VMEM((2, slots), jnp.int32)]
    row2 = row_block.reshape(1, -1)
    col2 = col_block.reshape(1, -1)
    relax2 = relax.reshape(1, -1)
    work = 2 * rows * rows * channels
    spread = jax.ShapeDtypeStruct((rows, LANES), F32)
    *cross, perm, wire, partial, to_mate, to_far, relax3 = call(
        functools.partial(first_body, sizes), (*matrices, *emitted, spread), 9 * work,
        [blocks, row2, col2, drive, relax2], [HBM] * 5,
        fetch + [pltpu.VMEM(drive.shape, F32), pltpu.VMEM((1, rows), F32), staging, pltpu.SemaphoreType.DMA((4 + PIECES,))],
    )
    own = None
    for sweep in range(ITERS):
        down = shifted(wire, "ka", -1)
        from_far = far(to_far)
        from_mate = mate(to_mate)
        if own is None:
            own = call(
                functools.partial(second_body, sizes), matrices, 6 * work, [blocks, row2, col2], [HBM] * 3,
                fetch + [pltpu.SemaphoreType.DMA((2 + PIECES,))],
            )
            sent = [mate(own[1]), far(own[2])]
        got = partial + from_mate[0].astype(F32) + from_far[0].astype(F32)
        received = shifted(got.astype(BF16), "ka", 1)
        nexts = [down, mate(down), far(down)]
        own_product = call(
            own_body, wide, 9 * work, [*own, *sent, wire, perm, from_mate, from_far],
            scratch=[staging, pltpu.VMEM((rows, channels), BF16)],
        )
        args = [*cross, *nexts, own_product, received, drive, relax3]
        if sweep + 1 == ITERS:
            return call(final_body, wide, 3 * work, args, scratch=[staging])
        perm, wire, partial, to_mate, to_far = call(update_body, emitted, 6 * work, args, scratch=[staging])


def solution(mesh):
    spread = P(("ka", "rows"))
    wide = P(("ka", "rows"), None)
    return jax.shard_map(
        local, mesh=mesh, in_specs=(wide, spread, wide, spread, spread), out_specs=wide, check_vma=False
    )
```

```python
import functools

import jax
import jax.numpy as jnp
from jax import lax
from jax.experimental import pallas as pl
from jax.experimental.pallas import tpu as pltpu
from jax.sharding import PartitionSpec as P

SIDE = 64
LANES = 128
ITERS = 2
PIECES = 4
BF16, F32 = jnp.bfloat16, jnp.float32
VMEM = pl.BlockSpec(memory_space=pltpu.VMEM)
HBM = pl.BlockSpec(memory_space=pltpu.HBM)


def log2(n):
    assert n & (n - 1) == 0
    return n.bit_length() - 1


def shifted(value, axis, steps):
    count = lax.axis_size(axis)
    return lax.ppermute(value, axis, [(source, (source + steps) % count) for source in range(count)])


def mate(value):
    return lax.ppermute(value, "rows", [(i, i ^ 1) for i in range(lax.axis_size("rows"))])


def far(value):
    count = lax.axis_size("rows")
    return lax.ppermute(value, "rows", [(i, (i + 1 if i & 1 else i - 1) % count) for i in range(count)])


def call(kernel, outs, flops, args, specs=None, scratch=()):
    if specs:
        args = [pltpu.with_memory_space_constraint(a, pltpu.HBM) for a in args]
    nbytes = sum(a.size * a.dtype.itemsize for a in args)
    return pl.pallas_call(
        kernel,
        out_shape=outs,
        in_specs=specs or [VMEM] * len(args),
        out_specs=jax.tree.map(lambda _: VMEM, outs),
        scratch_shapes=list(scratch),
        cost_estimate=pl.CostEstimate(flops=flops, transcendentals=0, bytes_accessed=nbytes),
        compiler_params=pltpu.CompilerParams(vmem_limit_bytes=5 << 20),
    )(*args)


def dot(a, b):
    return jnp.dot(a, b, preferred_element_type=F32)


def dot_t(a, b):
    return lax.dot_general(a, b, (((0,), (0,)), ((), ())), preferred_element_type=F32)


def interleave(value, scratch_ref, dst_ref):
    count = value.shape[0] // SIDE
    for g in range(value.shape[1] // LANES):
        lanes = slice(g * LANES, (g + 1) * LANES)
        scratch_ref[g] = value[:, lanes]
        for t in range(SIDE // 2):
            pair = [scratch_ref[g, pl.ds(2 * t + h, count, stride=SIDE), :] for h in range(2)]
            dst_ref[2 * t * count : (2 * t + 2) * count, lanes] = jnp.concatenate(pair, axis=0).astype(BF16)


def restored(value, scratch_ref):
    count = value.shape[0] // SIDE
    columns = []
    for g in range(value.shape[1] // LANES):
        scratch_ref[g] = value[:, g * LANES : (g + 1) * LANES]
        columns.append(jnp.concatenate([scratch_ref[g, pl.ds(b, SIDE, stride=count), :] for b in range(count)], axis=0))
    return jnp.concatenate(columns, axis=1)


def build(half, sizes, blocks_hbm, row_hbm, col_hbm, blocks, ids, sems, stores):
    count, row_devs, ka_devs = sizes
    bits, row_bits = log2(count), log2(row_devs)
    copies = [pltpu.make_async_copy(h, ids.at[k : k + 1], sems.at[k]) for k, h in enumerate((row_hbm, col_hbm))]
    width = blocks.shape[1] // PIECES
    for k in range(PIECES):
        lanes = pl.ds(k * width, width)
        copies.append(pltpu.make_async_copy(blocks_hbm.at[:, lanes], blocks.at[:, lanes], sems.at[2 + k]))
    for copy in copies:
        copy.start()
    copies[0].wait()
    copies[1].wait()
    row = ids[0:1, :]
    col = ids[1:2, :]
    row_place = (row >> bits) & (row_devs - 1)
    ka_step = ((col >> (bits + row_bits)) - (row >> (bits + row_bits))) & (ka_devs - 1)
    row_step = (((col >> bits) & (row_devs - 1)) - row_place + 1) & (row_devs - 1)
    is_mate = (row_step >> 1) == ((row_place & 1) ^ 1)
    group = jnp.where(row_step == 1, 0, jnp.where(is_mate, 1, 2))
    band = group * count + (col & (count - 1))
    pairs = 3 * count // 2
    place = ((band & 1) * pairs + (band >> 1)) * count + (row & (count - 1))
    place = jnp.where((row >= 0) & (ka_step == half), place, -1)
    slots = blocks.shape[0]
    chosen = lax.broadcasted_iota(jnp.int32, (2 * pairs * count, slots), 0) == place
    chosen = jnp.where(chosen, 1.0, 0.0).astype(BF16)
    low = lax.broadcasted_iota(jnp.int32, (pairs * count, LANES), 1) < SIDE
    for u in range(SIDE // 4):
        if u % (SIDE // 4 // PIECES) == 0:
            copies[2 + u // (SIDE // 4 // PIECES)].wait()
        found = dot(chosen, blocks[:, u * 2 * LANES : (u + 1) * 2 * LANES])
        for w in range(2):
            t = 2 * u + w
            even = found[: pairs * count, w * LANES : (w + 1) * LANES]
            odd = found[pairs * count :, w * LANES : (w + 1) * LANES]
            first = jnp.where(low, even, pltpu.roll(odd, SIDE, 1))
            second = jnp.where(low, pltpu.roll(even, SIDE, 1), odd)
            for q in range(pairs):
                pair = [v[q * count : (q + 1) * count, :] for v in (first, second)]
                tile = jnp.concatenate(pair, axis=0).astype(BF16)
                per = pairs // 3
                lanes = slice((q % per) * LANES, (q % per + 1) * LANES)
                stores[q // per][2 * t * count : (2 * t + 2) * count, lanes] = tile


def emit(cross, wire, perm_ref, wire_ref, self_ref, mate_ref, far_ref):
    perm = perm_ref[...]
    wire_ref[...] = wire
    self_ref[...] = dot_t(cross[0][...], perm)
    for k, ref in ((2, far_ref), (1, mate_ref)):
        ref[0] = dot_t(cross[k][...], perm).astype(BF16)
        ref[1] = wire


def first_body(sizes, blocks_hbm, row_hbm, col_hbm, drive_hbm, relax_hbm, *refs):
    cross, (perm_ref, wire_ref, self_ref, mate_ref, far_ref, spread_ref) = refs[:3], refs[3:9]
    blocks, ids, drive, relax, scratch, sems = refs[9:]
    later = [
        pltpu.make_async_copy(drive_hbm, drive, sems.at[2 + PIECES]),
        pltpu.make_async_copy(relax_hbm, relax, sems.at[3 + PIECES]),
    ]
    for copy in later:
        copy.start()
    build(1, sizes, blocks_hbm, row_hbm, col_hbm, blocks, ids, sems, cross)
    for copy in later:
        copy.wait()
    spread_ref[...] = jnp.broadcast_to(relax[...], (LANES, relax.shape[1])).T
    field = drive[...]
    interleave(field, scratch, perm_ref)
    emit(cross, field.astype(BF16), perm_ref, wire_ref, self_ref, mate_ref, far_ref)


def second_body(sizes, blocks_hbm, row_hbm, col_hbm, *refs):
    build(0, sizes, blocks_hbm, row_hbm, col_hbm, *refs[3:], refs[:3])


def sent_terms(sent, fields, scratch, other):
    total = 0.0
    for matrix, field in zip(sent, fields):
        interleave(field[1].astype(F32), scratch, other)
        total += dot_t(matrix[...], other[...])
    return total


def own_body(*refs):
    mats, (wire_ref, perm_ref, mate_ref, far_ref), sent = refs[:3], refs[3:7], refs[7:-3]
    out_ref, scratch, other = refs[-3:]
    total = dot_t(mats[0][...], perm_ref[...])
    straight = dot(mats[0][...], wire_ref[...])
    straight += dot(mats[1][...], mate_ref[1])
    straight += dot(mats[2][...], far_ref[1])
    if sent:
        total += sent_terms(sent, (mate_ref, far_ref), scratch, other)
    out_ref[...] = total + restored(straight, scratch)


def new_field(cross, nexts, own, drive_ref, relax_ref, scratch):
    straight = dot(cross[0][...], nexts[0][...])
    straight += dot(cross[1][...], nexts[1][...])
    straight += dot(cross[2][...], nexts[2][...])
    product = own + restored(straight, scratch)
    scale = jnp.concatenate([relax_ref[...]] * (product.shape[1] // LANES), axis=1)
    return drive_ref[...] + scale * product


def update_body(*refs):
    cross, nexts, rest, (mate_in, far_in), sent = refs[:3], refs[3:6], refs[6:9], refs[9:11], refs[11:13]
    perm_ref, wire_ref, self_ref, mate_ref, far_ref, scratch, other = refs[13:]
    drive_ref, relax_ref = rest[1:]
    late = sent_terms(sent, (mate_in, far_in), scratch, other)
    field = new_field(cross, nexts, rest[0][...] + late, drive_ref, relax_ref, scratch)
    interleave(field, scratch, perm_ref)
    emit(cross, field.astype(BF16), perm_ref, wire_ref, self_ref, mate_ref, far_ref)


def settle_body(own_ref, received_ref, out_ref):
    out_ref[...] = own_ref[...] + received_ref[...].astype(F32)


def final_body(*refs):
    refs[9][...] = new_field(refs[:3], refs[3:6], refs[6][...], *refs[7:9], refs[10])


def local(drive, relax, blocks, row_block, col_block):
    rows, channels = drive.shape
    slots = blocks.shape[0]
    sizes = (rows // SIDE, lax.axis_size("rows"), lax.axis_size("ka"))
    small = jax.ShapeDtypeStruct((rows, channels), BF16)
    double = jax.ShapeDtypeStruct((2, rows, channels), BF16)
    wide = jax.ShapeDtypeStruct((rows, channels), F32)
    matrices = (jax.ShapeDtypeStruct((rows, rows), BF16),) * 3
    emitted = (small, small, wide, double, double)
    staging = pltpu.VMEM((channels // LANES, rows, LANES), F32)
    fetch = [pltpu.VMEM(blocks.shape, BF16), pltpu.VMEM((2, slots), jnp.int32)]
    row2 = row_block.reshape(1, -1)
    col2 = col_block.reshape(1, -1)
    relax2 = relax.reshape(1, -1)
    work = 2 * rows * rows * channels
    spread = jax.ShapeDtypeStruct((rows, LANES), F32)
    *cross, perm, wire, partial, to_mate, to_far, relax3 = call(
        functools.partial(first_body, sizes), (*matrices, *emitted, spread), 9 * work,
        [blocks, row2, col2, drive, relax2], [HBM] * 5,
        fetch + [pltpu.VMEM(drive.shape, F32), pltpu.VMEM((1, rows), F32), staging, pltpu.SemaphoreType.DMA((4 + PIECES,))],
    )

    extra = [staging, pltpu.VMEM((rows, channels), BF16)]
    for sweep in range(ITERS):
        down = shifted(wire, "ka", -1)
        from_far = far(to_far)
        from_mate = mate(to_mate)
        if sweep == 0:
            own = call(
                functools.partial(second_body, sizes), matrices, 6 * work, [blocks, row2, col2], [HBM] * 3,
                fetch + [pltpu.SemaphoreType.DMA((2 + PIECES,))],
            )
        got = (partial + from_mate[0].astype(F32) + from_far[0].astype(F32)).astype(BF16)
        received = shifted(got, "ka", 1)
        nexts = [down, mate(down), far(down)]
        if sweep == 0:
            gated, _ = lax.optimization_barrier((own[1:], down))
            sent = [mate(gated[0]), far(gated[1])]
        args = [*own, wire, perm, from_mate, from_far, *(sent if sweep else [])]
        own_product = call(own_body, wide, 9 * work, args, scratch=extra)
        own_product = call(settle_body, wide, 90 * work, [own_product, received])
        args = [*cross, *nexts, own_product, drive, relax3]
        if sweep + 1 == ITERS:
            return call(final_body, wide, 3 * work, args, scratch=[staging])
        perm, wire, partial, to_mate, to_far = call(update_body, emitted, 8 * work, [*args, from_mate, from_far, *sent], scratch=extra)


def solution(mesh):
    spread = P(("ka", "rows"))
    wide = P(("ka", "rows"), None)
    return jax.shard_map(
        local, mesh=mesh, in_specs=(wide, spread, wide, spread, spread), out_specs=wide, check_vma=False
    )
```

```python
import functools

import jax
import jax.numpy as jnp
from jax import lax
from jax.experimental import pallas as pl
from jax.experimental.pallas import tpu as pltpu
from jax.sharding import PartitionSpec as P

SIDE = 64
LANES = 128
ITERS = 2
PIECES = 4
HEAVY = 90
BF16, F32 = jnp.bfloat16, jnp.float32
VMEM = pl.BlockSpec(memory_space=pltpu.VMEM)
HBM = pl.BlockSpec(memory_space=pltpu.HBM)


def log2(n):
    assert n & (n - 1) == 0
    return n.bit_length() - 1


def shifted(value, axis, steps):
    count = lax.axis_size(axis)
    return lax.ppermute(value, axis, [(source, (source + steps) % count) for source in range(count)])


def mate(value):
    return lax.ppermute(value, "rows", [(i, i ^ 1) for i in range(lax.axis_size("rows"))])


def far(value):
    count = lax.axis_size("rows")
    return lax.ppermute(value, "rows", [(i, (i + 1 if i & 1 else i - 1) % count) for i in range(count)])


def call(kernel, outs, flops, args, specs=None, scratch=()):
    if specs:
        args = [pltpu.with_memory_space_constraint(a, pltpu.HBM) for a in args]
    nbytes = sum(a.size * a.dtype.itemsize for a in args)
    return pl.pallas_call(
        kernel,
        out_shape=outs,
        in_specs=specs or [VMEM] * len(args),
        out_specs=jax.tree.map(lambda _: VMEM, outs),
        scratch_shapes=list(scratch),
        cost_estimate=pl.CostEstimate(flops=flops, transcendentals=0, bytes_accessed=nbytes),
        compiler_params=pltpu.CompilerParams(vmem_limit_bytes=5 << 20),
    )(*args)


def dot(a, b):
    return jnp.dot(a, b, preferred_element_type=F32)


def dot_t(a, b):
    return lax.dot_general(a, b, (((0,), (0,)), ((), ())), preferred_element_type=F32)


def interleave(value, scratch_ref, dst_ref):
    count = value.shape[0] // SIDE
    for g in range(value.shape[1] // LANES):
        lanes = slice(g * LANES, (g + 1) * LANES)
        scratch_ref[g] = value[:, lanes]
        for t in range(SIDE // 2):
            pair = [scratch_ref[g, pl.ds(2 * t + h, count, stride=SIDE), :] for h in range(2)]
            dst_ref[2 * t * count : (2 * t + 2) * count, lanes] = jnp.concatenate(pair, axis=0).astype(BF16)


def restored(value, scratch_ref):
    count = value.shape[0] // SIDE
    columns = []
    for g in range(value.shape[1] // LANES):
        scratch_ref[g] = value[:, g * LANES : (g + 1) * LANES]
        columns.append(jnp.concatenate([scratch_ref[g, pl.ds(b, SIDE, stride=count), :] for b in range(count)], axis=0))
    return jnp.concatenate(columns, axis=1)


def build(half, sizes, blocks_hbm, row_hbm, col_hbm, blocks, ids, sems, stores):
    count, row_devs, ka_devs = sizes
    bits, row_bits = log2(count), log2(row_devs)
    copies = [pltpu.make_async_copy(h, ids.at[k : k + 1], sems.at[k]) for k, h in enumerate((row_hbm, col_hbm))]
    width = blocks.shape[1] // PIECES
    for k in range(PIECES):
        lanes = pl.ds(k * width, width)
        copies.append(pltpu.make_async_copy(blocks_hbm.at[:, lanes], blocks.at[:, lanes], sems.at[2 + k]))
    for copy in copies:
        copy.start()
    copies[0].wait()
    copies[1].wait()
    row = ids[0:1, :]
    col = ids[1:2, :]
    row_place = (row >> bits) & (row_devs - 1)
    ka_step = ((col >> (bits + row_bits)) - (row >> (bits + row_bits))) & (ka_devs - 1)
    row_step = (((col >> bits) & (row_devs - 1)) - row_place + 1) & (row_devs - 1)
    is_mate = (row_step >> 1) == ((row_place & 1) ^ 1)
    group = jnp.where(row_step == 1, 0, jnp.where(is_mate, 1, 2))
    band = group * count + (col & (count - 1))
    pairs = 3 * count // 2
    place = ((band & 1) * pairs + (band >> 1)) * count + (row & (count - 1))
    place = jnp.where((row >= 0) & (ka_step == half), place, -1)
    slots = blocks.shape[0]
    chosen = lax.broadcasted_iota(jnp.int32, (2 * pairs * count, slots), 0) == place
    chosen = jnp.where(chosen, 1.0, 0.0).astype(BF16)
    low = lax.broadcasted_iota(jnp.int32, (pairs * count, LANES), 1) < SIDE
    for u in range(SIDE // 4):
        if u % (SIDE // 4 // PIECES) == 0:
            copies[2 + u // (SIDE // 4 // PIECES)].wait()
        found = dot(chosen, blocks[:, u * 2 * LANES : (u + 1) * 2 * LANES])
        for w in range(2):
            t = 2 * u + w
            even = found[: pairs * count, w * LANES : (w + 1) * LANES]
            odd = found[pairs * count :, w * LANES : (w + 1) * LANES]
            first = jnp.where(low, even, pltpu.roll(odd, SIDE, 1))
            second = jnp.where(low, pltpu.roll(even, SIDE, 1), odd)
            for q in range(pairs):
                pair = [v[q * count : (q + 1) * count, :] for v in (first, second)]
                tile = jnp.concatenate(pair, axis=0).astype(BF16)
                per = pairs // 3
                lanes = slice((q % per) * LANES, (q % per + 1) * LANES)
                stores[q // per][2 * t * count : (2 * t + 2) * count, lanes] = tile


def emit(cross, wire, perm_ref, wire_ref, self_ref, mate_ref, far_ref):
    perm = perm_ref[...]
    wire_ref[...] = wire
    self_ref[...] = dot_t(cross[0][...], perm)
    for k, ref in ((2, far_ref), (1, mate_ref)):
        ref[0] = dot_t(cross[k][...], perm).astype(BF16)
        ref[1] = wire


def first_body(sizes, blocks_hbm, row_hbm, col_hbm, drive_hbm, relax_hbm, *refs):
    cross, (perm_ref, wire_ref, self_ref, mate_ref, far_ref, spread_ref) = refs[:3], refs[3:9]
    blocks, ids, drive, relax, scratch, sems = refs[9:]
    later = [
        pltpu.make_async_copy(drive_hbm, drive, sems.at[2 + PIECES]),
        pltpu.make_async_copy(relax_hbm, relax, sems.at[3 + PIECES]),
    ]
    for copy in later:
        copy.start()
    build(1, sizes, blocks_hbm, row_hbm, col_hbm, blocks, ids, sems, cross)
    for copy in later:
        copy.wait()
    spread_ref[...] = jnp.broadcast_to(relax[...], (LANES, relax.shape[1])).T
    field = drive[...]
    interleave(field, scratch, perm_ref)
    emit(cross, field.astype(BF16), perm_ref, wire_ref, self_ref, mate_ref, far_ref)


def second_body(sizes, blocks_hbm, row_hbm, col_hbm, *refs):
    build(0, sizes, blocks_hbm, row_hbm, col_hbm, *refs[3:], refs[:3])


def sent_terms(sent, fields, scratch, other):
    total = 0.0
    for matrix, field in zip(sent, fields):
        interleave(field[1].astype(F32), scratch, other)
        total += dot_t(matrix[...], other[...])
    return total


def own_body(*refs):
    mats, (wire_ref, perm_ref, mate_ref, far_ref), sent = refs[:3], refs[3:7], refs[7:-3]
    out_ref, scratch, other = refs[-3:]
    total = dot_t(mats[0][...], perm_ref[...])
    straight = dot(mats[0][...], wire_ref[...])
    straight += dot(mats[1][...], mate_ref[1])
    straight += dot(mats[2][...], far_ref[1])
    if sent:
        total += sent_terms(sent, (mate_ref, far_ref), scratch, other)
    out_ref[...] = total + restored(straight, scratch)


def with_cross(cross, nexts, known_ref, scratch):
    straight = dot(cross[0][...], nexts[0][...])
    straight += dot(cross[1][...], nexts[1][...])
    straight += dot(cross[2][...], nexts[2][...])
    return known_ref[...] + restored(straight, scratch)


def advanced(product, drive_ref, relax_ref):
    scale = jnp.concatenate([relax_ref[...]] * (product.shape[1] // LANES), axis=1)
    return drive_ref[...] + scale * product


def cross_body(*refs):
    refs[7][...] = with_cross(refs[:3], refs[3:6], refs[6], refs[8])


def update_body(*refs):
    cross, (known_ref, drive_ref, relax_ref, mate_in, far_in), sent = refs[:3], refs[3:8], refs[8:10]
    perm_ref, wire_ref, self_ref, mate_ref, far_ref, scratch, other = refs[10:]
    late = sent_terms(sent, (mate_in, far_in), scratch, other)
    field = advanced(known_ref[...] + late, drive_ref, relax_ref)
    interleave(field, scratch, perm_ref)
    emit(cross, field.astype(BF16), perm_ref, wire_ref, self_ref, mate_ref, far_ref)


def settle_body(own_ref, received_ref, out_ref):
    out_ref[...] = own_ref[...] + received_ref[...].astype(F32)


def final_body(*refs):
    product = with_cross(refs[:3], refs[3:6], refs[6], refs[10])
    refs[9][...] = advanced(product, *refs[7:9])


def local(drive, relax, blocks, row_block, col_block):
    rows, channels = drive.shape
    slots = blocks.shape[0]
    sizes = (rows // SIDE, lax.axis_size("rows"), lax.axis_size("ka"))
    small = jax.ShapeDtypeStruct((rows, channels), BF16)
    double = jax.ShapeDtypeStruct((2, rows, channels), BF16)
    wide = jax.ShapeDtypeStruct((rows, channels), F32)
    matrices = (jax.ShapeDtypeStruct((rows, rows), BF16),) * 3
    emitted = (small, small, wide, double, double)
    staging = pltpu.VMEM((channels // LANES, rows, LANES), F32)
    fetch = [pltpu.VMEM(blocks.shape, BF16), pltpu.VMEM((2, slots), jnp.int32)]
    row2 = row_block.reshape(1, -1)
    col2 = col_block.reshape(1, -1)
    relax2 = relax.reshape(1, -1)
    work = 2 * rows * rows * channels
    spread = jax.ShapeDtypeStruct((rows, LANES), F32)
    *cross, perm, wire, partial, to_mate, to_far, relax3 = call(
        functools.partial(first_body, sizes), (*matrices, *emitted, spread), 9 * work,
        [blocks, row2, col2, drive, relax2], [HBM] * 5,
        fetch + [pltpu.VMEM(drive.shape, F32), pltpu.VMEM((1, rows), F32), staging, pltpu.SemaphoreType.DMA((4 + PIECES,))],
    )

    extra = [staging, pltpu.VMEM((rows, channels), BF16)]
    for sweep in range(ITERS):
        down = shifted(wire, "ka", -1)
        from_far = far(to_far)
        from_mate = mate(to_mate)
        if sweep == 0:
            own = call(
                functools.partial(second_body, sizes), matrices, 6 * work, [blocks, row2, col2], [HBM] * 3,
                fetch + [pltpu.SemaphoreType.DMA((2 + PIECES,))],
            )
        if sweep == 0:
            from_far, _ = lax.optimization_barrier((from_far, own))
        got = (partial + from_mate[0].astype(F32) + from_far[0].astype(F32)).astype(BF16)
        received = shifted(got, "ka", 1)
        if sweep == 0:
            gated, down = lax.optimization_barrier((own[1:], down))
            sent = [mate(gated[0]), far(gated[1])]
        nexts = [down, mate(down), far(down)]
        args = [*own, wire, perm, from_mate, from_far, *(sent if sweep else [])]
        known = call(own_body, wide, 9 * work, args, scratch=extra)
        known = call(settle_body, wide, HEAVY * work, [known, received])
        if sweep + 1 == ITERS:
            return call(final_body, wide, 3 * work, [*cross, *nexts, known, drive, relax3], scratch=[staging])
        known = call(cross_body, wide, HEAVY * work, [*cross, *nexts, known], scratch=[staging])
        args = [*cross, known, drive, relax3, from_mate, from_far, *sent]
        perm, wire, partial, to_mate, to_far = call(update_body, emitted, 8 * work, args, scratch=extra)


def solution(mesh):
    spread = P(("ka", "rows"))
    wide = P(("ka", "rows"), None)
    return jax.shard_map(
        local, mesh=mesh, in_specs=(wide, spread, wide, spread, spread), out_specs=wide, check_vma=False
    )
```

```python
import functools

import jax
import jax.numpy as jnp
from jax import lax
from jax.experimental import pallas as pl
from jax.experimental.pallas import tpu as pltpu
from jax.sharding import PartitionSpec as P

SIDE = 64
LANES = 128
ITERS = 2
PIECES = 4
HEAVY = 90
BF16, F32 = jnp.bfloat16, jnp.float32
VMEM = pl.BlockSpec(memory_space=pltpu.VMEM)
HBM = pl.BlockSpec(memory_space=pltpu.HBM)


def log2(n):
    assert n & (n - 1) == 0
    return n.bit_length() - 1


def shifted(value, axis, steps):
    count = lax.axis_size(axis)
    return lax.ppermute(value, axis, [(source, (source + steps) % count) for source in range(count)])


def mate(value):
    return lax.ppermute(value, "rows", [(i, i ^ 1) for i in range(lax.axis_size("rows"))])


def far(value):
    count = lax.axis_size("rows")
    return lax.ppermute(value, "rows", [(i, (i + 1 if i & 1 else i - 1) % count) for i in range(count)])


def call(kernel, outs, flops, args, specs=None, scratch=()):
    if specs:
        args = [pltpu.with_memory_space_constraint(a, pltpu.HBM) if s is HBM else a for a, s in zip(args, specs)]
    nbytes = sum(a.size * a.dtype.itemsize for a in args)
    return pl.pallas_call(
        kernel,
        out_shape=outs,
        in_specs=specs or [VMEM] * len(args),
        out_specs=jax.tree.map(lambda _: VMEM, outs),
        scratch_shapes=list(scratch),
        cost_estimate=pl.CostEstimate(flops=flops, transcendentals=0, bytes_accessed=nbytes),
        compiler_params=pltpu.CompilerParams(vmem_limit_bytes=5 << 20),
    )(*args)


def dot(a, b):
    return jnp.dot(a, b, preferred_element_type=F32)


def dot_t(a, b):
    return lax.dot_general(a, b, (((0,), (0,)), ((), ())), preferred_element_type=F32)


def interleave(value, scratch_ref, dst_ref):
    count = value.shape[0] // SIDE
    for g in range(value.shape[1] // LANES):
        lanes = slice(g * LANES, (g + 1) * LANES)
        scratch_ref[g] = value[:, lanes]
        for t in range(SIDE // 2):
            pair = [scratch_ref[g, pl.ds(2 * t + h, count, stride=SIDE), :] for h in range(2)]
            dst_ref[2 * t * count : (2 * t + 2) * count, lanes] = jnp.concatenate(pair, axis=0).astype(BF16)


def restored(value, scratch_ref):
    count = value.shape[0] // SIDE
    columns = []
    for g in range(value.shape[1] // LANES):
        scratch_ref[g] = value[:, g * LANES : (g + 1) * LANES]
        columns.append(jnp.concatenate([scratch_ref[g, pl.ds(b, SIDE, stride=count), :] for b in range(count)], axis=0))
    return jnp.concatenate(columns, axis=1)


def build(half, sizes, blocks_hbm, row_hbm, col_hbm, blocks, ids, sems, stores):
    count, row_devs, ka_devs = sizes
    bits, row_bits = log2(count), log2(row_devs)
    copies = [pltpu.make_async_copy(h, ids.at[k : k + 1], sems.at[k]) for k, h in enumerate((row_hbm, col_hbm))]
    width = blocks.shape[1] // PIECES
    for k in range(PIECES):
        lanes = pl.ds(k * width, width)
        copies.append(pltpu.make_async_copy(blocks_hbm.at[:, lanes], blocks.at[:, lanes], sems.at[2 + k]))
    for copy in copies:
        copy.start()
    copies[0].wait()
    copies[1].wait()
    row = ids[0:1, :]
    col = ids[1:2, :]
    row_place = (row >> bits) & (row_devs - 1)
    ka_step = ((col >> (bits + row_bits)) - (row >> (bits + row_bits))) & (ka_devs - 1)
    row_step = (((col >> bits) & (row_devs - 1)) - row_place + 1) & (row_devs - 1)
    is_mate = (row_step >> 1) == ((row_place & 1) ^ 1)
    group = jnp.where(row_step == 1, 0, jnp.where(is_mate, 1, 2))
    band = group * count + (col & (count - 1))
    pairs = 3 * count // 2
    place = ((band & 1) * pairs + (band >> 1)) * count + (row & (count - 1))
    place = jnp.where((row >= 0) & (ka_step == half), place, -1)
    slots = blocks.shape[0]
    chosen = lax.broadcasted_iota(jnp.int32, (2 * pairs * count, slots), 0) == place
    chosen = jnp.where(chosen, 1.0, 0.0).astype(BF16)
    low = lax.broadcasted_iota(jnp.int32, (pairs * count, LANES), 1) < SIDE
    for u in range(SIDE // 4):
        if u % (SIDE // 4 // PIECES) == 0:
            copies[2 + u // (SIDE // 4 // PIECES)].wait()
        found = dot(chosen, blocks[:, u * 2 * LANES : (u + 1) * 2 * LANES])
        for w in range(2):
            t = 2 * u + w
            even = found[: pairs * count, w * LANES : (w + 1) * LANES]
            odd = found[pairs * count :, w * LANES : (w + 1) * LANES]
            first = jnp.where(low, even, pltpu.roll(odd, SIDE, 1))
            second = jnp.where(low, pltpu.roll(even, SIDE, 1), odd)
            for q in range(pairs):
                pair = [v[q * count : (q + 1) * count, :] for v in (first, second)]
                tile = jnp.concatenate(pair, axis=0).astype(BF16)
                per = pairs // 3
                lanes = slice((q % per) * LANES, (q % per + 1) * LANES)
                stores[q // per][2 * t * count : (2 * t + 2) * count, lanes] = tile


def emit(cross, wire, perm_ref, wire_ref, self_ref, mate_ref, far_ref):
    perm = perm_ref[...]
    wire_ref[...] = wire
    self_ref[...] = dot_t(cross[0][...], perm)
    for k, ref in ((2, far_ref), (1, mate_ref)):
        ref[0] = dot_t(cross[k][...], perm).astype(BF16)
        ref[1] = wire


def first_body(sizes, blocks_hbm, row_hbm, col_hbm, drive_hbm, relax_hbm, *refs):
    cross, (perm_ref, wire_ref, self_ref, mate_ref, far_ref, spread_ref) = refs[:3], refs[3:9]
    blocks, ids, drive, relax, scratch, sems = refs[9:]
    later = [
        pltpu.make_async_copy(drive_hbm, drive, sems.at[2 + PIECES]),
        pltpu.make_async_copy(relax_hbm, relax, sems.at[3 + PIECES]),
    ]
    for copy in later:
        copy.start()
    build(1, sizes, blocks_hbm, row_hbm, col_hbm, blocks, ids, sems, cross)
    for copy in later:
        copy.wait()
    spread_ref[...] = jnp.broadcast_to(relax[...], (LANES, relax.shape[1])).T
    field = drive[...]
    interleave(field, scratch, perm_ref)
    emit(cross, field.astype(BF16), perm_ref, wire_ref, self_ref, mate_ref, far_ref)


def second_body(sizes, blocks_hbm, row_hbm, col_hbm, perm_ref, *refs):
    own, outs, (blocks, ids, sems) = refs[:3], refs[3:6], refs[6:]
    build(0, sizes, blocks_hbm, row_hbm, col_hbm, blocks, ids, sems, own)
    partials(own, perm_ref, outs)


def partials(mats, perm_ref, outs):
    perm = perm_ref[...]
    for matrix, ref in zip(mats, outs):
        ref[...] = dot_t(matrix[...], perm).astype(ref.dtype)


def third_body(*refs):
    partials(refs[:3], refs[3], refs[4:])


def own_body(*refs):
    mats, (wire_ref, mate_ref, far_ref, self_ref), (out_ref, scratch) = refs[:3], refs[3:7], refs[7:]
    straight = dot(mats[0][...], wire_ref[...])
    straight += dot(mats[1][...], mate_ref[1])
    straight += dot(mats[2][...], far_ref[1])
    out_ref[...] = self_ref[...] + restored(straight, scratch)


def with_cross(cross, down_ref, mate_ref, far_ref, known_ref, scratch):
    straight = dot(cross[0][...], down_ref[...])
    straight += dot(cross[1][...], mate_ref[0])
    straight += dot(cross[2][...], far_ref[0])
    return known_ref[...] + mate_ref[1].astype(F32) + far_ref[1].astype(F32) + restored(straight, scratch)


def advanced(product, drive_ref, relax_ref):
    scale = jnp.concatenate([relax_ref[...]] * (product.shape[1] // LANES), axis=1)
    return drive_ref[...] + scale * product


def update_body(*refs):
    cross, nexts, (drive_ref, relax_ref) = refs[:3], refs[3:7], refs[7:9]
    perm_ref, wire_ref, self_ref, mate_ref, far_ref, scratch = refs[9:]
    field = advanced(with_cross(cross, *nexts, scratch), drive_ref, relax_ref)
    interleave(field, scratch, perm_ref)
    emit(cross, field.astype(BF16), perm_ref, wire_ref, self_ref, mate_ref, far_ref)


def settle_body(own_ref, received_ref, out_ref):
    out_ref[...] = own_ref[...] + received_ref[...].astype(F32)


def final_body(*refs):
    product = with_cross(refs[:3], *refs[3:7], refs[10])
    refs[9][...] = advanced(product, *refs[7:9])


def local(drive, relax, blocks, row_block, col_block):
    rows, channels = drive.shape
    slots = blocks.shape[0]
    sizes = (rows // SIDE, lax.axis_size("rows"), lax.axis_size("ka"))
    small = jax.ShapeDtypeStruct((rows, channels), BF16)
    double = jax.ShapeDtypeStruct((2, rows, channels), BF16)
    wide = jax.ShapeDtypeStruct((rows, channels), F32)
    matrices = (jax.ShapeDtypeStruct((rows, rows), BF16),) * 3
    emitted = (small, small, wide, double, double)
    staging = pltpu.VMEM((channels // LANES, rows, LANES), F32)
    fetch = [pltpu.VMEM(blocks.shape, BF16), pltpu.VMEM((2, slots), jnp.int32)]
    row2 = row_block.reshape(1, -1)
    col2 = col_block.reshape(1, -1)
    relax2 = relax.reshape(1, -1)
    work = 2 * rows * rows * channels
    spread = jax.ShapeDtypeStruct((rows, LANES), F32)
    *cross, perm, wire, partial, to_mate, to_far, relax3 = call(
        functools.partial(first_body, sizes), (*matrices, *emitted, spread), 9 * work,
        [blocks, row2, col2, drive, relax2], [HBM] * 5,
        fetch + [pltpu.VMEM(drive.shape, F32), pltpu.VMEM((1, rows), F32), staging, pltpu.SemaphoreType.DMA((4 + PIECES,))],
    )

    for sweep in range(ITERS):
        down = shifted(wire, "ka", -1)
        from_far = far(to_far)
        from_mate = mate(to_mate)
        if sweep == 0:
            *own, own_self, own_mate, own_far = call(
                functools.partial(second_body, sizes), (*matrices, wide, small, small), 9 * work,
                [blocks, row2, col2, perm], [HBM] * 3 + [VMEM], fetch + [pltpu.SemaphoreType.DMA((2 + PIECES,))],
            )
        else:
            own_self, own_mate, own_far = call(third_body, (wide, small, small), 3 * work, [*own, perm])
        from_far, _ = lax.optimization_barrier((from_far, own_self))
        got = (partial + from_mate[0].astype(F32) + from_far[0].astype(F32)).astype(BF16)
        received = shifted(got, "ka", 1)
        second_mate = mate(jnp.stack([down, own_mate]))
        second_far = far(jnp.stack([down, own_far]))
        known = call(own_body, wide, 3 * work, [*own, wire, from_mate, from_far, own_self], scratch=[staging])
        known = call(settle_body, wide, HEAVY * work, [known, received])
        args = [*cross, down, second_mate, second_far, known, drive, relax3]
        if sweep + 1 == ITERS:
            return call(final_body, wide, 3 * work, args, scratch=[staging])
        perm, wire, partial, to_mate, to_far = call(update_body, emitted, 6 * work, args, scratch=[staging])


def solution(mesh):
    spread = P(("ka", "rows"))
    wide = P(("ka", "rows"), None)
    return jax.shard_map(
        local, mesh=mesh, in_specs=(wide, spread, wide, spread, spread), out_specs=wide, check_vma=False
    )
```

```python
import functools

import jax
import jax.numpy as jnp
from jax import lax
from jax.experimental import pallas as pl
from jax.experimental.pallas import tpu as pltpu
from jax.sharding import PartitionSpec as P

SIDE = 64
LANES = 128
ITERS = 2
PIECES = 4
HEAVY = 90
BF16, F32 = jnp.bfloat16, jnp.float32
VMEM = pl.BlockSpec(memory_space=pltpu.VMEM)
HBM = pl.BlockSpec(memory_space=pltpu.HBM)


def log2(n):
    assert n & (n - 1) == 0
    return n.bit_length() - 1


def shifted(value, axis, steps):
    count = lax.axis_size(axis)
    return lax.ppermute(value, axis, [(source, (source + steps) % count) for source in range(count)])


def mate(value):
    return lax.ppermute(value, "rows", [(i, i ^ 1) for i in range(lax.axis_size("rows"))])


def far(value):
    count = lax.axis_size("rows")
    return lax.ppermute(value, "rows", [(i, (i + 1 if i & 1 else i - 1) % count) for i in range(count)])


def call(kernel, outs, flops, args, specs=None, scratch=()):
    if specs:
        args = [pltpu.with_memory_space_constraint(a, pltpu.HBM) if s is HBM else a for a, s in zip(args, specs)]
    nbytes = sum(a.size * a.dtype.itemsize for a in args)
    return pl.pallas_call(
        kernel,
        out_shape=outs,
        in_specs=specs or [VMEM] * len(args),
        out_specs=jax.tree.map(lambda _: VMEM, outs),
        scratch_shapes=list(scratch),
        cost_estimate=pl.CostEstimate(flops=flops, transcendentals=0, bytes_accessed=nbytes),
        compiler_params=pltpu.CompilerParams(vmem_limit_bytes=5 << 20),
    )(*args)


def dot(a, b):
    return jnp.dot(a, b, preferred_element_type=F32)


def dot_t(a, b):
    return lax.dot_general(a, b, (((0,), (0,)), ((), ())), preferred_element_type=F32)


def interleave(value, scratch_ref, dst_ref):
    count = value.shape[0] // SIDE
    for g in range(value.shape[1] // LANES):
        lanes = slice(g * LANES, (g + 1) * LANES)
        scratch_ref[g] = value[:, lanes]
        for t in range(SIDE // 2):
            pair = [scratch_ref[g, pl.ds(2 * t + h, count, stride=SIDE), :] for h in range(2)]
            dst_ref[2 * t * count : (2 * t + 2) * count, lanes] = jnp.concatenate(pair, axis=0).astype(BF16)


def restored(value, scratch_ref):
    count = value.shape[0] // SIDE
    columns = []
    for g in range(value.shape[1] // LANES):
        scratch_ref[g] = value[:, g * LANES : (g + 1) * LANES]
        columns.append(jnp.concatenate([scratch_ref[g, pl.ds(b, SIDE, stride=count), :] for b in range(count)], axis=0))
    return jnp.concatenate(columns, axis=1)


def build(half, sizes, blocks_hbm, row_hbm, col_hbm, blocks, ids, sems, stores):
    count, row_devs, ka_devs = sizes
    bits, row_bits = log2(count), log2(row_devs)
    copies = [pltpu.make_async_copy(h, ids.at[k : k + 1], sems.at[k]) for k, h in enumerate((row_hbm, col_hbm))]
    width = blocks.shape[1] // PIECES
    for k in range(PIECES):
        lanes = pl.ds(k * width, width)
        copies.append(pltpu.make_async_copy(blocks_hbm.at[:, lanes], blocks.at[:, lanes], sems.at[2 + k]))
    for copy in copies:
        copy.start()
    copies[0].wait()
    copies[1].wait()
    row = ids[0:1, :]
    col = ids[1:2, :]
    row_place = (row >> bits) & (row_devs - 1)
    ka_step = ((col >> (bits + row_bits)) - (row >> (bits + row_bits))) & (ka_devs - 1)
    row_step = (((col >> bits) & (row_devs - 1)) - row_place + 1) & (row_devs - 1)
    is_mate = (row_step >> 1) == ((row_place & 1) ^ 1)
    group = jnp.where(row_step == 1, 0, jnp.where(is_mate, 1, 2))
    band = group * count + (col & (count - 1))
    pairs = 3 * count // 2
    place = ((band & 1) * pairs + (band >> 1)) * count + (row & (count - 1))
    place = jnp.where((row >= 0) & (ka_step == half), place, -1)
    slots = blocks.shape[0]
    chosen = lax.broadcasted_iota(jnp.int32, (2 * pairs * count, slots), 0) == place
    chosen = jnp.where(chosen, 1.0, 0.0).astype(BF16)
    low = lax.broadcasted_iota(jnp.int32, (pairs * count, LANES), 1) < SIDE
    for u in range(SIDE // 4):
        if u % (SIDE // 4 // PIECES) == 0:
            copies[2 + u // (SIDE // 4 // PIECES)].wait()
        found = dot(chosen, blocks[:, u * 2 * LANES : (u + 1) * 2 * LANES])
        for w in range(2):
            t = 2 * u + w
            even = found[: pairs * count, w * LANES : (w + 1) * LANES]
            odd = found[pairs * count :, w * LANES : (w + 1) * LANES]
            first = jnp.where(low, even, pltpu.roll(odd, SIDE, 1))
            second = jnp.where(low, pltpu.roll(even, SIDE, 1), odd)
            for q in range(pairs):
                pair = [v[q * count : (q + 1) * count, :] for v in (first, second)]
                tile = jnp.concatenate(pair, axis=0).astype(BF16)
                per = pairs // 3
                lanes = slice((q % per) * LANES, (q % per + 1) * LANES)
                stores[q // per][2 * t * count : (2 * t + 2) * count, lanes] = tile


def emit(cross, wire, perm_ref, wire_ref, self_ref, mate_ref, far_ref):
    perm = perm_ref[...]
    wire_ref[...] = wire
    self_ref[...] = dot_t(cross[0][...], perm)
    far_ref[...] = dot_t(cross[2][...], perm).astype(BF16)
    mate_ref[0] = dot_t(cross[1][...], perm).astype(BF16)
    mate_ref[1] = wire


def first_body(sizes, blocks_hbm, row_hbm, col_hbm, drive_hbm, relax_hbm, *refs):
    cross, (perm_ref, wire_ref, self_ref, mate_ref, far_ref, spread_ref) = refs[:3], refs[3:9]
    blocks, ids, drive, relax, scratch, sems = refs[9:]
    later = [
        pltpu.make_async_copy(drive_hbm, drive, sems.at[2 + PIECES]),
        pltpu.make_async_copy(relax_hbm, relax, sems.at[3 + PIECES]),
    ]
    for copy in later:
        copy.start()
    build(1, sizes, blocks_hbm, row_hbm, col_hbm, blocks, ids, sems, cross)
    for copy in later:
        copy.wait()
    spread_ref[...] = jnp.broadcast_to(relax[...], (LANES, relax.shape[1])).T
    field = drive[...]
    interleave(field, scratch, perm_ref)
    emit(cross, field.astype(BF16), perm_ref, wire_ref, self_ref, mate_ref, far_ref)


def second_body(sizes, blocks_hbm, row_hbm, col_hbm, perm_ref, wire_ref, *refs):
    own, outs, (blocks, ids, sems) = refs[:3], refs[3:6], refs[6:]
    build(0, sizes, blocks_hbm, row_hbm, col_hbm, blocks, ids, sems, own)
    own_partials(*own, perm_ref, wire_ref, *outs)


def own_partials(self_in, mate_in, far_in, perm_ref, wire_ref, self_ref, mate_ref, far_ref):
    perm = perm_ref[...]
    far_ref[0] = wire_ref[...]
    far_ref[1] = dot_t(far_in[...], perm).astype(BF16)
    mate_ref[...] = dot_t(mate_in[...], perm).astype(BF16)
    self_ref[...] = dot_t(self_in[...], perm)


def own_body(*refs):
    mats, (wire_ref, mate_ref, far_ref, self_ref), (out_ref, scratch) = refs[:3], refs[3:7], refs[7:]
    straight = dot(mats[0][...], wire_ref[...])
    straight += dot(mats[1][...], mate_ref[1])
    straight += dot(mats[2][...], far_ref[0])
    out_ref[...] = self_ref[...] + restored(straight, scratch)


def with_cross(cross, down_ref, mate_ref, far_ref, other_ref, known_ref, scratch):
    straight = dot(cross[0][...], down_ref[...])
    straight += dot(cross[1][...], mate_ref[0])
    straight += dot(cross[2][...], far_ref[...])
    return known_ref[...] + mate_ref[1].astype(F32) + other_ref[1].astype(F32) + restored(straight, scratch)


def advanced(product, drive_ref, relax_ref):
    scale = jnp.concatenate([relax_ref[...]] * (product.shape[1] // LANES), axis=1)
    return drive_ref[...] + scale * product


def update_body(*refs):
    cross, nexts, (drive_ref, relax_ref) = refs[:3], refs[3:8], refs[8:10]
    perm_ref, wire_ref, self_ref, mate_ref, far_ref, scratch = refs[10:]
    field = advanced(with_cross(cross, *nexts, scratch), drive_ref, relax_ref)
    interleave(field, scratch, perm_ref)
    emit(cross, field.astype(BF16), perm_ref, wire_ref, self_ref, mate_ref, far_ref)


def settle_body(own_ref, received_ref, out_ref):
    out_ref[...] = own_ref[...] + received_ref[...].astype(F32)


def final_body(*refs):
    product = with_cross(refs[:3], *refs[3:8], refs[11])
    refs[10][...] = advanced(product, *refs[8:10])


def local(drive, relax, blocks, row_block, col_block):
    rows, channels = drive.shape
    slots = blocks.shape[0]
    sizes = (rows // SIDE, lax.axis_size("rows"), lax.axis_size("ka"))
    small = jax.ShapeDtypeStruct((rows, channels), BF16)
    double = jax.ShapeDtypeStruct((2, rows, channels), BF16)
    wide = jax.ShapeDtypeStruct((rows, channels), F32)
    matrices = (jax.ShapeDtypeStruct((rows, rows), BF16),) * 3
    emitted = (small, small, wide, double, small)
    staging = pltpu.VMEM((channels // LANES, rows, LANES), F32)
    fetch = [pltpu.VMEM(blocks.shape, BF16), pltpu.VMEM((2, slots), jnp.int32)]
    row2 = row_block.reshape(1, -1)
    col2 = col_block.reshape(1, -1)
    relax2 = relax.reshape(1, -1)
    work = 2 * rows * rows * channels
    spread = jax.ShapeDtypeStruct((rows, LANES), F32)
    *cross, perm, wire, partial, to_mate, to_far, relax3 = call(
        functools.partial(first_body, sizes), (*matrices, *emitted, spread), 9 * work,
        [blocks, row2, col2, drive, relax2], [HBM] * 5,
        fetch + [pltpu.VMEM(drive.shape, F32), pltpu.VMEM((1, rows), F32), staging, pltpu.SemaphoreType.DMA((4 + PIECES,))],
    )

    for sweep in range(ITERS):
        down = shifted(wire, "ka", -1)
        from_far = far(to_far)
        from_mate = mate(to_mate)
        if sweep == 0:
            *own, own_self, own_mate, own_far = call(
                functools.partial(second_body, sizes), (*matrices, wide, small, double), 9 * work,
                [blocks, row2, col2, perm, wire], [HBM] * 3 + [VMEM] * 2, fetch + [pltpu.SemaphoreType.DMA((2 + PIECES,))],
            )
        else:
            own_self, own_mate, own_far = call(own_partials, (wide, small, double), 3 * work, [*own, perm, wire])
        other_far = far(own_far)
        from_far, _ = lax.optimization_barrier((from_far, own_self))
        got = (partial + from_mate[0].astype(F32) + from_far.astype(F32)).astype(BF16)
        received = shifted(got, "ka", 1)
        next_mate = mate(jnp.stack([down, own_mate]))
        next_far = far(down)
        known = call(own_body, wide, 3 * work, [*own, wire, from_mate, other_far, own_self], scratch=[staging])
        known = call(settle_body, wide, HEAVY * work, [known, received])
        args = [*cross, down, next_mate, next_far, other_far, known, drive, relax3]
        if sweep + 1 == ITERS:
            return call(final_body, wide, 3 * work, args, scratch=[staging])
        perm, wire, partial, to_mate, to_far = call(update_body, emitted, 6 * work, args, scratch=[staging])


def solution(mesh):
    spread = P(("ka", "rows"))
    wide = P(("ka", "rows"), None)
    return jax.shard_map(
        local, mesh=mesh, in_specs=(wide, spread, wide, spread, spread), out_specs=wide, check_vma=False
    )
```

```python
import functools

import jax
import jax.numpy as jnp
from jax import lax
from jax.experimental import pallas as pl
from jax.experimental.pallas import tpu as pltpu
from jax.sharding import PartitionSpec as P

SIDE = 64
LANES = 128
ITERS = 2
PIECES = 4
HEAVY = 90
BF16, F32 = jnp.bfloat16, jnp.float32
VMEM = pl.BlockSpec(memory_space=pltpu.VMEM)
HBM = pl.BlockSpec(memory_space=pltpu.HBM)


def log2(n):
    assert n & (n - 1) == 0
    return n.bit_length() - 1


def shifted(value, axis, steps):
    count = lax.axis_size(axis)
    return lax.ppermute(value, axis, [(source, (source + steps) % count) for source in range(count)])


def mate(value):
    return lax.ppermute(value, "rows", [(i, i ^ 1) for i in range(lax.axis_size("rows"))])


def far(value):
    count = lax.axis_size("rows")
    return lax.ppermute(value, "rows", [(i, (i + 1 if i & 1 else i - 1) % count) for i in range(count)])


def call(kernel, outs, flops, args, specs=None, scratch=()):
    if specs:
        args = [pltpu.with_memory_space_constraint(a, pltpu.HBM) if s is HBM else a for a, s in zip(args, specs)]
    nbytes = sum(a.size * a.dtype.itemsize for a in args)
    return pl.pallas_call(
        kernel,
        out_shape=outs,
        in_specs=specs or [VMEM] * len(args),
        out_specs=jax.tree.map(lambda _: VMEM, outs),
        scratch_shapes=list(scratch),
        cost_estimate=pl.CostEstimate(flops=flops, transcendentals=0, bytes_accessed=nbytes),
        compiler_params=pltpu.CompilerParams(vmem_limit_bytes=5 << 20),
    )(*args)


def dot(a, b):
    return jnp.dot(a, b, preferred_element_type=F32)


def dot_t(a, b):
    return lax.dot_general(a, b, (((0,), (0,)), ((), ())), preferred_element_type=F32)


def interleave(value, scratch_ref, dst_ref):
    count = value.shape[0] // SIDE
    for g in range(value.shape[1] // LANES):
        lanes = slice(g * LANES, (g + 1) * LANES)
        scratch_ref[g] = value[:, lanes]
        for t in range(SIDE // 2):
            pair = [scratch_ref[g, pl.ds(2 * t + h, count, stride=SIDE), :] for h in range(2)]
            dst_ref[2 * t * count : (2 * t + 2) * count, lanes] = jnp.concatenate(pair, axis=0).astype(BF16)


def restored(value, scratch_ref):
    count = value.shape[0] // SIDE
    columns = []
    for g in range(value.shape[1] // LANES):
        scratch_ref[g] = value[:, g * LANES : (g + 1) * LANES]
        columns.append(jnp.concatenate([scratch_ref[g, pl.ds(b, SIDE, stride=count), :] for b in range(count)], axis=0))
    return jnp.concatenate(columns, axis=1)


def build(half, sizes, blocks_hbm, row_hbm, col_hbm, blocks, ids, sems, stores):
    count, row_devs, ka_devs = sizes
    bits, row_bits = log2(count), log2(row_devs)
    copies = [pltpu.make_async_copy(h, ids.at[k : k + 1], sems.at[k]) for k, h in enumerate((row_hbm, col_hbm))]
    width = blocks.shape[1] // PIECES
    for k in range(PIECES):
        lanes = pl.ds(k * width, width)
        copies.append(pltpu.make_async_copy(blocks_hbm.at[:, lanes], blocks.at[:, lanes], sems.at[2 + k]))
    for copy in copies:
        copy.start()
    copies[0].wait()
    copies[1].wait()
    row = ids[0:1, :]
    col = ids[1:2, :]
    row_place = (row >> bits) & (row_devs - 1)
    ka_step = ((col >> (bits + row_bits)) - (row >> (bits + row_bits))) & (ka_devs - 1)
    row_step = (((col >> bits) & (row_devs - 1)) - row_place + 1) & (row_devs - 1)
    is_mate = (row_step >> 1) == ((row_place & 1) ^ 1)
    group = jnp.where(row_step == 1, 0, jnp.where(is_mate, 1, 2))
    band = group * count + (col & (count - 1))
    pairs = 3 * count // 2
    place = ((band & 1) * pairs + (band >> 1)) * count + (row & (count - 1))
    place = jnp.where((row >= 0) & (ka_step == half), place, -1)
    slots = blocks.shape[0]
    chosen = lax.broadcasted_iota(jnp.int32, (2 * pairs * count, slots), 0) == place
    chosen = jnp.where(chosen, 1.0, 0.0).astype(BF16)
    low = lax.broadcasted_iota(jnp.int32, (pairs * count, LANES), 1) < SIDE
    for u in range(SIDE // 4):
        if u % (SIDE // 4 // PIECES) == 0:
            copies[2 + u // (SIDE // 4 // PIECES)].wait()
        found = dot(chosen, blocks[:, u * 2 * LANES : (u + 1) * 2 * LANES])
        for w in range(2):
            t = 2 * u + w
            even = found[: pairs * count, w * LANES : (w + 1) * LANES]
            odd = found[pairs * count :, w * LANES : (w + 1) * LANES]
            first = jnp.where(low, even, pltpu.roll(odd, SIDE, 1))
            second = jnp.where(low, pltpu.roll(even, SIDE, 1), odd)
            for q in range(pairs):
                pair = [v[q * count : (q + 1) * count, :] for v in (first, second)]
                tile = jnp.concatenate(pair, axis=0).astype(BF16)
                per = pairs // 3
                lanes = slice((q % per) * LANES, (q % per + 1) * LANES)
                stores[q // per][2 * t * count : (2 * t + 2) * count, lanes] = tile


def emit(cross, wire, perm_ref, wire_ref, self_ref, mate_ref, far_ref):
    perm = perm_ref[...]
    wire_ref[...] = wire
    self_ref[...] = dot_t(cross[0][...], perm)
    for k, ref in ((2, far_ref), (1, mate_ref)):
        ref[0] = dot_t(cross[k][...], perm).astype(BF16)
        ref[1] = wire


def first_body(sizes, blocks_hbm, row_hbm, col_hbm, drive_hbm, relax_hbm, *refs):
    cross, (perm_ref, wire_ref, self_ref, mate_ref, far_ref, spread_ref) = refs[:3], refs[3:9]
    blocks, ids, drive, relax, scratch, sems = refs[9:]
    later = [
        pltpu.make_async_copy(drive_hbm, drive, sems.at[2 + PIECES]),
        pltpu.make_async_copy(relax_hbm, relax, sems.at[3 + PIECES]),
    ]
    for copy in later:
        copy.start()
    build(1, sizes, blocks_hbm, row_hbm, col_hbm, blocks, ids, sems, cross)
    for copy in later:
        copy.wait()
    spread_ref[...] = jnp.broadcast_to(relax[...], (LANES, relax.shape[1])).T
    field = drive[...]
    interleave(field, scratch, perm_ref)
    emit(cross, field.astype(BF16), perm_ref, wire_ref, self_ref, mate_ref, far_ref)


def second_body(sizes, blocks_hbm, row_hbm, col_hbm, perm_ref, *refs):
    own, outs, (blocks, ids, sems) = refs[:3], refs[3:6], refs[6:]
    build(0, sizes, blocks_hbm, row_hbm, col_hbm, blocks, ids, sems, own)
    partials(own, perm_ref, outs)


def partials(mats, perm_ref, outs):
    perm = perm_ref[...]
    for matrix, ref in zip(mats, outs):
        ref[...] = dot_t(matrix[...], perm).astype(ref.dtype)


def third_body(*refs):
    partials(refs[:3], refs[3], refs[4:])


def own_body(*refs):
    mats, (wire_ref, mate_ref, far_ref, self_ref), (out_ref, scratch) = refs[:3], refs[3:7], refs[7:]
    straight = dot(mats[0][...], wire_ref[...])
    straight += dot(mats[1][...], mate_ref[1])
    straight += dot(mats[2][...], far_ref[1])
    out_ref[...] = self_ref[...] + restored(straight, scratch)


def with_cross(cross, down_ref, mate_ref, far_ref, known_ref, scratch):
    straight = dot(cross[0][...], down_ref[...])
    straight += dot(cross[1][...], mate_ref[0])
    straight += dot(cross[2][...], far_ref[0])
    return known_ref[...] + mate_ref[1].astype(F32) + far_ref[1].astype(F32) + restored(straight, scratch)


def advanced(product, drive_ref, relax_ref):
    scale = jnp.concatenate([relax_ref[...]] * (product.shape[1] // LANES), axis=1)
    return drive_ref[...] + scale * product


def update_body(*refs):
    cross, nexts, (drive_ref, relax_ref) = refs[:3], refs[3:7], refs[7:9]
    perm_ref, wire_ref, self_ref, mate_ref, far_ref, scratch = refs[9:]
    field = advanced(with_cross(cross, *nexts, scratch), drive_ref, relax_ref)
    interleave(field, scratch, perm_ref)
    emit(cross, field.astype(BF16), perm_ref, wire_ref, self_ref, mate_ref, far_ref)


def settle_body(own_ref, received_ref, out_ref):
    out_ref[...] = own_ref[...] + received_ref[...].astype(F32)


def pack_body(down_ref, own_mate, own_far, mate_ref, far_ref):
    for ref, own in ((mate_ref, own_mate), (far_ref, own_far)):
        ref[0] = down_ref[...]
        ref[1] = own[...]


def final_body(*refs):
    product = with_cross(refs[:3], *refs[3:7], refs[10])
    refs[9][...] = advanced(product, *refs[7:9])


def local(drive, relax, blocks, row_block, col_block):
    rows, channels = drive.shape
    slots = blocks.shape[0]
    sizes = (rows // SIDE, lax.axis_size("rows"), lax.axis_size("ka"))
    small = jax.ShapeDtypeStruct((rows, channels), BF16)
    double = jax.ShapeDtypeStruct((2, rows, channels), BF16)
    wide = jax.ShapeDtypeStruct((rows, channels), F32)
    matrices = (jax.ShapeDtypeStruct((rows, rows), BF16),) * 3
    emitted = (small, small, wide, double, double)
    staging = pltpu.VMEM((channels // LANES, rows, LANES), F32)
    fetch = [pltpu.VMEM(blocks.shape, BF16), pltpu.VMEM((2, slots), jnp.int32)]
    row2 = row_block.reshape(1, -1)
    col2 = col_block.reshape(1, -1)
    relax2 = relax.reshape(1, -1)
    work = 2 * rows * rows * channels
    spread = jax.ShapeDtypeStruct((rows, LANES), F32)
    *cross, perm, wire, partial, to_mate, to_far, relax3 = call(
        functools.partial(first_body, sizes), (*matrices, *emitted, spread), 9 * work,
        [blocks, row2, col2, drive, relax2], [HBM] * 5,
        fetch + [pltpu.VMEM(drive.shape, F32), pltpu.VMEM((1, rows), F32), staging, pltpu.SemaphoreType.DMA((4 + PIECES,))],
    )

    for sweep in range(ITERS):
        down = shifted(wire, "ka", -1)
        from_far = far(to_far)
        from_mate = mate(to_mate)
        if sweep == 0:
            *own, own_self, own_mate, own_far = call(
                functools.partial(second_body, sizes), (*matrices, wide, small, small), 9 * work,
                [blocks, row2, col2, perm], [HBM] * 3 + [VMEM], fetch + [pltpu.SemaphoreType.DMA((2 + PIECES,))],
            )
        else:
            own_self, own_mate, own_far = call(third_body, (wide, small, small), 3 * work, [*own, perm])
        next_mate, next_far = call(pack_body, (double, double), HEAVY * work, [down, own_mate, own_far])
        from_far, _ = lax.optimization_barrier((from_far, next_far))
        got = (partial + from_mate[0].astype(F32) + from_far[0].astype(F32)).astype(BF16)
        received = shifted(got, "ka", 1)
        second_mate = mate(next_mate)
        second_far = far(next_far)
        known = call(own_body, wide, 3 * work, [*own, wire, from_mate, from_far, own_self], scratch=[staging])
        known = call(settle_body, wide, HEAVY * work, [known, received])
        args = [*cross, down, second_mate, second_far, known, drive, relax3]
        if sweep + 1 == ITERS:
            return call(final_body, wide, 3 * work, args, scratch=[staging])
        perm, wire, partial, to_mate, to_far = call(update_body, emitted, 6 * work, args, scratch=[staging])


def solution(mesh):
    spread = P(("ka", "rows"))
    wide = P(("ka", "rows"), None)
    return jax.shard_map(
        local, mesh=mesh, in_specs=(wide, spread, wide, spread, spread), out_specs=wide, check_vma=False
    )
```

```python
import functools

import jax
import jax.numpy as jnp
from jax import lax
from jax.experimental import pallas as pl
from jax.experimental.pallas import tpu as pltpu
from jax.sharding import PartitionSpec as P

SIDE = 64
LANES = 128
ITERS = 2
PIECES = 4
HEAVY = 90
BF16, F32 = jnp.bfloat16, jnp.float32
VMEM = pl.BlockSpec(memory_space=pltpu.VMEM)
HBM = pl.BlockSpec(memory_space=pltpu.HBM)


def log2(n):
    assert n & (n - 1) == 0
    return n.bit_length() - 1


def shifted(value, axis, steps):
    count = lax.axis_size(axis)
    return lax.ppermute(value, axis, [(source, (source + steps) % count) for source in range(count)])


def mate(value):
    return lax.ppermute(value, "rows", [(i, i ^ 1) for i in range(lax.axis_size("rows"))])


def far(value):
    count = lax.axis_size("rows")
    return lax.ppermute(value, "rows", [(i, (i + 1 if i & 1 else i - 1) % count) for i in range(count)])


def call(kernel, outs, flops, args, specs=None, scratch=()):
    if specs:
        args = [pltpu.with_memory_space_constraint(a, pltpu.HBM) if s is HBM else a for a, s in zip(args, specs)]
    nbytes = sum(a.size * a.dtype.itemsize for a in args)
    return pl.pallas_call(
        kernel,
        out_shape=outs,
        in_specs=specs or [VMEM] * len(args),
        out_specs=jax.tree.map(lambda _: VMEM, outs),
        scratch_shapes=list(scratch),
        cost_estimate=pl.CostEstimate(flops=flops, transcendentals=0, bytes_accessed=nbytes),
        compiler_params=pltpu.CompilerParams(vmem_limit_bytes=5 << 20),
    )(*args)


def dot(a, b):
    return jnp.dot(a, b, preferred_element_type=F32)


def dot_t(a, b):
    return lax.dot_general(a, b, (((0,), (0,)), ((), ())), preferred_element_type=F32)


def interleave(value, scratch_ref, dst_ref):
    count = value.shape[0] // SIDE
    for g in range(value.shape[1] // LANES):
        lanes = slice(g * LANES, (g + 1) * LANES)
        scratch_ref[g] = value[:, lanes]
        for t in range(SIDE // 2):
            pair = [scratch_ref[g, pl.ds(2 * t + h, count, stride=SIDE), :] for h in range(2)]
            dst_ref[2 * t * count : (2 * t + 2) * count, lanes] = jnp.concatenate(pair, axis=0).astype(BF16)


def restored(value, scratch_ref):
    count = value.shape[0] // SIDE
    columns = []
    for g in range(value.shape[1] // LANES):
        scratch_ref[g] = value[:, g * LANES : (g + 1) * LANES]
        columns.append(jnp.concatenate([scratch_ref[g, pl.ds(b, SIDE, stride=count), :] for b in range(count)], axis=0))
    return jnp.concatenate(columns, axis=1)


def build(half, sizes, blocks_hbm, row_hbm, col_hbm, blocks, ids, sems, stores):
    count, row_devs, ka_devs = sizes
    bits, row_bits = log2(count), log2(row_devs)
    copies = [pltpu.make_async_copy(h, ids.at[k : k + 1], sems.at[k]) for k, h in enumerate((row_hbm, col_hbm))]
    width = blocks.shape[1] // PIECES
    for k in range(PIECES):
        lanes = pl.ds(k * width, width)
        copies.append(pltpu.make_async_copy(blocks_hbm.at[:, lanes], blocks.at[:, lanes], sems.at[2 + k]))
    for copy in copies:
        copy.start()
    copies[0].wait()
    copies[1].wait()
    row = ids[0:1, :]
    col = ids[1:2, :]
    row_place = (row >> bits) & (row_devs - 1)
    ka_step = ((col >> (bits + row_bits)) - (row >> (bits + row_bits))) & (ka_devs - 1)
    row_step = (((col >> bits) & (row_devs - 1)) - row_place + 1) & (row_devs - 1)
    is_mate = (row_step >> 1) == ((row_place & 1) ^ 1)
    group = jnp.where(row_step == 1, 0, jnp.where(is_mate, 1, 2))
    band = group * count + (col & (count - 1))
    pairs = 3 * count // 2
    place = ((band & 1) * pairs + (band >> 1)) * count + (row & (count - 1))
    place = jnp.where((row >= 0) & (ka_step == half), place, -1)
    slots = blocks.shape[0]
    chosen = lax.broadcasted_iota(jnp.int32, (2 * pairs * count, slots), 0) == place
    chosen = jnp.where(chosen, 1.0, 0.0).astype(BF16)
    low = lax.broadcasted_iota(jnp.int32, (pairs * count, LANES), 1) < SIDE
    for u in range(SIDE // 4):
        if u % (SIDE // 4 // PIECES) == 0:
            copies[2 + u // (SIDE // 4 // PIECES)].wait()
        found = dot(chosen, blocks[:, u * 2 * LANES : (u + 1) * 2 * LANES])
        for w in range(2):
            t = 2 * u + w
            even = found[: pairs * count, w * LANES : (w + 1) * LANES]
            odd = found[pairs * count :, w * LANES : (w + 1) * LANES]
            first = jnp.where(low, even, pltpu.roll(odd, SIDE, 1))
            second = jnp.where(low, pltpu.roll(even, SIDE, 1), odd)
            for q in range(pairs):
                pair = [v[q * count : (q + 1) * count, :] for v in (first, second)]
                tile = jnp.concatenate(pair, axis=0).astype(BF16)
                per = pairs // 3
                lanes = slice((q % per) * LANES, (q % per + 1) * LANES)
                stores[q // per][2 * t * count : (2 * t + 2) * count, lanes] = tile


def emit(cross, wire, perm_ref, wire_ref, self_ref, mate_ref, far_ref):
    perm = perm_ref[...]
    wire_ref[...] = wire
    self_ref[...] = dot_t(cross[0][...], perm)
    far_ref[...] = dot_t(cross[2][...], perm).astype(BF16)
    mate_ref[0] = dot_t(cross[1][...], perm).astype(BF16)
    mate_ref[1] = wire


def first_body(sizes, blocks_hbm, row_hbm, col_hbm, drive_hbm, relax_hbm, *refs):
    cross, (perm_ref, wire_ref, self_ref, mate_ref, far_ref, spread_ref) = refs[:3], refs[3:9]
    blocks, ids, drive, relax, scratch, sems = refs[9:]
    later = [
        pltpu.make_async_copy(drive_hbm, drive, sems.at[2 + PIECES]),
        pltpu.make_async_copy(relax_hbm, relax, sems.at[3 + PIECES]),
    ]
    for copy in later:
        copy.start()
    build(1, sizes, blocks_hbm, row_hbm, col_hbm, blocks, ids, sems, cross)
    for copy in later:
        copy.wait()
    spread_ref[...] = jnp.broadcast_to(relax[...], (LANES, relax.shape[1])).T
    field = drive[...]
    interleave(field, scratch, perm_ref)
    emit(cross, field.astype(BF16), perm_ref, wire_ref, self_ref, mate_ref, far_ref)


def second_body(sizes, blocks_hbm, row_hbm, col_hbm, perm_ref, wire_ref, *refs):
    own, outs, (blocks, ids, sems) = refs[:3], refs[3:6], refs[6:]
    build(0, sizes, blocks_hbm, row_hbm, col_hbm, blocks, ids, sems, own)
    own_partials(*own, perm_ref, wire_ref, *outs)


def own_partials(self_in, mate_in, far_in, perm_ref, wire_ref, self_ref, mate_ref, far_ref):
    perm = perm_ref[...]
    far_ref[0] = wire_ref[...]
    far_ref[1] = dot_t(far_in[...], perm).astype(BF16)
    mate_ref[...] = dot_t(mate_in[...], perm).astype(BF16)
    self_ref[...] = dot_t(self_in[...], perm)


def own_body(*refs):
    mats, (wire_ref, mate_ref, self_ref), (out_ref, scratch) = refs[:2], refs[2:5], refs[5:]
    straight = dot(mats[0][...], wire_ref[...])
    straight += dot(mats[1][...], mate_ref[1])
    out_ref[...] = self_ref[...] + restored(straight, scratch)


def with_cross(mats, down_ref, mate_ref, far_ref, other_ref, known_ref, scratch):
    straight = dot(mats[0][...], down_ref[...])
    straight += dot(mats[1][...], mate_ref[0])
    straight += dot(mats[2][...], far_ref[...])
    straight += dot(mats[3][...], other_ref[0])
    return known_ref[...] + mate_ref[1].astype(F32) + other_ref[1].astype(F32) + restored(straight, scratch)


def advanced(product, drive_ref, relax_ref):
    scale = jnp.concatenate([relax_ref[...]] * (product.shape[1] // LANES), axis=1)
    return drive_ref[...] + scale * product


def update_body(*refs):
    mats, nexts, (drive_ref, relax_ref) = refs[:4], refs[4:9], refs[9:11]
    perm_ref, wire_ref, self_ref, mate_ref, far_ref, scratch = refs[11:]
    field = advanced(with_cross(mats, *nexts, scratch), drive_ref, relax_ref)
    interleave(field, scratch, perm_ref)
    emit(mats, field.astype(BF16), perm_ref, wire_ref, self_ref, mate_ref, far_ref)


def settle_body(own_ref, received_ref, out_ref):
    out_ref[...] = own_ref[...] + received_ref[...].astype(F32)


def final_body(*refs):
    product = with_cross(refs[:4], *refs[4:9], refs[12])
    refs[11][...] = advanced(product, *refs[9:11])


def local(drive, relax, blocks, row_block, col_block):
    rows, channels = drive.shape
    slots = blocks.shape[0]
    sizes = (rows // SIDE, lax.axis_size("rows"), lax.axis_size("ka"))
    small = jax.ShapeDtypeStruct((rows, channels), BF16)
    double = jax.ShapeDtypeStruct((2, rows, channels), BF16)
    wide = jax.ShapeDtypeStruct((rows, channels), F32)
    matrices = (jax.ShapeDtypeStruct((rows, rows), BF16),) * 3
    emitted = (small, small, wide, double, small)
    staging = pltpu.VMEM((channels // LANES, rows, LANES), F32)
    fetch = [pltpu.VMEM(blocks.shape, BF16), pltpu.VMEM((2, slots), jnp.int32)]
    row2 = row_block.reshape(1, -1)
    col2 = col_block.reshape(1, -1)
    relax2 = relax.reshape(1, -1)
    work = 2 * rows * rows * channels
    spread = jax.ShapeDtypeStruct((rows, LANES), F32)
    *cross, perm, wire, partial, to_mate, to_far, relax3 = call(
        functools.partial(first_body, sizes), (*matrices, *emitted, spread), 9 * work,
        [blocks, row2, col2, drive, relax2], [HBM] * 5,
        fetch + [pltpu.VMEM(drive.shape, F32), pltpu.VMEM((1, rows), F32), staging, pltpu.SemaphoreType.DMA((4 + PIECES,))],
    )

    for sweep in range(ITERS):
        down = shifted(wire, "ka", -1)
        from_far = far(to_far)
        from_mate = mate(to_mate)
        if sweep == 0:
            *own, own_self, own_mate, own_far = call(
                functools.partial(second_body, sizes), (*matrices, wide, small, double), 9 * work,
                [blocks, row2, col2, perm, wire], [HBM] * 3 + [VMEM] * 2, fetch + [pltpu.SemaphoreType.DMA((2 + PIECES,))],
            )
        else:
            own_self, own_mate, own_far = call(own_partials, (wide, small, double), 3 * work, [*own, perm, wire])
        other_far = far(own_far)
        if sweep == 0:
            from_far, _ = lax.optimization_barrier((from_far, own_self))
        got = (partial + from_mate[0].astype(F32) + from_far.astype(F32)).astype(BF16)
        received = shifted(got, "ka", 1)
        next_mate = mate(jnp.stack([down, own_mate]))
        next_far = far(down)
        known = call(own_body, wide, 2 * work, [*own[:2], wire, from_mate, own_self], scratch=[staging])
        known = call(settle_body, wide, HEAVY * work, [known, received])
        args = [*cross, own[2], down, next_mate, next_far, other_far, known, drive, relax3]
        if sweep + 1 == ITERS:
            return call(final_body, wide, 3 * work, args, scratch=[staging])
        perm, wire, partial, to_mate, to_far = call(update_body, emitted, 6 * work, args, scratch=[staging])


def solution(mesh):
    spread = P(("ka", "rows"))
    wide = P(("ka", "rows"), None)
    return jax.shard_map(
        local, mesh=mesh, in_specs=(wide, spread, wide, spread, spread), out_specs=wide, check_vma=False
    )
```

```python
import functools

import jax
import jax.numpy as jnp
from jax import lax
from jax.experimental import pallas as pl
from jax.experimental.pallas import tpu as pltpu
from jax.sharding import PartitionSpec as P

SIDE = 64
LANES = 128
ITERS = 2
PIECES = 4
HEAVY = 90
BF16, F32 = jnp.bfloat16, jnp.float32
VMEM = pl.BlockSpec(memory_space=pltpu.VMEM)
HBM = pl.BlockSpec(memory_space=pltpu.HBM)


def log2(n):
    assert n & (n - 1) == 0
    return n.bit_length() - 1


def shifted(value, axis, steps):
    count = lax.axis_size(axis)
    return lax.ppermute(value, axis, [(source, (source + steps) % count) for source in range(count)])


def mate(value):
    return lax.ppermute(value, "rows", [(i, i ^ 1) for i in range(lax.axis_size("rows"))])


def far(value):
    count = lax.axis_size("rows")
    return lax.ppermute(value, "rows", [(i, (i + 1 if i & 1 else i - 1) % count) for i in range(count)])


def wrapped(place, count):
    return ((place + 1) % (count // 2) == 0) | (place % (count // 2) == 0)


def far_slanted(value, step):
    devices, count = lax.axis_size("ka"), lax.axis_size("rows")
    pairs = []
    for ka in range(devices):
        for i in range(count):
            other = (i + 1 if i & 1 else i - 1) % count
            target = (ka + step) % devices if wrapped(i, count) else ka
            pairs.append((ka * count + i, target * count + other))
    return lax.ppermute(value, ("ka", "rows"), pairs)


def call(kernel, outs, flops, args, specs=None, scratch=()):
    if specs:
        args = [pltpu.with_memory_space_constraint(a, pltpu.HBM) if s is HBM else a for a, s in zip(args, specs)]
    nbytes = sum(a.size * a.dtype.itemsize for a in args)
    return pl.pallas_call(
        kernel,
        out_shape=outs,
        in_specs=specs or [VMEM] * len(args),
        out_specs=jax.tree.map(lambda _: VMEM, outs),
        scratch_shapes=list(scratch),
        cost_estimate=pl.CostEstimate(flops=flops, transcendentals=0, bytes_accessed=nbytes),
        compiler_params=pltpu.CompilerParams(vmem_limit_bytes=5 << 20),
    )(*args)


def dot(a, b):
    return jnp.dot(a, b, preferred_element_type=F32)


def dot_t(a, b):
    return lax.dot_general(a, b, (((0,), (0,)), ((), ())), preferred_element_type=F32)


def interleave(value, scratch_ref, dst_ref):
    count = value.shape[0] // SIDE
    for g in range(value.shape[1] // LANES):
        lanes = slice(g * LANES, (g + 1) * LANES)
        scratch_ref[g] = value[:, lanes]
        for t in range(SIDE // 2):
            pair = [scratch_ref[g, pl.ds(2 * t + h, count, stride=SIDE), :] for h in range(2)]
            dst_ref[2 * t * count : (2 * t + 2) * count, lanes] = jnp.concatenate(pair, axis=0).astype(BF16)


def restored(value, scratch_ref):
    count = value.shape[0] // SIDE
    columns = []
    for g in range(value.shape[1] // LANES):
        scratch_ref[g] = value[:, g * LANES : (g + 1) * LANES]
        columns.append(jnp.concatenate([scratch_ref[g, pl.ds(b, SIDE, stride=count), :] for b in range(count)], axis=0))
    return jnp.concatenate(columns, axis=1)


def build(half, sizes, blocks_hbm, row_hbm, col_hbm, blocks, ids, sems, stores):
    count, row_devs, ka_devs = sizes
    bits, row_bits = log2(count), log2(row_devs)
    copies = [pltpu.make_async_copy(h, ids.at[k : k + 1], sems.at[k]) for k, h in enumerate((row_hbm, col_hbm))]
    width = blocks.shape[1] // PIECES
    for k in range(PIECES):
        lanes = pl.ds(k * width, width)
        copies.append(pltpu.make_async_copy(blocks_hbm.at[:, lanes], blocks.at[:, lanes], sems.at[2 + k]))
    for copy in copies:
        copy.start()
    copies[0].wait()
    copies[1].wait()
    row = ids[0:1, :]
    col = ids[1:2, :]
    row_place = (row >> bits) & (row_devs - 1)
    ka_step = ((col >> (bits + row_bits)) - (row >> (bits + row_bits))) & (ka_devs - 1)
    row_step = (((col >> bits) & (row_devs - 1)) - row_place + 1) & (row_devs - 1)
    is_mate = (row_step >> 1) == ((row_place & 1) ^ 1)
    group = jnp.where(row_step == 1, 0, jnp.where(is_mate, 1, 2))
    band = group * count + (col & (count - 1))
    pairs = 3 * count // 2
    place = ((band & 1) * pairs + (band >> 1)) * count + (row & (count - 1))
    place = jnp.where((row >= 0) & (ka_step == half), place, -1)
    slots = blocks.shape[0]
    chosen = lax.broadcasted_iota(jnp.int32, (2 * pairs * count, slots), 0) == place
    chosen = jnp.where(chosen, 1.0, 0.0).astype(BF16)
    low = lax.broadcasted_iota(jnp.int32, (pairs * count, LANES), 1) < SIDE
    for u in range(SIDE // 4):
        if u % (SIDE // 4 // PIECES) == 0:
            copies[2 + u // (SIDE // 4 // PIECES)].wait()
        found = dot(chosen, blocks[:, u * 2 * LANES : (u + 1) * 2 * LANES])
        for w in range(2):
            t = 2 * u + w
            even = found[: pairs * count, w * LANES : (w + 1) * LANES]
            odd = found[pairs * count :, w * LANES : (w + 1) * LANES]
            first = jnp.where(low, even, pltpu.roll(odd, SIDE, 1))
            second = jnp.where(low, pltpu.roll(even, SIDE, 1), odd)
            for q in range(pairs):
                pair = [v[q * count : (q + 1) * count, :] for v in (first, second)]
                tile = jnp.concatenate(pair, axis=0).astype(BF16)
                per = pairs // 3
                lanes = slice((q % per) * LANES, (q % per + 1) * LANES)
                stores[q // per][2 * t * count : (2 * t + 2) * count, lanes] = tile


def emit(cross, wire, perm_ref, wire_ref, self_ref, mate_ref, far_ref):
    perm = perm_ref[...]
    wire_ref[...] = wire
    self_ref[...] = dot_t(cross[0][...], perm)
    far_ref[...] = dot_t(cross[2][...], perm).astype(BF16)
    mate_ref[0] = dot_t(cross[1][...], perm).astype(BF16)
    mate_ref[1] = wire


def first_body(sizes, blocks_hbm, row_hbm, col_hbm, drive_hbm, relax_hbm, *refs):
    cross, (perm_ref, wire_ref, self_ref, mate_ref, far_ref, spread_ref, flag_ref) = refs[:3], refs[3:10]
    blocks, ids, drive, relax, scratch, sems = refs[10:]
    later = [
        pltpu.make_async_copy(drive_hbm, drive, sems.at[2 + PIECES]),
        pltpu.make_async_copy(relax_hbm, relax, sems.at[3 + PIECES]),
    ]
    for copy in later:
        copy.start()
    build(1, sizes, blocks_hbm, row_hbm, col_hbm, blocks, ids, sems, cross)
    for copy in later:
        copy.wait()
    place = (jnp.max(ids[0:1, :], axis=1, keepdims=True) >> log2(sizes[0])) & (sizes[1] - 1)
    half = sizes[1] // 2 - 1
    slanted = (((place + 1) & half) == 0) | ((place & half) == 0)
    flag_ref[...] = jnp.broadcast_to(jnp.where(slanted, 1.0, 0.0), flag_ref.shape)
    spread_ref[...] = jnp.broadcast_to(relax[...], (LANES, relax.shape[1])).T
    field = drive[...]
    interleave(field, scratch, perm_ref)
    emit(cross, field.astype(BF16), perm_ref, wire_ref, self_ref, mate_ref, far_ref)


def second_body(sizes, blocks_hbm, row_hbm, col_hbm, perm_ref, wire_ref, *refs):
    own, outs, (blocks, ids, sems) = refs[:3], refs[3:6], refs[6:]
    build(0, sizes, blocks_hbm, row_hbm, col_hbm, blocks, ids, sems, own)
    own_partials(*own, perm_ref, wire_ref, *outs)


def own_partials(self_in, mate_in, far_in, perm_ref, wire_ref, self_ref, mate_ref, far_ref):
    perm = perm_ref[...]
    far_ref[0] = wire_ref[...]
    far_ref[1] = dot_t(far_in[...], perm).astype(BF16)
    mate_ref[...] = dot_t(mate_in[...], perm).astype(BF16)
    self_ref[...] = dot_t(self_in[...], perm)


def own_body(*refs):
    mats, (wire_ref, mate_ref, self_ref, partial_ref, flag_ref), (out_ref, scratch) = refs[:2], refs[2:7], refs[7:]
    straight = dot(mats[0][...], wire_ref[...])
    straight += dot(mats[1][...], mate_ref[1])
    here = jnp.where(flag_ref[...] > 0, partial_ref[...].astype(F32), 0.0)
    out_ref[...] = self_ref[...] + here + restored(straight, scratch)


def with_cross(mats, down_ref, mate_ref, far_ref, other_ref, known_ref, scratch):
    straight = dot(mats[0][...], down_ref[...])
    straight += dot(mats[1][...], mate_ref[0])
    straight += dot(mats[2][...], far_ref[...])
    straight += dot(mats[3][...], other_ref[0])
    return known_ref[...] + mate_ref[1].astype(F32) + other_ref[1].astype(F32) + restored(straight, scratch)


def advanced(product, drive_ref, relax_ref):
    scale = jnp.concatenate([relax_ref[...]] * (product.shape[1] // LANES), axis=1)
    return drive_ref[...] + scale * product


def update_body(*refs):
    mats, nexts, (drive_ref, relax_ref) = refs[:4], refs[4:9], refs[9:11]
    perm_ref, wire_ref, self_ref, mate_ref, far_ref, scratch = refs[11:]
    field = advanced(with_cross(mats, *nexts, scratch), drive_ref, relax_ref)
    interleave(field, scratch, perm_ref)
    emit(mats, field.astype(BF16), perm_ref, wire_ref, self_ref, mate_ref, far_ref)


def settle_body(own_ref, received_ref, out_ref):
    out_ref[...] = own_ref[...] + received_ref[...].astype(F32)


def final_body(*refs):
    product = with_cross(refs[:4], *refs[4:9], refs[12])
    refs[11][...] = advanced(product, *refs[9:11])


def local(drive, relax, blocks, row_block, col_block):
    rows, channels = drive.shape
    slots = blocks.shape[0]
    sizes = (rows // SIDE, lax.axis_size("rows"), lax.axis_size("ka"))
    small = jax.ShapeDtypeStruct((rows, channels), BF16)
    double = jax.ShapeDtypeStruct((2, rows, channels), BF16)
    wide = jax.ShapeDtypeStruct((rows, channels), F32)
    matrices = (jax.ShapeDtypeStruct((rows, rows), BF16),) * 3
    emitted = (small, small, wide, double, small)
    staging = pltpu.VMEM((channels // LANES, rows, LANES), F32)
    fetch = [pltpu.VMEM(blocks.shape, BF16), pltpu.VMEM((2, slots), jnp.int32)]
    row2 = row_block.reshape(1, -1)
    col2 = col_block.reshape(1, -1)
    relax2 = relax.reshape(1, -1)
    work = 2 * rows * rows * channels
    spread = jax.ShapeDtypeStruct((rows, LANES), F32)
    *cross, perm, wire, partial, to_mate, to_far, relax3, flag = call(
        functools.partial(first_body, sizes), (*matrices, *emitted, spread, jax.ShapeDtypeStruct((1, channels), F32)), 9 * work,
        [blocks, row2, col2, drive, relax2], [HBM] * 5,
        fetch + [pltpu.VMEM(drive.shape, F32), pltpu.VMEM((1, rows), F32), staging, pltpu.SemaphoreType.DMA((4 + PIECES,))],
    )

    slanted = flag > 0
    for sweep in range(ITERS):
        down = shifted(wire, "ka", -1)
        from_far = far_slanted(to_far, 1)
        from_mate = mate(to_mate)
        if sweep == 0:
            *own, own_self, own_mate, own_far = call(
                functools.partial(second_body, sizes), (*matrices, wide, small, double), 9 * work,
                [blocks, row2, col2, perm, wire], [HBM] * 3 + [VMEM] * 2, fetch + [pltpu.SemaphoreType.DMA((2 + PIECES,))],
            )
        else:
            own_self, own_mate, own_far = call(own_partials, (wide, small, double), 3 * work, [*own, perm, wire])
        other_far = far(own_far)
        if sweep == 0:
            from_far, _ = lax.optimization_barrier((from_far, own_self))
        got = partial + from_mate[0].astype(F32) + jnp.where(slanted, 0.0, from_far.astype(F32))
        got = got.astype(BF16)
        received = shifted(got, "ka", 1)
        next_mate = mate(jnp.stack([down, own_mate]))
        next_far = far_slanted(jnp.where(slanted, wire, down), -1)
        known = call(
            own_body, wide, 2 * work, [*own[:2], wire, from_mate, own_self, from_far, flag], scratch=[staging]
        )
        known = call(settle_body, wide, HEAVY * work, [known, received])
        args = [*cross, own[2], down, next_mate, next_far, other_far, known, drive, relax3]
        if sweep + 1 == ITERS:
            return call(final_body, wide, 3 * work, args, scratch=[staging])
        perm, wire, partial, to_mate, to_far = call(update_body, emitted, 6 * work, args, scratch=[staging])


def solution(mesh):
    spread = P(("ka", "rows"))
    wide = P(("ka", "rows"), None)
    return jax.shard_map(
        local, mesh=mesh, in_specs=(wide, spread, wide, spread, spread), out_specs=wide, check_vma=False
    )
```

```python
import functools

import jax
import jax.numpy as jnp
from jax import lax
from jax.experimental import pallas as pl
from jax.experimental.pallas import tpu as pltpu
from jax.sharding import PartitionSpec as P

SIDE = 64
LANES = 128
ITERS = 2
PIECES = 4
HEAVY = 90
BF16, F32 = jnp.bfloat16, jnp.float32
VMEM = pl.BlockSpec(memory_space=pltpu.VMEM)
HBM = pl.BlockSpec(memory_space=pltpu.HBM)


def log2(n):
    assert n & (n - 1) == 0
    return n.bit_length() - 1


def shifted(value, axis, steps):
    count = lax.axis_size(axis)
    return lax.ppermute(value, axis, [(source, (source + steps) % count) for source in range(count)])


def mate(value):
    return lax.ppermute(value, "rows", [(i, i ^ 1) for i in range(lax.axis_size("rows"))])


def far(value):
    count = lax.axis_size("rows")
    return lax.ppermute(value, "rows", [(i, (i + 1 if i & 1 else i - 1) % count) for i in range(count)])


def wrapped(place, count):
    return ((place + 1) % (count // 2) == 0) | (place % (count // 2) == 0)


def far_slanted(value, step):
    devices, count = lax.axis_size("ka"), lax.axis_size("rows")
    pairs = []
    for ka in range(devices):
        for i in range(count):
            other = (i + 1 if i & 1 else i - 1) % count
            target = (ka + step) % devices if wrapped(i, count) else ka
            pairs.append((ka * count + i, target * count + other))
    return lax.ppermute(value, ("ka", "rows"), pairs)


def call(kernel, outs, flops, args, specs=None, scratch=()):
    if specs:
        args = [pltpu.with_memory_space_constraint(a, pltpu.HBM) if s is HBM else a for a, s in zip(args, specs)]
    nbytes = sum(a.size * a.dtype.itemsize for a in args)
    return pl.pallas_call(
        kernel,
        out_shape=outs,
        in_specs=specs or [VMEM] * len(args),
        out_specs=jax.tree.map(lambda _: VMEM, outs),
        scratch_shapes=list(scratch),
        cost_estimate=pl.CostEstimate(flops=flops, transcendentals=0, bytes_accessed=nbytes),
        compiler_params=pltpu.CompilerParams(vmem_limit_bytes=5 << 20),
    )(*args)


def dot(a, b):
    return jnp.dot(a, b, preferred_element_type=F32)


def dot_t(a, b):
    return lax.dot_general(a, b, (((0,), (0,)), ((), ())), preferred_element_type=F32)


def interleave(value, scratch_ref, dst_ref):
    count = value.shape[0] // SIDE
    for g in range(value.shape[1] // LANES):
        lanes = slice(g * LANES, (g + 1) * LANES)
        scratch_ref[g] = value[:, lanes]
        for t in range(SIDE // 2):
            pair = [scratch_ref[g, pl.ds(2 * t + h, count, stride=SIDE), :] for h in range(2)]
            dst_ref[2 * t * count : (2 * t + 2) * count, lanes] = jnp.concatenate(pair, axis=0).astype(BF16)


def restored(value, scratch_ref):
    count = value.shape[0] // SIDE
    columns = []
    for g in range(value.shape[1] // LANES):
        scratch_ref[g] = value[:, g * LANES : (g + 1) * LANES]
        columns.append(jnp.concatenate([scratch_ref[g, pl.ds(b, SIDE, stride=count), :] for b in range(count)], axis=0))
    return jnp.concatenate(columns, axis=1)


def build(half, sizes, blocks_hbm, row_hbm, col_hbm, blocks, ids, sems, stores):
    count, row_devs, ka_devs = sizes
    bits, row_bits = log2(count), log2(row_devs)
    copies = [pltpu.make_async_copy(h, ids.at[k : k + 1], sems.at[k]) for k, h in enumerate((row_hbm, col_hbm))]
    width = blocks.shape[1] // PIECES
    for k in range(PIECES):
        lanes = pl.ds(k * width, width)
        copies.append(pltpu.make_async_copy(blocks_hbm.at[:, lanes], blocks.at[:, lanes], sems.at[2 + k]))
    for copy in copies:
        copy.start()
    copies[0].wait()
    copies[1].wait()
    row = ids[0:1, :]
    col = ids[1:2, :]
    row_place = (row >> bits) & (row_devs - 1)
    ka_step = ((col >> (bits + row_bits)) - (row >> (bits + row_bits))) & (ka_devs - 1)
    row_step = (((col >> bits) & (row_devs - 1)) - row_place + 1) & (row_devs - 1)
    is_mate = (row_step >> 1) == ((row_place & 1) ^ 1)
    group = jnp.where(row_step == 1, 0, jnp.where(is_mate, 1, 2))
    band = group * count + (col & (count - 1))
    pairs = 3 * count // 2
    place = ((band & 1) * pairs + (band >> 1)) * count + (row & (count - 1))
    place = jnp.where((row >= 0) & (ka_step == half), place, -1)
    slots = blocks.shape[0]
    chosen = lax.broadcasted_iota(jnp.int32, (2 * pairs * count, slots), 0) == place
    chosen = jnp.where(chosen, 1.0, 0.0).astype(BF16)
    low = lax.broadcasted_iota(jnp.int32, (pairs * count, LANES), 1) < SIDE
    for u in range(SIDE // 4):
        if u % (SIDE // 4 // PIECES) == 0:
            copies[2 + u // (SIDE // 4 // PIECES)].wait()
        found = dot(chosen, blocks[:, u * 2 * LANES : (u + 1) * 2 * LANES])
        for w in range(2):
            t = 2 * u + w
            even = found[: pairs * count, w * LANES : (w + 1) * LANES]
            odd = found[pairs * count :, w * LANES : (w + 1) * LANES]
            first = jnp.where(low, even, pltpu.roll(odd, SIDE, 1))
            second = jnp.where(low, pltpu.roll(even, SIDE, 1), odd)
            for q in range(pairs):
                pair = [v[q * count : (q + 1) * count, :] for v in (first, second)]
                tile = jnp.concatenate(pair, axis=0).astype(BF16)
                per = pairs // 3
                lanes = slice((q % per) * LANES, (q % per + 1) * LANES)
                stores[q // per][2 * t * count : (2 * t + 2) * count, lanes] = tile


def emit(cross, wire, perm_ref, wire_ref, self_ref, mate_ref, far_ref):
    perm = perm_ref[...]
    wire_ref[...] = wire
    self_ref[...] = dot_t(cross[0][...], perm)
    far_ref[...] = dot_t(cross[2][...], perm).astype(BF16)
    mate_ref[0] = dot_t(cross[1][...], perm).astype(BF16)
    mate_ref[1] = wire


def first_body(sizes, blocks_hbm, row_hbm, col_hbm, drive_hbm, relax_hbm, *refs):
    cross, (perm_ref, wire_ref, self_ref, mate_ref, far_ref, spread_ref, flag_ref) = refs[:3], refs[3:10]
    blocks, ids, drive, relax, scratch, sems = refs[10:]
    later = [
        pltpu.make_async_copy(drive_hbm, drive, sems.at[2 + PIECES]),
        pltpu.make_async_copy(relax_hbm, relax, sems.at[3 + PIECES]),
    ]
    for copy in later:
        copy.start()
    build(1, sizes, blocks_hbm, row_hbm, col_hbm, blocks, ids, sems, cross)
    for copy in later:
        copy.wait()
    place = (jnp.max(ids[0:1, :], axis=1, keepdims=True) >> log2(sizes[0])) & (sizes[1] - 1)
    half = sizes[1] // 2 - 1
    slanted = (((place + 1) & half) == 0) | ((place & half) == 0)
    flag_ref[...] = jnp.broadcast_to(jnp.where(slanted, 1.0, 0.0), flag_ref.shape)
    spread_ref[...] = jnp.broadcast_to(relax[...], (LANES, relax.shape[1])).T
    field = drive[...]
    interleave(field, scratch, perm_ref)
    emit(cross, field.astype(BF16), perm_ref, wire_ref, self_ref, mate_ref, far_ref)


def second_body(sizes, blocks_hbm, row_hbm, col_hbm, perm_ref, wire_ref, *refs):
    own, outs, (blocks, ids, sems) = refs[:3], refs[3:6], refs[6:]
    build(0, sizes, blocks_hbm, row_hbm, col_hbm, blocks, ids, sems, own)
    own_partials(*own, perm_ref, wire_ref, *outs)


def own_partials(self_in, mate_in, far_in, perm_ref, wire_ref, self_ref, mate_ref, far_ref):
    perm = perm_ref[...]
    far_ref[0] = wire_ref[...]
    far_ref[1] = dot_t(far_in[...], perm).astype(BF16)
    mate_ref[...] = dot_t(mate_in[...], perm).astype(BF16)
    self_ref[...] = dot_t(self_in[...], perm)


def own_body(*refs):
    mats, (wire_ref, mate_ref, self_ref, partial_ref, flag_ref), (out_ref, scratch) = refs[:2], refs[2:7], refs[7:]
    straight = dot(mats[0][...], wire_ref[...])
    straight += dot(mats[1][...], mate_ref[1])
    here = jnp.where(flag_ref[...] > 0, partial_ref[...].astype(F32), 0.0)
    out_ref[...] = self_ref[...] + here + restored(straight, scratch)


def with_cross(mats, down_ref, mate_ref, far_ref, other_ref, known_ref, scratch):
    straight = dot(mats[0][...], down_ref[...])
    straight += dot(mats[1][...], mate_ref[0])
    straight += dot(mats[2][...], far_ref[...])
    straight += dot(mats[3][...], other_ref[0])
    return known_ref[...] + mate_ref[1].astype(F32) + other_ref[1].astype(F32) + restored(straight, scratch)


def advanced(product, drive_ref, relax_ref):
    scale = jnp.concatenate([relax_ref[...]] * (product.shape[1] // LANES), axis=1)
    return drive_ref[...] + scale * product


def update_body(*refs):
    mats, nexts, (drive_ref, relax_ref) = refs[:4], refs[4:9], refs[9:11]
    perm_ref, wire_ref, self_ref, mate_ref, far_ref, scratch = refs[11:]
    field = advanced(with_cross(mats, *nexts, scratch), drive_ref, relax_ref)
    interleave(field, scratch, perm_ref)
    emit(mats, field.astype(BF16), perm_ref, wire_ref, self_ref, mate_ref, far_ref)


def settle_body(own_ref, received_ref, out_ref):
    out_ref[...] = own_ref[...] + received_ref[...].astype(F32)


def final_body(*refs):
    product = with_cross(refs[:4], *refs[4:9], refs[12])
    refs[11][...] = advanced(product, *refs[9:11])


def local(drive, relax, blocks, row_block, col_block):
    rows, channels = drive.shape
    slots = blocks.shape[0]
    sizes = (rows // SIDE, lax.axis_size("rows"), lax.axis_size("ka"))
    small = jax.ShapeDtypeStruct((rows, channels), BF16)
    double = jax.ShapeDtypeStruct((2, rows, channels), BF16)
    wide = jax.ShapeDtypeStruct((rows, channels), F32)
    matrices = (jax.ShapeDtypeStruct((rows, rows), BF16),) * 3
    emitted = (small, small, wide, double, small)
    staging = pltpu.VMEM((channels // LANES, rows, LANES), F32)
    fetch = [pltpu.VMEM(blocks.shape, BF16), pltpu.VMEM((2, slots), jnp.int32)]
    row2 = row_block.reshape(1, -1)
    col2 = col_block.reshape(1, -1)
    relax2 = relax.reshape(1, -1)
    work = 2 * rows * rows * channels
    spread = jax.ShapeDtypeStruct((rows, LANES), F32)
    *cross, perm, wire, partial, to_mate, to_far, relax3, flag = call(
        functools.partial(first_body, sizes), (*matrices, *emitted, spread, jax.ShapeDtypeStruct((1, channels), F32)), 9 * work,
        [blocks, row2, col2, drive, relax2], [HBM] * 5,
        fetch + [pltpu.VMEM(drive.shape, F32), pltpu.VMEM((1, rows), F32), staging, pltpu.SemaphoreType.DMA((4 + PIECES,))],
    )

    slanted = flag > 0
    for sweep in range(ITERS):
        down = shifted(wire, "ka", -1)
        from_far = far_slanted(to_far, 1)
        from_mate = mate(to_mate)
        if sweep == 0:
            *own, own_self, own_mate, own_far = call(
                functools.partial(second_body, sizes), (*matrices, wide, small, double), 9 * work,
                [blocks, row2, col2, perm, wire], [HBM] * 3 + [VMEM] * 2, fetch + [pltpu.SemaphoreType.DMA((2 + PIECES,))],
            )
        else:
            own_self, own_mate, own_far = call(own_partials, (wide, small, double), 3 * work, [*own, perm, wire])
        if sweep == 0:
            from_far, _ = lax.optimization_barrier((from_far, own_self))
        got = partial + from_mate[0].astype(F32) + jnp.where(slanted, 0.0, from_far.astype(F32))
        got = got.astype(BF16)
        received = shifted(got, "ka", 1)
        own_far, _ = lax.optimization_barrier((own_far, got))
        other_far = far(own_far)
        next_mate = mate(jnp.stack([down, own_mate]))
        next_far = far_slanted(jnp.where(slanted, wire, down), -1)
        known = call(
            own_body, wide, 2 * work, [*own[:2], wire, from_mate, own_self, from_far, flag], scratch=[staging]
        )
        known = call(settle_body, wide, HEAVY * work, [known, received])
        args = [*cross, own[2], down, next_mate, next_far, other_far, known, drive, relax3]
        if sweep + 1 == ITERS:
            return call(final_body, wide, 3 * work, args, scratch=[staging])
        perm, wire, partial, to_mate, to_far = call(update_body, emitted, 6 * work, args, scratch=[staging])


def solution(mesh):
    spread = P(("ka", "rows"))
    wide = P(("ka", "rows"), None)
    return jax.shard_map(
        local, mesh=mesh, in_specs=(wide, spread, wide, spread, spread), out_specs=wide, check_vma=False
    )
```

```python
import functools

import jax
import jax.numpy as jnp
from jax import lax
from jax.experimental import pallas as pl
from jax.experimental.pallas import tpu as pltpu
from jax.sharding import PartitionSpec as P

SIDE = 64
LANES = 128
ITERS = 2
PIECES = 4
HEAVY = 90
BF16, F32 = jnp.bfloat16, jnp.float32
VMEM = pl.BlockSpec(memory_space=pltpu.VMEM)
HBM = pl.BlockSpec(memory_space=pltpu.HBM)


def log2(n):
    assert n & (n - 1) == 0
    return n.bit_length() - 1


def shifted(value, axis, steps):
    count = lax.axis_size(axis)
    return lax.ppermute(value, axis, [(source, (source + steps) % count) for source in range(count)])


def mate(value):
    return lax.ppermute(value, "rows", [(i, i ^ 1) for i in range(lax.axis_size("rows"))])


def far(value):
    count = lax.axis_size("rows")
    return lax.ppermute(value, "rows", [(i, (i + 1 if i & 1 else i - 1) % count) for i in range(count)])


def wrapped(place, count):
    return ((place + 1) % (count // 2) == 0) | (place % (count // 2) == 0)


def far_slanted(value, step):
    devices, count = lax.axis_size("ka"), lax.axis_size("rows")
    pairs = []
    for ka in range(devices):
        for i in range(count):
            other = (i + 1 if i & 1 else i - 1) % count
            target = (ka + step) % devices if wrapped(i, count) else ka
            pairs.append((ka * count + i, target * count + other))
    return lax.ppermute(value, ("ka", "rows"), pairs)


def call(kernel, outs, flops, args, specs=None, scratch=()):
    if specs:
        args = [pltpu.with_memory_space_constraint(a, pltpu.HBM) if s is HBM else a for a, s in zip(args, specs)]
    nbytes = sum(a.size * a.dtype.itemsize for a in args)
    return pl.pallas_call(
        kernel,
        out_shape=outs,
        in_specs=specs or [VMEM] * len(args),
        out_specs=jax.tree.map(lambda _: VMEM, outs),
        scratch_shapes=list(scratch),
        cost_estimate=pl.CostEstimate(flops=flops, transcendentals=0, bytes_accessed=nbytes),
        compiler_params=pltpu.CompilerParams(vmem_limit_bytes=5 << 20),
    )(*args)


def dot(a, b):
    return jnp.dot(a, b, preferred_element_type=F32)


def dot_t(a, b):
    return lax.dot_general(a, b, (((0,), (0,)), ((), ())), preferred_element_type=F32)


def interleave(value, scratch_ref, dst_ref):
    count = value.shape[0] // SIDE
    for g in range(value.shape[1] // LANES):
        lanes = slice(g * LANES, (g + 1) * LANES)
        scratch_ref[g] = value[:, lanes]
        for t in range(SIDE // 2):
            pair = [scratch_ref[g, pl.ds(2 * t + h, count, stride=SIDE), :] for h in range(2)]
            dst_ref[2 * t * count : (2 * t + 2) * count, lanes] = jnp.concatenate(pair, axis=0).astype(BF16)


def restored(value, scratch_ref):
    count = value.shape[0] // SIDE
    columns = []
    for g in range(value.shape[1] // LANES):
        scratch_ref[g] = value[:, g * LANES : (g + 1) * LANES]
        columns.append(jnp.concatenate([scratch_ref[g, pl.ds(b, SIDE, stride=count), :] for b in range(count)], axis=0))
    return jnp.concatenate(columns, axis=1)


def build(half, sizes, blocks_hbm, row_hbm, col_hbm, blocks, ids, sems, stores):
    count, row_devs, ka_devs = sizes
    bits, row_bits = log2(count), log2(row_devs)
    copies = [pltpu.make_async_copy(h, ids.at[k : k + 1], sems.at[k]) for k, h in enumerate((row_hbm, col_hbm))]
    width = blocks.shape[1] // PIECES
    for k in range(PIECES):
        lanes = pl.ds(k * width, width)
        copies.append(pltpu.make_async_copy(blocks_hbm.at[:, lanes], blocks.at[:, lanes], sems.at[2 + k]))
    for copy in copies:
        copy.start()
    copies[0].wait()
    copies[1].wait()
    row = ids[0:1, :]
    col = ids[1:2, :]
    row_place = (row >> bits) & (row_devs - 1)
    ka_step = ((col >> (bits + row_bits)) - (row >> (bits + row_bits))) & (ka_devs - 1)
    row_step = (((col >> bits) & (row_devs - 1)) - row_place + 1) & (row_devs - 1)
    is_mate = (row_step >> 1) == ((row_place & 1) ^ 1)
    group = jnp.where(row_step == 1, 0, jnp.where(is_mate, 1, 2))
    band = group * count + (col & (count - 1))
    pairs = 3 * count // 2
    place = ((band & 1) * pairs + (band >> 1)) * count + (row & (count - 1))
    place = jnp.where((row >= 0) & (ka_step == half), place, -1)
    slots = blocks.shape[0]
    chosen = lax.broadcasted_iota(jnp.int32, (2 * pairs * count, slots), 0) == place
    chosen = jnp.where(chosen, 1.0, 0.0).astype(BF16)
    low = lax.broadcasted_iota(jnp.int32, (pairs * count, LANES), 1) < SIDE
    for u in range(SIDE // 4):
        if u % (SIDE // 4 // PIECES) == 0:
            copies[2 + u // (SIDE // 4 // PIECES)].wait()
        found = dot(chosen, blocks[:, u * 2 * LANES : (u + 1) * 2 * LANES])
        for w in range(2):
            t = 2 * u + w
            even = found[: pairs * count, w * LANES : (w + 1) * LANES]
            odd = found[pairs * count :, w * LANES : (w + 1) * LANES]
            first = jnp.where(low, even, pltpu.roll(odd, SIDE, 1))
            second = jnp.where(low, pltpu.roll(even, SIDE, 1), odd)
            for q in range(pairs):
                pair = [v[q * count : (q + 1) * count, :] for v in (first, second)]
                tile = jnp.concatenate(pair, axis=0).astype(BF16)
                per = pairs // 3
                lanes = slice((q % per) * LANES, (q % per + 1) * LANES)
                stores[q // per][2 * t * count : (2 * t + 2) * count, lanes] = tile


def emit(cross, wire, perm_ref, wire_ref, self_ref, mate_ref, far_ref):
    perm = perm_ref[...]
    wire_ref[...] = wire
    self_ref[...] = dot_t(cross[0][...], perm)
    far_ref[...] = dot_t(cross[2][...], perm).astype(BF16)
    mate_ref[0] = dot_t(cross[1][...], perm).astype(BF16)
    mate_ref[1] = wire


def first_body(sizes, blocks_hbm, row_hbm, col_hbm, drive_hbm, relax_hbm, *refs):
    cross, (perm_ref, wire_ref, self_ref, mate_ref, far_ref, spread_ref, flag_ref) = refs[:3], refs[3:10]
    blocks, ids, drive, relax, scratch, sems = refs[10:]
    later = [
        pltpu.make_async_copy(drive_hbm, drive, sems.at[2 + PIECES]),
        pltpu.make_async_copy(relax_hbm, relax, sems.at[3 + PIECES]),
    ]
    for copy in later:
        copy.start()
    build(1, sizes, blocks_hbm, row_hbm, col_hbm, blocks, ids, sems, cross)
    for copy in later:
        copy.wait()
    place = (jnp.max(ids[0:1, :], axis=1, keepdims=True) >> log2(sizes[0])) & (sizes[1] - 1)
    half = sizes[1] // 2 - 1
    slanted = (((place + 1) & half) == 0) | ((place & half) == 0)
    flag_ref[...] = jnp.broadcast_to(jnp.where(slanted, 1.0, 0.0), flag_ref.shape)
    spread_ref[...] = jnp.broadcast_to(relax[...], (LANES, relax.shape[1])).T
    field = drive[...]
    interleave(field, scratch, perm_ref)
    emit(cross, field.astype(BF16), perm_ref, wire_ref, self_ref, mate_ref, far_ref)


def second_body(sizes, blocks_hbm, row_hbm, col_hbm, perm_ref, wire_ref, *refs):
    own, outs, (blocks, ids, sems) = refs[:3], refs[3:6], refs[6:]
    build(0, sizes, blocks_hbm, row_hbm, col_hbm, blocks, ids, sems, own)
    own_partials(*own, perm_ref, wire_ref, *outs)


def own_partials(self_in, mate_in, far_in, perm_ref, wire_ref, self_ref, mate_ref, far_ref):
    perm = perm_ref[...]
    far_ref[0] = wire_ref[...]
    far_ref[1] = dot_t(far_in[...], perm).astype(BF16)
    mate_ref[...] = dot_t(mate_in[...], perm).astype(BF16)
    self_ref[...] = dot_t(self_in[...], perm)


def own_body(*refs):
    mats, (wire_ref, mate_ref, self_ref, partial_ref, flag_ref), (out_ref, scratch) = refs[:2], refs[2:7], refs[7:]
    straight = dot(mats[0][...], wire_ref[...])
    straight += dot(mats[1][...], mate_ref[1])
    here = jnp.where(flag_ref[...] > 0, partial_ref[...].astype(F32), 0.0)
    out_ref[...] = self_ref[...] + here + restored(straight, scratch)


def with_cross(mats, down_ref, mate_ref, far_ref, known_ref, scratch):
    straight = dot(mats[0][...], down_ref[...])
    straight += dot(mats[1][...], mate_ref[0])
    straight += dot(mats[2][...], far_ref[...])
    return known_ref[...] + mate_ref[1].astype(F32) + restored(straight, scratch)


def advanced(product, drive_ref, relax_ref):
    scale = jnp.concatenate([relax_ref[...]] * (product.shape[1] // LANES), axis=1)
    return drive_ref[...] + scale * product


def update_body(*refs):
    mats, nexts, (drive_ref, relax_ref) = refs[:3], refs[3:7], refs[7:9]
    perm_ref, wire_ref, self_ref, mate_ref, far_ref, scratch = refs[9:]
    field = advanced(with_cross(mats, *nexts, scratch), drive_ref, relax_ref)
    interleave(field, scratch, perm_ref)
    emit(mats, field.astype(BF16), perm_ref, wire_ref, self_ref, mate_ref, far_ref)


def settle_body(far_in, other_ref, known_ref, received_ref, out_ref, scratch):
    known = known_ref[...] + other_ref[1].astype(F32) + received_ref[...].astype(F32)
    out_ref[...] = known + restored(dot(far_in[...], other_ref[0]), scratch)


def final_body(*refs):
    product = with_cross(refs[:3], *refs[3:7], refs[10])
    refs[9][...] = advanced(product, *refs[7:9])


def local(drive, relax, blocks, row_block, col_block):
    rows, channels = drive.shape
    slots = blocks.shape[0]
    sizes = (rows // SIDE, lax.axis_size("rows"), lax.axis_size("ka"))
    small = jax.ShapeDtypeStruct((rows, channels), BF16)
    double = jax.ShapeDtypeStruct((2, rows, channels), BF16)
    wide = jax.ShapeDtypeStruct((rows, channels), F32)
    matrices = (jax.ShapeDtypeStruct((rows, rows), BF16),) * 3
    emitted = (small, small, wide, double, small)
    staging = pltpu.VMEM((channels // LANES, rows, LANES), F32)
    fetch = [pltpu.VMEM(blocks.shape, BF16), pltpu.VMEM((2, slots), jnp.int32)]
    row2 = row_block.reshape(1, -1)
    col2 = col_block.reshape(1, -1)
    relax2 = relax.reshape(1, -1)
    work = 2 * rows * rows * channels
    spread = jax.ShapeDtypeStruct((rows, LANES), F32)
    *cross, perm, wire, partial, to_mate, to_far, relax3, flag = call(
        functools.partial(first_body, sizes), (*matrices, *emitted, spread, jax.ShapeDtypeStruct((1, channels), F32)), 9 * work,
        [blocks, row2, col2, drive, relax2], [HBM] * 5,
        fetch + [pltpu.VMEM(drive.shape, F32), pltpu.VMEM((1, rows), F32), staging, pltpu.SemaphoreType.DMA((4 + PIECES,))],
    )

    slanted = flag > 0
    for sweep in range(ITERS):
        down = shifted(wire, "ka", -1)
        from_far = far_slanted(to_far, 1)
        from_mate = mate(to_mate)
        if sweep == 0:
            *own, own_self, own_mate, own_far = call(
                functools.partial(second_body, sizes), (*matrices, wide, small, double), 9 * work,
                [blocks, row2, col2, perm, wire], [HBM] * 3 + [VMEM] * 2, fetch + [pltpu.SemaphoreType.DMA((2 + PIECES,))],
            )
        else:
            own_self, own_mate, own_far = call(own_partials, (wide, small, double), 3 * work, [*own, perm, wire])
        if sweep == 0:
            from_far, _ = lax.optimization_barrier((from_far, own_self))
        got = partial + from_mate[0].astype(F32) + jnp.where(slanted, 0.0, from_far.astype(F32))
        got = got.astype(BF16)
        received = shifted(got, "ka", 1)
        own_far, _ = lax.optimization_barrier((own_far, got))
        other_far = far(own_far)
        next_mate = mate(jnp.stack([down, own_mate]))
        next_far = far_slanted(jnp.where(slanted, wire, down), -1)
        known = call(
            own_body, wide, 2 * work, [*own[:2], wire, from_mate, own_self, from_far, flag], scratch=[staging]
        )
        known = call(settle_body, wide, HEAVY * work, [own[2], other_far, known, received], scratch=[staging])
        args = [*cross, down, next_mate, next_far, known, drive, relax3]
        if sweep + 1 == ITERS:
            return call(final_body, wide, 3 * work, args, scratch=[staging])
        perm, wire, partial, to_mate, to_far = call(update_body, emitted, 6 * work, args, scratch=[staging])


def solution(mesh):
    spread = P(("ka", "rows"))
    wide = P(("ka", "rows"), None)
    return jax.shard_map(
        local, mesh=mesh, in_specs=(wide, spread, wide, spread, spread), out_specs=wide, check_vma=False
    )
```

```python
import functools

import jax
import jax.numpy as jnp
from jax import lax
from jax.experimental import pallas as pl
from jax.experimental.pallas import tpu as pltpu
from jax.sharding import PartitionSpec as P

SIDE = 64
LANES = 128
ITERS = 2
PIECES = 4
HEAVY = 90
BF16, F32 = jnp.bfloat16, jnp.float32
VMEM = pl.BlockSpec(memory_space=pltpu.VMEM)
HBM = pl.BlockSpec(memory_space=pltpu.HBM)


def log2(n):
    assert n & (n - 1) == 0
    return n.bit_length() - 1


def shifted(value, axis, steps):
    count = lax.axis_size(axis)
    return lax.ppermute(value, axis, [(source, (source + steps) % count) for source in range(count)])


def mate(value):
    return lax.ppermute(value, "rows", [(i, i ^ 1) for i in range(lax.axis_size("rows"))])


def far(value):
    count = lax.axis_size("rows")
    return lax.ppermute(value, "rows", [(i, (i + 1 if i & 1 else i - 1) % count) for i in range(count)])


def call(kernel, outs, flops, args, specs=None, scratch=()):
    if specs:
        args = [pltpu.with_memory_space_constraint(a, pltpu.HBM) if s is HBM else a for a, s in zip(args, specs)]
    nbytes = sum(a.size * a.dtype.itemsize for a in args)
    return pl.pallas_call(
        kernel,
        out_shape=outs,
        in_specs=specs or [VMEM] * len(args),
        out_specs=jax.tree.map(lambda _: VMEM, outs),
        scratch_shapes=list(scratch),
        cost_estimate=pl.CostEstimate(flops=flops, transcendentals=0, bytes_accessed=nbytes),
        compiler_params=pltpu.CompilerParams(vmem_limit_bytes=5 << 20),
    )(*args)


def dot(a, b):
    return jnp.dot(a, b, preferred_element_type=F32)


def dot_t(a, b):
    return lax.dot_general(a, b, (((0,), (0,)), ((), ())), preferred_element_type=F32)


def interleave(value, scratch_ref, dst_ref):
    count = value.shape[0] // SIDE
    for g in range(value.shape[1] // LANES):
        lanes = slice(g * LANES, (g + 1) * LANES)
        scratch_ref[g] = value[:, lanes]
        for t in range(SIDE // 2):
            pair = [scratch_ref[g, pl.ds(2 * t + h, count, stride=SIDE), :] for h in range(2)]
            dst_ref[2 * t * count : (2 * t + 2) * count, lanes] = jnp.concatenate(pair, axis=0).astype(BF16)


def restored(value, scratch_ref):
    count = value.shape[0] // SIDE
    columns = []
    for g in range(value.shape[1] // LANES):
        scratch_ref[g] = value[:, g * LANES : (g + 1) * LANES]
        columns.append(jnp.concatenate([scratch_ref[g, pl.ds(b, SIDE, stride=count), :] for b in range(count)], axis=0))
    return jnp.concatenate(columns, axis=1)


def build(half, sizes, blocks_hbm, row_hbm, col_hbm, blocks, ids, sems, stores):
    count, row_devs, ka_devs = sizes
    bits, row_bits = log2(count), log2(row_devs)
    copies = [pltpu.make_async_copy(h, ids.at[k : k + 1], sems.at[k]) for k, h in enumerate((row_hbm, col_hbm))]
    width = blocks.shape[1] // PIECES
    for k in range(PIECES):
        lanes = pl.ds(k * width, width)
        copies.append(pltpu.make_async_copy(blocks_hbm.at[:, lanes], blocks.at[:, lanes], sems.at[2 + k]))
    for copy in copies:
        copy.start()
    copies[0].wait()
    copies[1].wait()
    row = ids[0:1, :]
    col = ids[1:2, :]
    row_place = (row >> bits) & (row_devs - 1)
    ka_step = ((col >> (bits + row_bits)) - (row >> (bits + row_bits))) & (ka_devs - 1)
    row_step = (((col >> bits) & (row_devs - 1)) - row_place + 1) & (row_devs - 1)
    is_mate = (row_step >> 1) == ((row_place & 1) ^ 1)
    group = jnp.where(row_step == 1, 0, jnp.where(is_mate, 1, 2))
    band = group * count + (col & (count - 1))
    pairs = 3 * count // 2
    place = ((band & 1) * pairs + (band >> 1)) * count + (row & (count - 1))
    place = jnp.where((row >= 0) & (ka_step == half), place, -1)
    slots = blocks.shape[0]
    chosen = lax.broadcasted_iota(jnp.int32, (2 * pairs * count, slots), 0) == place
    chosen = jnp.where(chosen, 1.0, 0.0).astype(BF16)
    low = lax.broadcasted_iota(jnp.int32, (pairs * count, LANES), 1) < SIDE
    for u in range(SIDE // 4):
        if u % (SIDE // 4 // PIECES) == 0:
            copies[2 + u // (SIDE // 4 // PIECES)].wait()
        found = dot(chosen, blocks[:, u * 2 * LANES : (u + 1) * 2 * LANES])
        for w in range(2):
            t = 2 * u + w
            even = found[: pairs * count, w * LANES : (w + 1) * LANES]
            odd = found[pairs * count :, w * LANES : (w + 1) * LANES]
            first = jnp.where(low, even, pltpu.roll(odd, SIDE, 1))
            second = jnp.where(low, pltpu.roll(even, SIDE, 1), odd)
            for q in range(pairs):
                pair = [v[q * count : (q + 1) * count, :] for v in (first, second)]
                tile = jnp.concatenate(pair, axis=0).astype(BF16)
                per = pairs // 3
                lanes = slice((q % per) * LANES, (q % per + 1) * LANES)
                stores[q // per][2 * t * count : (2 * t + 2) * count, lanes] = tile


def emit(cross, wire, perm, self_ref, mate_ref, far_ref):
    self_ref[...] = dot_t(cross[0][...], perm)
    for k, ref in ((2, far_ref), (1, mate_ref)):
        ref[0] = dot_t(cross[k][...], perm).astype(BF16)
        ref[1] = wire


def emit_body(*refs):
    emit(refs[:3], refs[4][...], refs[3][...], *refs[5:])


def lanes_of(half):
    return slice(half * LANES, (half + 1) * LANES)


def first_body(sizes, blocks_hbm, row_hbm, col_hbm, drive_hbm, relax_hbm, *refs):
    cross, perms, wires, spread_ref = refs[:3], refs[3:5], refs[5:7], refs[7]
    blocks, ids, drive, relax, scratch, sems = refs[8:]
    later = [
        pltpu.make_async_copy(drive_hbm, drive, sems.at[2 + PIECES]),
        pltpu.make_async_copy(relax_hbm, relax, sems.at[3 + PIECES]),
    ]
    for copy in later:
        copy.start()
    build(1, sizes, blocks_hbm, row_hbm, col_hbm, blocks, ids, sems, cross)
    for copy in later:
        copy.wait()
    spread_ref[...] = jnp.broadcast_to(relax[...], (LANES, relax.shape[1])).T
    for half in range(2):
        field = drive[:, lanes_of(half)]
        interleave(field, scratch, perms[half])
        wires[half][...] = field.astype(BF16)


def second_body(sizes, blocks_hbm, row_hbm, col_hbm, *refs):
    build(0, sizes, blocks_hbm, row_hbm, col_hbm, *refs[3:], refs[:3])


def partials(mats, perm_ref, outs):
    perm = perm_ref[...]
    for matrix, ref in zip(mats, outs):
        ref[...] = dot_t(matrix[...], perm).astype(ref.dtype)


def third_body(*refs):
    partials(refs[:3], refs[3], refs[4:])


def own_body(*refs):
    mats, (wire_ref, mate_ref, far_ref, self_ref), (out_ref, scratch) = refs[:3], refs[3:7], refs[7:]
    straight = dot(mats[0][...], wire_ref[...])
    straight += dot(mats[1][...], mate_ref[1])
    straight += dot(mats[2][...], far_ref[1])
    out_ref[...] = self_ref[...] + restored(straight, scratch)


def with_cross(cross, down_ref, mate_ref, far_ref, known_ref, scratch):
    straight = dot(cross[0][...], down_ref[...])
    straight += dot(cross[1][...], mate_ref[0])
    straight += dot(cross[2][...], far_ref[0])
    return known_ref[...] + mate_ref[1].astype(F32) + far_ref[1].astype(F32) + restored(straight, scratch)


def advanced(half, product, drive_ref, relax_ref):
    return drive_ref[:, lanes_of(half)] + relax_ref[...] * product


def update_body(half, *refs):
    cross, nexts, (drive_ref, relax_ref) = refs[:3], refs[3:7], refs[7:9]
    perm_ref, wire_ref, self_ref, mate_ref, far_ref, scratch = refs[9:]
    field = advanced(half, with_cross(cross, *nexts, scratch), drive_ref, relax_ref)
    interleave(field, scratch, perm_ref)
    wire_ref[...] = field.astype(BF16)
    emit(cross, wire_ref[...], perm_ref[...], self_ref, mate_ref, far_ref)


def settle_body(own_ref, received_ref, out_ref):
    out_ref[...] = own_ref[...] + received_ref[...].astype(F32)


def final_body(half, *refs):
    product = with_cross(refs[:3], *refs[3:7], refs[-1])
    refs[-2][:, lanes_of(half) if half else slice(None)] = advanced(half, product, *refs[7:9])
    if half:
        refs[-2][:, lanes_of(0)] = refs[9][...]


def local(drive, relax, blocks, row_block, col_block):
    rows, channels = drive.shape
    slots = blocks.shape[0]
    sizes = (rows // SIDE, lax.axis_size("rows"), lax.axis_size("ka"))
    full = jax.ShapeDtypeStruct((rows, channels), F32)
    small = jax.ShapeDtypeStruct((rows, LANES), BF16)
    double = jax.ShapeDtypeStruct((2, rows, LANES), BF16)
    wide = jax.ShapeDtypeStruct((rows, LANES), F32)
    emitted = (wide, double, double)
    matrices = (jax.ShapeDtypeStruct((rows, rows), BF16),) * 3
    staging = pltpu.VMEM((1, rows, LANES), F32)
    fetch = [pltpu.VMEM(blocks.shape, BF16), pltpu.VMEM((2, slots), jnp.int32)]
    row2 = row_block.reshape(1, -1)
    col2 = col_block.reshape(1, -1)
    relax2 = relax.reshape(1, -1)
    work = rows * rows * channels
    *cross, perm0, perm1, wire0, wire1, relax3 = call(
        functools.partial(first_body, sizes), (*matrices, small, small, small, small, wide), 12 * work,
        [blocks, row2, col2, drive, relax2], [HBM] * 5,
        fetch + [pltpu.VMEM(drive.shape, F32), pltpu.VMEM((1, rows), F32), staging, pltpu.SemaphoreType.DMA((4 + PIECES,))],
    )
    streams = [(perm, wire, *call(emit_body, emitted, 3 * work, [*cross, perm, wire])) for perm, wire in ((perm0, wire0), (perm1, wire1))]
    own = call(
        functools.partial(second_body, sizes), matrices, 9 * work, [blocks, row2, col2], [HBM] * 3,
        fetch + [pltpu.SemaphoreType.DMA((2 + PIECES,))],
    )
    done = []
    for sweep in range(ITERS):
        for half in range(2):
            perm, wire, partial, to_mate, to_far = streams[half]
            down = shifted(wire, "ka", -1)
            from_far = far(to_far)
            from_mate = mate(to_mate)
            own_self, own_mate, own_far = call(third_body, (wide, small, small), 3 * work, [*own, perm])
            from_far, _ = lax.optimization_barrier((from_far, own_self))
            got = (partial + from_mate[0].astype(F32) + from_far[0].astype(F32)).astype(BF16)
            received = shifted(got, "ka", 1)
            second_mate = mate(jnp.stack([down, own_mate]))
            second_far = far(jnp.stack([down, own_far]))
            known = call(own_body, wide, 3 * work, [*own, wire, from_mate, from_far, own_self], scratch=[staging])
            known = call(settle_body, wide, HEAVY * work, [known, received])
            args = [*cross, down, second_mate, second_far, known, drive, relax3]
            if sweep + 1 == ITERS:
                out = full if half else wide
                done.append(call(functools.partial(final_body, half), out, 3 * work, [*args, *done], scratch=[staging]))
            else:
                body = functools.partial(update_body, half)
                streams[half] = call(body, (small, small, *emitted), 6 * work, args, scratch=[staging])
    return done[1]


def solution(mesh):
    spread = P(("ka", "rows"))
    wide = P(("ka", "rows"), None)
    return jax.shard_map(
        local, mesh=mesh, in_specs=(wide, spread, wide, spread, spread), out_specs=wide, check_vma=False
    )
```

```python
import functools

import jax
import jax.numpy as jnp
from jax import lax
from jax.experimental import pallas as pl
from jax.experimental.pallas import tpu as pltpu
from jax.sharding import PartitionSpec as P

SIDE = 64
LANES = 128
ITERS = 2
PIECES = 4
HEAVY = 90
BF16, F32 = jnp.bfloat16, jnp.float32
VMEM = pl.BlockSpec(memory_space=pltpu.VMEM)
HBM = pl.BlockSpec(memory_space=pltpu.HBM)


def log2(n):
    assert n & (n - 1) == 0
    return n.bit_length() - 1


def shifted(value, axis, steps):
    count = lax.axis_size(axis)
    return lax.ppermute(value, axis, [(source, (source + steps) % count) for source in range(count)])


def mate(value):
    return lax.ppermute(value, "rows", [(i, i ^ 1) for i in range(lax.axis_size("rows"))])


def far(value):
    count = lax.axis_size("rows")
    return lax.ppermute(value, "rows", [(i, (i + 1 if i & 1 else i - 1) % count) for i in range(count)])


def call(kernel, outs, flops, args, specs=None, scratch=()):
    if specs:
        args = [pltpu.with_memory_space_constraint(a, pltpu.HBM) for a in args]
    nbytes = sum(a.size * a.dtype.itemsize for a in args)
    return pl.pallas_call(
        kernel,
        out_shape=outs,
        in_specs=specs or [VMEM] * len(args),
        out_specs=jax.tree.map(lambda _: VMEM, outs),
        scratch_shapes=list(scratch),
        cost_estimate=pl.CostEstimate(flops=flops, transcendentals=0, bytes_accessed=nbytes),
        compiler_params=pltpu.CompilerParams(vmem_limit_bytes=5 << 20),
    )(*args)


def dot(a, b):
    return jnp.dot(a, b, preferred_element_type=F32)


def dot_t(a, b):
    return lax.dot_general(a, b, (((0,), (0,)), ((), ())), preferred_element_type=F32)


def interleave(value, scratch_ref, dst_ref):
    count = value.shape[0] // SIDE
    for g in range(value.shape[1] // LANES):
        lanes = slice(g * LANES, (g + 1) * LANES)
        scratch_ref[g] = value[:, lanes]
        for t in range(SIDE // 2):
            pair = [scratch_ref[g, pl.ds(2 * t + h, count, stride=SIDE), :] for h in range(2)]
            dst_ref[2 * t * count : (2 * t + 2) * count, lanes] = jnp.concatenate(pair, axis=0).astype(BF16)


def restored(value, scratch_ref):
    count = value.shape[0] // SIDE
    columns = []
    for g in range(value.shape[1] // LANES):
        scratch_ref[g] = value[:, g * LANES : (g + 1) * LANES]
        columns.append(jnp.concatenate([scratch_ref[g, pl.ds(b, SIDE, stride=count), :] for b in range(count)], axis=0))
    return jnp.concatenate(columns, axis=1)


def build(half, sizes, blocks_hbm, row_hbm, col_hbm, blocks, ids, sems, stores):
    count, row_devs, ka_devs = sizes
    bits, row_bits = log2(count), log2(row_devs)
    copies = [pltpu.make_async_copy(h, ids.at[k : k + 1], sems.at[k]) for k, h in enumerate((row_hbm, col_hbm))]
    width = blocks.shape[1] // PIECES
    for k in range(PIECES):
        lanes = pl.ds(k * width, width)
        copies.append(pltpu.make_async_copy(blocks_hbm.at[:, lanes], blocks.at[:, lanes], sems.at[2 + k]))
    for copy in copies:
        copy.start()
    copies[0].wait()
    copies[1].wait()
    row = ids[0:1, :]
    col = ids[1:2, :]
    row_place = (row >> bits) & (row_devs - 1)
    ka_step = ((col >> (bits + row_bits)) - (row >> (bits + row_bits))) & (ka_devs - 1)
    row_step = (((col >> bits) & (row_devs - 1)) - row_place + 1) & (row_devs - 1)
    is_mate = (row_step >> 1) == ((row_place & 1) ^ 1)
    group = jnp.where(row_step == 1, 0, jnp.where(is_mate, 1, 2))
    band = group * count + (col & (count - 1))
    pairs = 3 * count // 2
    place = ((band & 1) * pairs + (band >> 1)) * count + (row & (count - 1))
    place = jnp.where((row >= 0) & (ka_step == half), place, -1)
    slots = blocks.shape[0]
    chosen = lax.broadcasted_iota(jnp.int32, (2 * pairs * count, slots), 0) == place
    chosen = jnp.where(chosen, 1.0, 0.0).astype(BF16)
    low = lax.broadcasted_iota(jnp.int32, (pairs * count, LANES), 1) < SIDE
    for u in range(SIDE // 4):
        if u % (SIDE // 4 // PIECES) == 0:
            copies[2 + u // (SIDE // 4 // PIECES)].wait()
        found = dot(chosen, blocks[:, u * 2 * LANES : (u + 1) * 2 * LANES])
        for w in range(2):
            t = 2 * u + w
            even = found[: pairs * count, w * LANES : (w + 1) * LANES]
            odd = found[pairs * count :, w * LANES : (w + 1) * LANES]
            first = jnp.where(low, even, pltpu.roll(odd, SIDE, 1))
            second = jnp.where(low, pltpu.roll(even, SIDE, 1), odd)
            for q in range(pairs):
                pair = [v[q * count : (q + 1) * count, :] for v in (first, second)]
                tile = jnp.concatenate(pair, axis=0).astype(BF16)
                per = pairs // 3
                lanes = slice((q % per) * LANES, (q % per + 1) * LANES)
                stores[q // per][2 * t * count : (2 * t + 2) * count, lanes] = tile


def emit(cross, wire, perm_ref, wire_ref, self_ref, mate_ref, far_ref):
    perm = perm_ref[...]
    wire_ref[...] = wire
    self_ref[...] = dot_t(cross[0][...], perm)
    far_ref[...] = dot_t(cross[2][...], perm).astype(BF16)
    mate_ref[0] = dot_t(cross[1][...], perm).astype(BF16)
    mate_ref[1] = wire


def first_body(sizes, blocks_hbm, row_hbm, col_hbm, drive_hbm, relax_hbm, *refs):
    cross, (perm_ref, wire_ref, self_ref, mate_ref, far_ref, spread_ref) = refs[:3], refs[3:9]
    blocks, ids, drive, relax, scratch, sems = refs[9:]
    later = [
        pltpu.make_async_copy(drive_hbm, drive, sems.at[2 + PIECES]),
        pltpu.make_async_copy(relax_hbm, relax, sems.at[3 + PIECES]),
    ]
    for copy in later:
        copy.start()
    build(1, sizes, blocks_hbm, row_hbm, col_hbm, blocks, ids, sems, cross)
    for copy in later:
        copy.wait()
    spread_ref[...] = jnp.broadcast_to(relax[...], (LANES, relax.shape[1])).T
    field = drive[...]
    interleave(field, scratch, perm_ref)
    emit(cross, field.astype(BF16), perm_ref, wire_ref, self_ref, mate_ref, far_ref)


def second_body(sizes, blocks_hbm, row_hbm, col_hbm, *refs):
    build(0, sizes, blocks_hbm, row_hbm, col_hbm, *refs[3:], refs[:3])


def sent_terms(sent, fields, scratch, other):
    total = 0.0
    for matrix, field in zip(sent, fields):
        interleave(field.astype(F32), scratch, other)
        total += dot_t(matrix[...], other[...])
    return total


def own_body(*refs):
    mats, (wire_ref, perm_ref, mate_ref, field_ref), sent = refs[:3], refs[3:7], refs[7:-3]
    out_ref, scratch, other = refs[-3:]
    straight = dot(mats[0][...], wire_ref[...])
    straight += dot(mats[1][...], mate_ref[1])
    straight += dot(mats[2][...], field_ref[...])
    total = dot_t(mats[0][...], perm_ref[...])
    if sent:
        total += sent_terms(sent, (mate_ref[1], field_ref[...]), scratch, other)
    out_ref[...] = total + restored(straight, scratch)


def with_cross(cross, nexts, known_ref, scratch):
    straight = dot(cross[0][...], nexts[0][...])
    straight += dot(cross[1][...], nexts[1][...])
    straight += dot(cross[2][...], nexts[2][...])
    return known_ref[...] + restored(straight, scratch)


def advanced(product, drive_ref, relax_ref):
    scale = jnp.concatenate([relax_ref[...]] * (product.shape[1] // LANES), axis=1)
    return drive_ref[...] + scale * product


def cross_body(*refs):
    refs[7][...] = with_cross(refs[:3], refs[3:6], refs[6], refs[8])


def update_body(*refs):
    cross, (known_ref, drive_ref, relax_ref, mate_in, field_in), sent = refs[:3], refs[3:8], refs[8:10]
    perm_ref, wire_ref, self_ref, mate_ref, far_ref, scratch, other = refs[10:]
    late = sent_terms(sent, (mate_in[1], field_in[...]), scratch, other)
    field = advanced(known_ref[...] + late, drive_ref, relax_ref)
    interleave(field, scratch, perm_ref)
    emit(cross, field.astype(BF16), perm_ref, wire_ref, self_ref, mate_ref, far_ref)


def settle_body(own_ref, received_ref, out_ref):
    out_ref[...] = own_ref[...] + received_ref[...].astype(F32)


def final_body(*refs):
    product = with_cross(refs[:3], refs[3:6], refs[6], refs[10])
    refs[9][...] = advanced(product, *refs[7:9])


def local(drive, relax, blocks, row_block, col_block):
    rows, channels = drive.shape
    slots = blocks.shape[0]
    sizes = (rows // SIDE, lax.axis_size("rows"), lax.axis_size("ka"))
    small = jax.ShapeDtypeStruct((rows, channels), BF16)
    double = jax.ShapeDtypeStruct((2, rows, channels), BF16)
    wide = jax.ShapeDtypeStruct((rows, channels), F32)
    matrices = (jax.ShapeDtypeStruct((rows, rows), BF16),) * 3
    emitted = (small, small, wide, double, small)
    staging = pltpu.VMEM((channels // LANES, rows, LANES), F32)
    fetch = [pltpu.VMEM(blocks.shape, BF16), pltpu.VMEM((2, slots), jnp.int32)]
    row2 = row_block.reshape(1, -1)
    col2 = col_block.reshape(1, -1)
    relax2 = relax.reshape(1, -1)
    work = 2 * rows * rows * channels
    spread = jax.ShapeDtypeStruct((rows, LANES), F32)
    *cross, perm, wire, partial, to_mate, to_far, relax3 = call(
        functools.partial(first_body, sizes), (*matrices, *emitted, spread), 9 * work,
        [blocks, row2, col2, drive, relax2], [HBM] * 5,
        fetch + [pltpu.VMEM(drive.shape, F32), pltpu.VMEM((1, rows), F32), staging, pltpu.SemaphoreType.DMA((4 + PIECES,))],
    )

    extra = [staging, pltpu.VMEM((rows, channels), BF16)]
    for sweep in range(ITERS):
        down = shifted(wire, "ka", -1)
        from_far = far(to_far)
        from_mate = mate(to_mate)
        if sweep == 0:
            own = call(
                functools.partial(second_body, sizes), matrices, 6 * work, [blocks, row2, col2], [HBM] * 3,
                fetch + [pltpu.SemaphoreType.DMA((2 + PIECES,))],
            )
        if sweep == 0:
            from_far, _ = lax.optimization_barrier((from_far, own))
        got = (partial + from_mate[0].astype(F32) + from_far.astype(F32)).astype(BF16)
        received = shifted(got, "ka", 1)
        if sweep == 0:
            gated, down = lax.optimization_barrier((own[1:], down))
            sent = [mate(gated[0]), far(gated[1])]
        nexts = [down, mate(down), far(down)]
        gated, _ = lax.optimization_barrier((wire, got))
        from_other = far(gated)
        args = [*own, wire, perm, from_mate, from_other, *(sent if sweep else [])]
        known = call(own_body, wide, 9 * work, args, scratch=extra)
        known = call(settle_body, wide, HEAVY * work, [known, received])
        if sweep + 1 == ITERS:
            return call(final_body, wide, 3 * work, [*cross, *nexts, known, drive, relax3], scratch=[staging])
        known = call(cross_body, wide, HEAVY * work, [*cross, *nexts, known], scratch=[staging])
        args = [*cross, known, drive, relax3, from_mate, from_other, *sent]
        perm, wire, partial, to_mate, to_far = call(update_body, emitted, 8 * work, args, scratch=extra)


def solution(mesh):
    spread = P(("ka", "rows"))
    wide = P(("ka", "rows"), None)
    return jax.shard_map(
        local, mesh=mesh, in_specs=(wide, spread, wide, spread, spread), out_specs=wide, check_vma=False
    )
```

```python
import functools

import jax
import jax.numpy as jnp
from jax import lax
from jax.experimental import pallas as pl
from jax.experimental.pallas import tpu as pltpu
from jax.sharding import PartitionSpec as P

SIDE = 64
LANES = 128
ITERS = 2
PIECES = 4
HEAVY = 90
BF16, F32 = jnp.bfloat16, jnp.float32
VMEM = pl.BlockSpec(memory_space=pltpu.VMEM)
HBM = pl.BlockSpec(memory_space=pltpu.HBM)


def log2(n):
    assert n & (n - 1) == 0
    return n.bit_length() - 1


def shifted(value, axis, steps):
    count = lax.axis_size(axis)
    return lax.ppermute(value, axis, [(source, (source + steps) % count) for source in range(count)])


def mate(value):
    return lax.ppermute(value, "rows", [(i, i ^ 1) for i in range(lax.axis_size("rows"))])


def far(value):
    count = lax.axis_size("rows")
    return lax.ppermute(value, "rows", [(i, (i + 1 if i & 1 else i - 1) % count) for i in range(count)])


def call(kernel, outs, flops, args, specs=None, scratch=()):
    if specs:
        args = [pltpu.with_memory_space_constraint(a, pltpu.HBM) for a in args]
    nbytes = sum(a.size * a.dtype.itemsize for a in args)
    return pl.pallas_call(
        kernel,
        out_shape=outs,
        in_specs=specs or [VMEM] * len(args),
        out_specs=jax.tree.map(lambda _: VMEM, outs),
        scratch_shapes=list(scratch),
        cost_estimate=pl.CostEstimate(flops=flops, transcendentals=0, bytes_accessed=nbytes),
        compiler_params=pltpu.CompilerParams(vmem_limit_bytes=5 << 20),
    )(*args)


def dot(a, b):
    return jnp.dot(a, b, preferred_element_type=F32)


def dot_t(a, b):
    return lax.dot_general(a, b, (((0,), (0,)), ((), ())), preferred_element_type=F32)


def interleave(value, scratch_ref, dst_ref):
    count = value.shape[0] // SIDE
    for g in range(value.shape[1] // LANES):
        lanes = slice(g * LANES, (g + 1) * LANES)
        scratch_ref[g] = value[:, lanes]
        for t in range(SIDE // 2):
            pair = [scratch_ref[g, pl.ds(2 * t + h, count, stride=SIDE), :] for h in range(2)]
            dst_ref[2 * t * count : (2 * t + 2) * count, lanes] = jnp.concatenate(pair, axis=0).astype(BF16)


def restored(value, scratch_ref):
    count = value.shape[0] // SIDE
    columns = []
    for g in range(value.shape[1] // LANES):
        scratch_ref[g] = value[:, g * LANES : (g + 1) * LANES]
        columns.append(jnp.concatenate([scratch_ref[g, pl.ds(b, SIDE, stride=count), :] for b in range(count)], axis=0))
    return jnp.concatenate(columns, axis=1)


def build(half, sizes, blocks_hbm, row_hbm, col_hbm, blocks, ids, sems, stores):
    count, row_devs, ka_devs = sizes
    bits, row_bits = log2(count), log2(row_devs)
    copies = [pltpu.make_async_copy(h, ids.at[k : k + 1], sems.at[k]) for k, h in enumerate((row_hbm, col_hbm))]
    width = blocks.shape[1] // PIECES
    for k in range(PIECES):
        lanes = pl.ds(k * width, width)
        copies.append(pltpu.make_async_copy(blocks_hbm.at[:, lanes], blocks.at[:, lanes], sems.at[2 + k]))
    for copy in copies:
        copy.start()
    copies[0].wait()
    copies[1].wait()
    row = ids[0:1, :]
    col = ids[1:2, :]
    row_place = (row >> bits) & (row_devs - 1)
    ka_step = ((col >> (bits + row_bits)) - (row >> (bits + row_bits))) & (ka_devs - 1)
    row_step = (((col >> bits) & (row_devs - 1)) - row_place + 1) & (row_devs - 1)
    is_mate = (row_step >> 1) == ((row_place & 1) ^ 1)
    group = jnp.where(row_step == 1, 0, jnp.where(is_mate, 1, 2))
    band = group * count + (col & (count - 1))
    pairs = 3 * count // 2
    place = ((band & 1) * pairs + (band >> 1)) * count + (row & (count - 1))
    place = jnp.where((row >= 0) & (ka_step == half), place, -1)
    slots = blocks.shape[0]
    chosen = lax.broadcasted_iota(jnp.int32, (2 * pairs * count, slots), 0) == place
    chosen = jnp.where(chosen, 1.0, 0.0).astype(BF16)
    low = lax.broadcasted_iota(jnp.int32, (pairs * count, LANES), 1) < SIDE
    for u in range(SIDE // 4):
        if u % (SIDE // 4 // PIECES) == 0:
            copies[2 + u // (SIDE // 4 // PIECES)].wait()
        found = dot(chosen, blocks[:, u * 2 * LANES : (u + 1) * 2 * LANES])
        for w in range(2):
            t = 2 * u + w
            even = found[: pairs * count, w * LANES : (w + 1) * LANES]
            odd = found[pairs * count :, w * LANES : (w + 1) * LANES]
            first = jnp.where(low, even, pltpu.roll(odd, SIDE, 1))
            second = jnp.where(low, pltpu.roll(even, SIDE, 1), odd)
            for q in range(pairs):
                pair = [v[q * count : (q + 1) * count, :] for v in (first, second)]
                tile = jnp.concatenate(pair, axis=0).astype(BF16)
                per = pairs // 3
                lanes = slice((q % per) * LANES, (q % per + 1) * LANES)
                stores[q // per][2 * t * count : (2 * t + 2) * count, lanes] = tile


def emit(cross, wire, perm_ref, wire_ref, self_ref, mate_ref, far_ref):
    perm = perm_ref[...]
    wire_ref[...] = wire
    self_ref[...] = dot_t(cross[0][...], perm)
    far_ref[...] = dot_t(cross[2][...], perm).astype(BF16)
    mate_ref[0] = dot_t(cross[1][...], perm).astype(BF16)
    mate_ref[1] = wire


def first_body(sizes, blocks_hbm, row_hbm, col_hbm, drive_hbm, relax_hbm, *refs):
    cross, (perm_ref, wire_ref, self_ref, mate_ref, far_ref, spread_ref) = refs[:3], refs[3:9]
    blocks, ids, drive, relax, scratch, sems = refs[9:]
    later = [
        pltpu.make_async_copy(drive_hbm, drive, sems.at[2 + PIECES]),
        pltpu.make_async_copy(relax_hbm, relax, sems.at[3 + PIECES]),
    ]
    for copy in later:
        copy.start()
    build(1, sizes, blocks_hbm, row_hbm, col_hbm, blocks, ids, sems, cross)
    for copy in later:
        copy.wait()
    spread_ref[...] = jnp.broadcast_to(relax[...], (LANES, relax.shape[1])).T
    field = drive[...]
    interleave(field, scratch, perm_ref)
    emit(cross, field.astype(BF16), perm_ref, wire_ref, self_ref, mate_ref, far_ref)


def second_body(sizes, blocks_hbm, row_hbm, col_hbm, *refs):
    build(0, sizes, blocks_hbm, row_hbm, col_hbm, *refs[3:], refs[:3])


def sent_terms(sent, fields, scratch, other):
    total = 0.0
    for matrix, field in zip(sent, fields):
        interleave(field.astype(F32), scratch, other)
        total += dot_t(matrix[...], other[...])
    return total


def own_body(*refs):
    mats, (wire_ref, perm_ref, mate_ref, field_ref), sent = refs[:3], refs[3:7], refs[7:-3]
    out_ref, scratch, other = refs[-3:]
    straight = dot(mats[0][...], wire_ref[...])
    straight += dot(mats[1][...], mate_ref[1])
    straight += dot(mats[2][...], field_ref[...])
    total = dot_t(mats[0][...], perm_ref[...])
    if sent:
        total += sent_terms(sent, (mate_ref[1], field_ref[...]), scratch, other)
    out_ref[...] = total + restored(straight, scratch)


def with_cross(cross, nexts, known_ref, scratch):
    straight = dot(cross[0][...], nexts[0][...])
    straight += dot(cross[1][...], nexts[1][...])
    straight += dot(cross[2][...], nexts[2][...])
    return known_ref[...] + restored(straight, scratch)


def advanced(product, drive_ref, relax_ref):
    scale = jnp.concatenate([relax_ref[...]] * (product.shape[1] // LANES), axis=1)
    return drive_ref[...] + scale * product


def cross_body(*refs):
    refs[7][...] = with_cross(refs[:3], refs[3:6], refs[6], refs[8])


def update_body(*refs):
    cross, (known_ref, drive_ref, relax_ref, mate_in, field_in), sent = refs[:3], refs[3:8], refs[8:10]
    perm_ref, wire_ref, self_ref, mate_ref, far_ref, scratch, other = refs[10:]
    late = sent_terms(sent, (mate_in[1], field_in[...]), scratch, other)
    field = advanced(known_ref[...] + late, drive_ref, relax_ref)
    interleave(field, scratch, perm_ref)
    emit(cross, field.astype(BF16), perm_ref, wire_ref, self_ref, mate_ref, far_ref)


def settle_body(own_ref, received_ref, out_ref):
    out_ref[...] = own_ref[...] + received_ref[...].astype(F32)


def final_body(*refs):
    product = with_cross(refs[:3], refs[3:6], refs[6], refs[10])
    refs[9][...] = advanced(product, *refs[7:9])


def local(drive, relax, blocks, row_block, col_block):
    rows, channels = drive.shape
    slots = blocks.shape[0]
    sizes = (rows // SIDE, lax.axis_size("rows"), lax.axis_size("ka"))
    small = jax.ShapeDtypeStruct((rows, channels), BF16)
    double = jax.ShapeDtypeStruct((2, rows, channels), BF16)
    wide = jax.ShapeDtypeStruct((rows, channels), F32)
    matrices = (jax.ShapeDtypeStruct((rows, rows), BF16),) * 3
    emitted = (small, small, wide, double, small)
    staging = pltpu.VMEM((channels // LANES, rows, LANES), F32)
    fetch = [pltpu.VMEM(blocks.shape, BF16), pltpu.VMEM((2, slots), jnp.int32)]
    row2 = row_block.reshape(1, -1)
    col2 = col_block.reshape(1, -1)
    relax2 = relax.reshape(1, -1)
    work = 2 * rows * rows * channels
    spread = jax.ShapeDtypeStruct((rows, LANES), F32)
    *cross, perm, wire, partial, to_mate, to_far, relax3 = call(
        functools.partial(first_body, sizes), (*matrices, *emitted, spread), 9 * work,
        [blocks, row2, col2, drive, relax2], [HBM] * 5,
        fetch + [pltpu.VMEM(drive.shape, F32), pltpu.VMEM((1, rows), F32), staging, pltpu.SemaphoreType.DMA((4 + PIECES,))],
    )

    extra = [staging, pltpu.VMEM((rows, channels), BF16)]
    for sweep in range(ITERS):
        down = shifted(wire, "ka", -1)
        from_far = far(to_far)
        from_mate = mate(to_mate)
        if sweep == 0:
            own = call(
                functools.partial(second_body, sizes), matrices, 6 * work, [blocks, row2, col2], [HBM] * 3,
                fetch + [pltpu.SemaphoreType.DMA((2 + PIECES,))],
            )
        if sweep == 0:
            from_far, _ = lax.optimization_barrier((from_far, own))
        got = (partial + from_mate[0].astype(F32) + from_far.astype(F32)).astype(BF16)
        received = shifted(got, "ka", 1)
        if sweep == 0:
            gated, down = lax.optimization_barrier((own[1:], down))
            sent = [mate(gated[0]), far(gated[1])]
        nexts = [down, mate(down), far(down)]
        from_other = far(wire)
        args = [*own, wire, perm, from_mate, from_other, *(sent if sweep else [])]
        known = call(own_body, wide, 9 * work, args, scratch=extra)
        known = call(settle_body, wide, HEAVY * work, [known, received])
        if sweep + 1 == ITERS:
            return call(final_body, wide, 3 * work, [*cross, *nexts, known, drive, relax3], scratch=[staging])
        known = call(cross_body, wide, HEAVY * work, [*cross, *nexts, known], scratch=[staging])
        args = [*cross, known, drive, relax3, from_mate, from_other, *sent]
        perm, wire, partial, to_mate, to_far = call(update_body, emitted, 8 * work, args, scratch=extra)


def solution(mesh):
    spread = P(("ka", "rows"))
    wide = P(("ka", "rows"), None)
    return jax.shard_map(
        local, mesh=mesh, in_specs=(wide, spread, wide, spread, spread), out_specs=wide, check_vma=False
    )
```

```python
import functools

import jax
import jax.numpy as jnp
from jax import lax
from jax.experimental import pallas as pl
from jax.experimental.pallas import tpu as pltpu
from jax.sharding import PartitionSpec as P

SIDE = 64
LANES = 128
ITERS = 2
PIECES = 4
HEAVY = 90
BF16, F32 = jnp.bfloat16, jnp.float32
VMEM = pl.BlockSpec(memory_space=pltpu.VMEM)
HBM = pl.BlockSpec(memory_space=pltpu.HBM)


def log2(n):
    assert n & (n - 1) == 0
    return n.bit_length() - 1


def shifted(value, axis, steps):
    count = lax.axis_size(axis)
    return lax.ppermute(value, axis, [(source, (source + steps) % count) for source in range(count)])


def mate(value):
    return lax.ppermute(value, "rows", [(i, i ^ 1) for i in range(lax.axis_size("rows"))])


def far(value):
    count = lax.axis_size("rows")
    return lax.ppermute(value, "rows", [(i, (i + 1 if i & 1 else i - 1) % count) for i in range(count)])


def call(kernel, outs, flops, args, specs=None, scratch=()):
    if specs:
        args = [pltpu.with_memory_space_constraint(a, pltpu.HBM) for a in args]
    nbytes = sum(a.size * a.dtype.itemsize for a in args)
    return pl.pallas_call(
        kernel,
        out_shape=outs,
        in_specs=specs or [VMEM] * len(args),
        out_specs=jax.tree.map(lambda _: VMEM, outs),
        scratch_shapes=list(scratch),
        cost_estimate=pl.CostEstimate(flops=flops, transcendentals=0, bytes_accessed=nbytes),
        compiler_params=pltpu.CompilerParams(vmem_limit_bytes=5 << 20),
    )(*args)


def dot(a, b):
    return jnp.dot(a, b, preferred_element_type=F32)


def dot_t(a, b):
    return lax.dot_general(a, b, (((0,), (0,)), ((), ())), preferred_element_type=F32)


def interleave(value, scratch_ref, dst_ref):
    count = value.shape[0] // SIDE
    for g in range(value.shape[1] // LANES):
        lanes = slice(g * LANES, (g + 1) * LANES)
        scratch_ref[g] = value[:, lanes]
        for t in range(SIDE // 2):
            pair = [scratch_ref[g, pl.ds(2 * t + h, count, stride=SIDE), :] for h in range(2)]
            dst_ref[2 * t * count : (2 * t + 2) * count, lanes] = jnp.concatenate(pair, axis=0).astype(BF16)


def restored(value, scratch_ref):
    count = value.shape[0] // SIDE
    columns = []
    for g in range(value.shape[1] // LANES):
        scratch_ref[g] = value[:, g * LANES : (g + 1) * LANES]
        columns.append(jnp.concatenate([scratch_ref[g, pl.ds(b, SIDE, stride=count), :] for b in range(count)], axis=0))
    return jnp.concatenate(columns, axis=1)


def build(half, sizes, blocks_hbm, row_hbm, col_hbm, blocks, ids, sems, stores):
    count, row_devs, ka_devs = sizes
    bits, row_bits = log2(count), log2(row_devs)
    copies = [pltpu.make_async_copy(h, ids.at[k : k + 1], sems.at[k]) for k, h in enumerate((row_hbm, col_hbm))]
    width = blocks.shape[1] // PIECES
    for k in range(PIECES):
        lanes = pl.ds(k * width, width)
        copies.append(pltpu.make_async_copy(blocks_hbm.at[:, lanes], blocks.at[:, lanes], sems.at[2 + k]))
    for copy in copies:
        copy.start()
    copies[0].wait()
    copies[1].wait()
    row = ids[0:1, :]
    col = ids[1:2, :]
    row_place = (row >> bits) & (row_devs - 1)
    ka_step = ((col >> (bits + row_bits)) - (row >> (bits + row_bits))) & (ka_devs - 1)
    row_step = (((col >> bits) & (row_devs - 1)) - row_place + 1) & (row_devs - 1)
    is_mate = (row_step >> 1) == ((row_place & 1) ^ 1)
    group = jnp.where(row_step == 1, 0, jnp.where(is_mate, 1, 2))
    band = group * count + (col & (count - 1))
    pairs = 3 * count // 2
    place = ((band & 1) * pairs + (band >> 1)) * count + (row & (count - 1))
    place = jnp.where((row >= 0) & (ka_step == half), place, -1)
    slots = blocks.shape[0]
    chosen = lax.broadcasted_iota(jnp.int32, (2 * pairs * count, slots), 0) == place
    chosen = jnp.where(chosen, 1.0, 0.0).astype(BF16)
    low = lax.broadcasted_iota(jnp.int32, (pairs * count, LANES), 1) < SIDE
    for u in range(SIDE // 4):
        if u % (SIDE // 4 // PIECES) == 0:
            copies[2 + u // (SIDE // 4 // PIECES)].wait()
        found = dot(chosen, blocks[:, u * 2 * LANES : (u + 1) * 2 * LANES])
        for w in range(2):
            t = 2 * u + w
            even = found[: pairs * count, w * LANES : (w + 1) * LANES]
            odd = found[pairs * count :, w * LANES : (w + 1) * LANES]
            first = jnp.where(low, even, pltpu.roll(odd, SIDE, 1))
            second = jnp.where(low, pltpu.roll(even, SIDE, 1), odd)
            for q in range(pairs):
                pair = [v[q * count : (q + 1) * count, :] for v in (first, second)]
                tile = jnp.concatenate(pair, axis=0).astype(BF16)
                per = pairs // 3
                lanes = slice((q % per) * LANES, (q % per + 1) * LANES)
                stores[q // per][2 * t * count : (2 * t + 2) * count, lanes] = tile


def emit(cross, wire, perm_ref, wire_ref, self_ref, mate_ref, far_ref):
    perm = perm_ref[...]
    wire_ref[...] = wire
    self_ref[...] = dot_t(cross[0][...], perm)
    part = dot_t(cross[2][...], perm).astype(BF16)
    if len(far_ref.shape) == 2:
        far_ref[...] = part
    else:
        far_ref[0] = part
        far_ref[1] = wire
    mate_ref[0] = dot_t(cross[1][...], perm).astype(BF16)
    mate_ref[1] = wire


def first_body(sizes, blocks_hbm, row_hbm, col_hbm, drive_hbm, relax_hbm, *refs):
    cross, (perm_ref, wire_ref, self_ref, mate_ref, far_ref, spread_ref) = refs[:3], refs[3:9]
    blocks, ids, drive, relax, scratch, sems = refs[9:]
    later = [
        pltpu.make_async_copy(drive_hbm, drive, sems.at[2 + PIECES]),
        pltpu.make_async_copy(relax_hbm, relax, sems.at[3 + PIECES]),
    ]
    for copy in later:
        copy.start()
    build(1, sizes, blocks_hbm, row_hbm, col_hbm, blocks, ids, sems, cross)
    for copy in later:
        copy.wait()
    spread_ref[...] = jnp.broadcast_to(relax[...], (LANES, relax.shape[1])).T
    field = drive[...]
    interleave(field, scratch, perm_ref)
    emit(cross, field.astype(BF16), perm_ref, wire_ref, self_ref, mate_ref, far_ref)


def second_body(sizes, blocks_hbm, row_hbm, col_hbm, *refs):
    build(0, sizes, blocks_hbm, row_hbm, col_hbm, *refs[3:], refs[:3])


def field_of(ref):
    return ref[...] if len(ref.shape) == 2 else ref[1]


def sent_terms(sent, fields, scratch, other):
    total = 0.0
    for matrix, field in zip(sent, fields):
        interleave(field.astype(F32), scratch, other)
        total += dot_t(matrix[...], other[...])
    return total


def own_body(*refs):
    mats, (wire_ref, perm_ref, mate_ref, field_ref), sent = refs[:3], refs[3:7], refs[7:-3]
    out_ref, scratch, other = refs[-3:]
    straight = dot(mats[0][...], wire_ref[...])
    straight += dot(mats[1][...], mate_ref[1])
    straight += dot(mats[2][...], field_of(field_ref))
    total = dot_t(mats[0][...], perm_ref[...])
    if sent:
        total += sent_terms(sent, (mate_ref[1], field_of(field_ref)), scratch, other)
    out_ref[...] = total + restored(straight, scratch)


def with_cross(cross, nexts, known_ref, scratch):
    straight = dot(cross[0][...], nexts[0][...])
    straight += dot(cross[1][...], nexts[1][...])
    straight += dot(cross[2][...], nexts[2][...])
    return known_ref[...] + restored(straight, scratch)


def advanced(product, drive_ref, relax_ref):
    scale = jnp.concatenate([relax_ref[...]] * (product.shape[1] // LANES), axis=1)
    return drive_ref[...] + scale * product


def cross_body(*refs):
    refs[7][...] = with_cross(refs[:3], refs[3:6], refs[6], refs[8])


def update_body(*refs):
    cross, (known_ref, drive_ref, relax_ref, mate_in, field_in), sent = refs[:3], refs[3:8], refs[8:10]
    perm_ref, wire_ref, self_ref, mate_ref, far_ref, scratch, other = refs[10:]
    late = sent_terms(sent, (mate_in[1], field_of(field_in)), scratch, other)
    field = advanced(known_ref[...] + late, drive_ref, relax_ref)
    interleave(field, scratch, perm_ref)
    emit(cross, field.astype(BF16), perm_ref, wire_ref, self_ref, mate_ref, far_ref)


def settle_body(own_ref, received_ref, out_ref):
    out_ref[...] = own_ref[...] + received_ref[...].astype(F32)


def final_body(*refs):
    product = with_cross(refs[:3], refs[3:6], refs[6], refs[10])
    refs[9][...] = advanced(product, *refs[7:9])


def local(drive, relax, blocks, row_block, col_block):
    rows, channels = drive.shape
    slots = blocks.shape[0]
    sizes = (rows // SIDE, lax.axis_size("rows"), lax.axis_size("ka"))
    small = jax.ShapeDtypeStruct((rows, channels), BF16)
    double = jax.ShapeDtypeStruct((2, rows, channels), BF16)
    wide = jax.ShapeDtypeStruct((rows, channels), F32)
    matrices = (jax.ShapeDtypeStruct((rows, rows), BF16),) * 3
    emitted = (small, small, wide, double, small)
    staging = pltpu.VMEM((channels // LANES, rows, LANES), F32)
    fetch = [pltpu.VMEM(blocks.shape, BF16), pltpu.VMEM((2, slots), jnp.int32)]
    row2 = row_block.reshape(1, -1)
    col2 = col_block.reshape(1, -1)
    relax2 = relax.reshape(1, -1)
    work = 2 * rows * rows * channels
    spread = jax.ShapeDtypeStruct((rows, LANES), F32)
    *cross, perm, wire, partial, to_mate, to_far, relax3 = call(
        functools.partial(first_body, sizes), (*matrices, *emitted[:4], double, spread), 9 * work,
        [blocks, row2, col2, drive, relax2], [HBM] * 5,
        fetch + [pltpu.VMEM(drive.shape, F32), pltpu.VMEM((1, rows), F32), staging, pltpu.SemaphoreType.DMA((4 + PIECES,))],
    )

    extra = [staging, pltpu.VMEM((rows, channels), BF16)]
    for sweep in range(ITERS):
        down = shifted(wire, "ka", -1)
        from_far = far(to_far)
        from_mate = mate(to_mate)
        if sweep == 0:
            own = call(
                functools.partial(second_body, sizes), matrices, 6 * work, [blocks, row2, col2], [HBM] * 3,
                fetch + [pltpu.SemaphoreType.DMA((2 + PIECES,))],
            )
        if sweep == 0:
            from_far, _ = lax.optimization_barrier((from_far, own))
        got = (partial + from_mate[0].astype(F32) + (from_far if sweep else from_far[0]).astype(F32)).astype(BF16)
        received = shifted(got, "ka", 1)
        if sweep == 0:
            gated, down = lax.optimization_barrier((own[1:], down))
            sent = [mate(gated[0]), far(gated[1])]
        nexts = [down, mate(down), far(down)]
        from_other = far(wire) if sweep else from_far
        args = [*own, wire, perm, from_mate, from_other, *(sent if sweep else [])]
        known = call(own_body, wide, 9 * work, args, scratch=extra)
        known = call(settle_body, wide, HEAVY * work, [known, received])
        if sweep + 1 == ITERS:
            return call(final_body, wide, 3 * work, [*cross, *nexts, known, drive, relax3], scratch=[staging])
        known = call(cross_body, wide, HEAVY * work, [*cross, *nexts, known], scratch=[staging])
        args = [*cross, known, drive, relax3, from_mate, from_other, *sent]
        perm, wire, partial, to_mate, to_far = call(update_body, emitted, 8 * work, args, scratch=extra)


def solution(mesh):
    spread = P(("ka", "rows"))
    wide = P(("ka", "rows"), None)
    return jax.shard_map(
        local, mesh=mesh, in_specs=(wide, spread, wide, spread, spread), out_specs=wide, check_vma=False
    )
```

```python
import functools

import jax
import jax.numpy as jnp
from jax import lax
from jax.experimental import pallas as pl
from jax.experimental.pallas import tpu as pltpu
from jax.sharding import PartitionSpec as P

SIDE = 64
LANES = 128
ITERS = 2
PIECES = 4
HEAVY = 90
BF16, F32 = jnp.bfloat16, jnp.float32
VMEM = pl.BlockSpec(memory_space=pltpu.VMEM)
HBM = pl.BlockSpec(memory_space=pltpu.HBM)


def log2(n):
    assert n & (n - 1) == 0
    return n.bit_length() - 1


def shifted(value, axis, steps):
    count = lax.axis_size(axis)
    return lax.ppermute(value, axis, [(source, (source + steps) % count) for source in range(count)])


def mate(value):
    return lax.ppermute(value, "rows", [(i, i ^ 1) for i in range(lax.axis_size("rows"))])


def far(value):
    count = lax.axis_size("rows")
    return lax.ppermute(value, "rows", [(i, (i + 1 if i & 1 else i - 1) % count) for i in range(count)])


def call(kernel, outs, flops, args, specs=None, scratch=()):
    if specs:
        args = [pltpu.with_memory_space_constraint(a, pltpu.HBM) for a in args]
    nbytes = sum(a.size * a.dtype.itemsize for a in args)
    return pl.pallas_call(
        kernel,
        out_shape=outs,
        in_specs=specs or [VMEM] * len(args),
        out_specs=jax.tree.map(lambda _: VMEM, outs),
        scratch_shapes=list(scratch),
        cost_estimate=pl.CostEstimate(flops=flops, transcendentals=0, bytes_accessed=nbytes),
        compiler_params=pltpu.CompilerParams(vmem_limit_bytes=5 << 20),
    )(*args)


def dot(a, b):
    return jnp.dot(a, b, preferred_element_type=F32)


def dot_t(a, b):
    return lax.dot_general(a, b, (((0,), (0,)), ((), ())), preferred_element_type=F32)


def interleave(value, scratch_ref, dst_ref):
    count = value.shape[0] // SIDE
    for g in range(value.shape[1] // LANES):
        lanes = slice(g * LANES, (g + 1) * LANES)
        scratch_ref[g] = value[:, lanes]
        for t in range(SIDE // 2):
            pair = [scratch_ref[g, pl.ds(2 * t + h, count, stride=SIDE), :] for h in range(2)]
            dst_ref[2 * t * count : (2 * t + 2) * count, lanes] = jnp.concatenate(pair, axis=0).astype(BF16)


def restored(value, scratch_ref):
    count = value.shape[0] // SIDE
    columns = []
    for g in range(value.shape[1] // LANES):
        scratch_ref[g] = value[:, g * LANES : (g + 1) * LANES]
        columns.append(jnp.concatenate([scratch_ref[g, pl.ds(b, SIDE, stride=count), :] for b in range(count)], axis=0))
    return jnp.concatenate(columns, axis=1)


def build(half, sizes, blocks_hbm, row_hbm, col_hbm, blocks, ids, sems, stores, meanwhile=lambda: None):
    count, row_devs, ka_devs = sizes
    bits, row_bits = log2(count), log2(row_devs)
    copies = [pltpu.make_async_copy(h, ids.at[k : k + 1], sems.at[k]) for k, h in enumerate((row_hbm, col_hbm))]
    width = blocks.shape[1] // PIECES
    for k in range(PIECES):
        lanes = pl.ds(k * width, width)
        copies.append(pltpu.make_async_copy(blocks_hbm.at[:, lanes], blocks.at[:, lanes], sems.at[2 + k]))
    for copy in copies:
        copy.start()
    meanwhile()
    copies[0].wait()
    copies[1].wait()
    row = ids[0:1, :]
    col = ids[1:2, :]
    row_place = (row >> bits) & (row_devs - 1)
    ka_step = ((col >> (bits + row_bits)) - (row >> (bits + row_bits))) & (ka_devs - 1)
    row_step = (((col >> bits) & (row_devs - 1)) - row_place + 1) & (row_devs - 1)
    is_mate = (row_step >> 1) == ((row_place & 1) ^ 1)
    group = jnp.where(row_step == 1, 0, jnp.where(is_mate, 1, 2))
    band = group * count + (col & (count - 1))
    pairs = 3 * count // 2
    place = ((band & 1) * pairs + (band >> 1)) * count + (row & (count - 1))
    place = jnp.where((row >= 0) & (ka_step == half), place, -1)
    slots = blocks.shape[0]
    chosen = lax.broadcasted_iota(jnp.int32, (2 * pairs * count, slots), 0) == place
    chosen = jnp.where(chosen, 1.0, 0.0).astype(BF16)
    low = lax.broadcasted_iota(jnp.int32, (pairs * count, LANES), 1) < SIDE
    for u in range(SIDE // 4):
        if u % (SIDE // 4 // PIECES) == 0:
            copies[2 + u // (SIDE // 4 // PIECES)].wait()
        found = dot(chosen, blocks[:, u * 2 * LANES : (u + 1) * 2 * LANES])
        for w in range(2):
            t = 2 * u + w
            even = found[: pairs * count, w * LANES : (w + 1) * LANES]
            odd = found[pairs * count :, w * LANES : (w + 1) * LANES]
            first = jnp.where(low, even, pltpu.roll(odd, SIDE, 1))
            second = jnp.where(low, pltpu.roll(even, SIDE, 1), odd)
            for q in range(pairs):
                pair = [v[q * count : (q + 1) * count, :] for v in (first, second)]
                tile = jnp.concatenate(pair, axis=0).astype(BF16)
                per = pairs // 3
                lanes = slice((q % per) * LANES, (q % per + 1) * LANES)
                stores[q // per][2 * t * count : (2 * t + 2) * count, lanes] = tile


def emit(cross, wire, perm_ref, wire_ref, self_ref, mate_ref, far_ref):
    perm = perm_ref[...]
    wire_ref[...] = wire
    self_ref[...] = dot_t(cross[0][...], perm)
    for k, ref in ((2, far_ref), (1, mate_ref)):
        ref[0] = dot_t(cross[k][...], perm).astype(BF16)
        ref[1] = wire


def first_body(sizes, blocks_hbm, row_hbm, col_hbm, drive_hbm, relax_hbm, *refs):
    cross, (perm_ref, wire_ref, self_ref, mate_ref, far_ref, spread_ref) = refs[:3], refs[3:9]
    blocks, ids, drive, relax, scratch, sems = refs[9:]
    later = [
        pltpu.make_async_copy(drive_hbm, drive, sems.at[2 + PIECES]),
        pltpu.make_async_copy(relax_hbm, relax, sems.at[3 + PIECES]),
    ]
    for copy in later:
        copy.start()

    def place_field():
        for copy in later:
            copy.wait()
        spread_ref[...] = jnp.broadcast_to(relax[...], (LANES, relax.shape[1])).T
        interleave(drive[...], scratch, perm_ref)

    build(1, sizes, blocks_hbm, row_hbm, col_hbm, blocks, ids, sems, cross, place_field)
    emit(cross, drive[...].astype(BF16), perm_ref, wire_ref, self_ref, mate_ref, far_ref)


def second_body(sizes, blocks_hbm, row_hbm, col_hbm, *refs):
    build(0, sizes, blocks_hbm, row_hbm, col_hbm, *refs[3:], refs[:3])


def sent_terms(sent, fields, scratch, other):
    total = 0.0
    for matrix, field in zip(sent, fields):
        interleave(field[1].astype(F32), scratch, other)
        total += dot_t(matrix[...], other[...])
    return total


def own_body(*refs):
    mats, (wire_ref, perm_ref, mate_ref, far_ref), sent = refs[:3], refs[3:7], refs[7:-3]
    out_ref, scratch, other = refs[-3:]
    total = dot_t(mats[0][...], perm_ref[...])
    straight = dot(mats[0][...], wire_ref[...])
    straight += dot(mats[1][...], mate_ref[1])
    straight += dot(mats[2][...], far_ref[1])
    if sent:
        total += sent_terms(sent, (mate_ref, far_ref), scratch, other)
    out_ref[...] = total + restored(straight, scratch)


def with_cross(cross, nexts, known_ref, scratch):
    straight = dot(cross[0][...], nexts[0][...])
    straight += dot(cross[1][...], nexts[1][...])
    straight += dot(cross[2][...], nexts[2][...])
    return known_ref[...] + restored(straight, scratch)


def advanced(product, drive_ref, relax_ref):
    scale = jnp.concatenate([relax_ref[...]] * (product.shape[1] // LANES), axis=1)
    return drive_ref[...] + scale * product


def cross_body(*refs):
    refs[7][...] = with_cross(refs[:3], refs[3:6], refs[6], refs[8])


def update_body(*refs):
    cross, (known_ref, drive_ref, relax_ref, mate_in, far_in), sent = refs[:3], refs[3:8], refs[8:10]
    perm_ref, wire_ref, self_ref, mate_ref, far_ref, scratch, other = refs[10:]
    late = sent_terms(sent, (mate_in, far_in), scratch, other)
    field = advanced(known_ref[...] + late, drive_ref, relax_ref)
    interleave(field, scratch, perm_ref)
    emit(cross, field.astype(BF16), perm_ref, wire_ref, self_ref, mate_ref, far_ref)


def settle_body(own_ref, received_ref, out_ref):
    out_ref[...] = own_ref[...] + received_ref[...].astype(F32)


def final_body(*refs):
    product = with_cross(refs[:3], refs[3:6], refs[6], refs[10])
    refs[9][...] = advanced(product, *refs[7:9])


def local(drive, relax, blocks, row_block, col_block):
    rows, channels = drive.shape
    slots = blocks.shape[0]
    sizes = (rows // SIDE, lax.axis_size("rows"), lax.axis_size("ka"))
    small = jax.ShapeDtypeStruct((rows, channels), BF16)
    double = jax.ShapeDtypeStruct((2, rows, channels), BF16)
    wide = jax.ShapeDtypeStruct((rows, channels), F32)
    matrices = (jax.ShapeDtypeStruct((rows, rows), BF16),) * 3
    emitted = (small, small, wide, double, double)
    staging = pltpu.VMEM((channels // LANES, rows, LANES), F32)
    fetch = [pltpu.VMEM(blocks.shape, BF16), pltpu.VMEM((2, slots), jnp.int32)]
    row2 = row_block.reshape(1, -1)
    col2 = col_block.reshape(1, -1)
    relax2 = relax.reshape(1, -1)
    work = 2 * rows * rows * channels
    spread = jax.ShapeDtypeStruct((rows, LANES), F32)
    *cross, perm, wire, partial, to_mate, to_far, relax3 = call(
        functools.partial(first_body, sizes), (*matrices, *emitted, spread), 9 * work,
        [blocks, row2, col2, drive, relax2], [HBM] * 5,
        fetch + [pltpu.VMEM(drive.shape, F32), pltpu.VMEM((1, rows), F32), staging, pltpu.SemaphoreType.DMA((4 + PIECES,))],
    )

    extra = [staging, pltpu.VMEM((rows, channels), BF16)]
    for sweep in range(ITERS):
        down = shifted(wire, "ka", -1)
        from_far = far(to_far)
        from_mate = mate(to_mate)
        if sweep == 0:
            own = call(
                functools.partial(second_body, sizes), matrices, 6 * work, [blocks, row2, col2], [HBM] * 3,
                fetch + [pltpu.SemaphoreType.DMA((2 + PIECES,))],
            )
        if sweep == 0:
            from_far, _ = lax.optimization_barrier((from_far, own))
        got = (partial + from_mate[0].astype(F32) + from_far[0].astype(F32)).astype(BF16)
        received = shifted(got, "ka", 1)
        if sweep == 0:
            gated, down = lax.optimization_barrier((own[1:], down))
            sent = [mate(gated[0]), far(gated[1])]
        nexts = [down, mate(down), far(down)]
        args = [*own, wire, perm, from_mate, from_far, *(sent if sweep else [])]
        known = call(own_body, wide, 9 * work, args, scratch=extra)
        known = call(settle_body, wide, HEAVY * work, [known, received])
        if sweep + 1 == ITERS:
            return call(final_body, wide, 3 * work, [*cross, *nexts, known, drive, relax3], scratch=[staging])
        known = call(cross_body, wide, HEAVY * work, [*cross, *nexts, known], scratch=[staging])
        args = [*cross, known, drive, relax3, from_mate, from_far, *sent]
        perm, wire, partial, to_mate, to_far = call(update_body, emitted, 8 * work, args, scratch=extra)


def solution(mesh):
    spread = P(("ka", "rows"))
    wide = P(("ka", "rows"), None)
    return jax.shard_map(
        local, mesh=mesh, in_specs=(wide, spread, wide, spread, spread), out_specs=wide, check_vma=False
    )
```
